128 devices in a mesh: req: 4 (over x), exp: 32 (over z, y, core).
Axes of the slice: x: 4, y: 4, z: 4, core: 2. Of those that a mesh axis runs over, the one named last changes fastest.
Arguments:
- hidden_in: bfloat16 [4, 32, 128, 2048], P('req', 'exp'), may hold values from -6 to 6
- queries: bfloat16 [4, 32, 128, 2048], P('req', 'exp'), may hold values from -6 to 6
- suffix_pairs: bfloat16 [4, 32, 2, 128, 2048], P('req', 'exp'), may hold values from -6 to 6
- prefix_cache: bfloat16 [32, 4, 2, 384, 2048], P('exp', 'req'), may hold values from -6 to 6
- suffix_length: int32 [4, 32], P('req', 'exp'), may hold values from 1 to 128, 3072 in all within a row
- request_group: int32 [4, 32], P('req', 'exp'), may hold values from 0 to 3
- prefix_owner: int32 [32, 4], P('exp'), may hold values from 0 to 3, each once within a row
- out_weight: bfloat16 [2048, 2048], replicated, may hold values from -0.8984375 to 0.8984375
- norm_gain: float32 [2048], replicated, may hold values from 0.1 to 1.9
- routes: int32 [4, 32, 128, 8], P('req', 'exp'), may hold values from 0 to 31, all different within a row; in each aligned block of 128 rows (0 to 127, 128 to 255, ..., all dimensions but the last counted through in order) at most 40 rows name the same one
- gate_values: float32 [4, 32, 128, 8], P('req', 'exp'), may hold values from 0.05 to 0.3
- expert_upward: bfloat16 [32, 2048, 2048], P('exp'), may hold values from -0.125 to 0.125
- expert_downward: bfloat16 [32, 1024, 2048], P('exp'), may hold values from -0.1875 to 0.1875
Outputs:
- layer_out: bfloat16 [4, 32, 128, 2048], P('req', 'exp')
The draws below stay inside these ranges and needn't reach their ends.
Inputs may be any that keep to these rules, and one draw needn't show every extreme that they name: The request at row r and column e reads the group held at prefix_cache[e, prefix_owner[e, request_group[r, e]]]. `prefix_owner`: each row is a permutation of 0 to 3. `routes`: a row names 8 different experts; on the rows of one device no expert is named more than 40 times, and on the rows of some device one expert is named exactly 40 times.
All inputs are finite; a program needn't handle non-finite values. No bound on the sum of `suffix_length` on one device may be relied on, other than what follows from the above.
Results may differ from the reference program's by a relative error of at most 0.0052.
Values may be sent and summed in bfloat16 or wider, within the bound.
A program may use at most 128 MiB of HBM per device.

```python
import math
import jax
import jax.numpy as jnp
import numpy as np
from jax import lax

D = 2048
H = 16
HD = 128
FF = 1024
TOP = 8
SUF = 128
WIN = 384
SINK = 4
EXPERTS = 32
CAP = 40
N_REQ = 4
N_EXP = 32


def draw_queries(key, part):
    drawn = jnp.clip(jax.random.normal(jax.random.fold_in(key, 1), (N_REQ, N_EXP, SUF, H, HD), jnp.float32), -6.0, 6.0)
    return drawn.reshape(N_REQ, N_EXP, SUF, D).astype(jnp.bfloat16)


def draw_suffix_pairs(key, part):
    drawn = jnp.clip(jax.random.normal(jax.random.fold_in(key, 2), (N_REQ, N_EXP, 2, SUF, H, HD), jnp.float32), -6.0, 6.0)
    return drawn.reshape(N_REQ, N_EXP, 2, SUF, D).astype(jnp.bfloat16)


def draw_prefix_cache(key, part):
    drawn = jnp.clip(jax.random.normal(jax.random.fold_in(key, 3), (N_EXP, N_REQ, 2, WIN, H, HD), jnp.float32), -6.0, 6.0)
    return drawn.reshape(N_EXP, N_REQ, 2, WIN, D).astype(jnp.bfloat16)


def place_ends(result, key, low, high):
    extent = result.shape
    index_at = [jax.random.randint(jax.random.fold_in(key, axis), (), 0, extent[axis]) for axis in range(len(extent))]
    result = result.at[tuple(index_at)].set(low)
    longest = extent.index(max(extent))
    index_at[longest] = (index_at[longest] + 1) % extent[longest]
    return result.at[tuple(index_at)].set(high)


def block_levels(key, shape, pieces, low, high):
    gain, own = 1.0, jax.random.fold_in(key, 6)
    for dim, blocks in pieces:
        steps = jnp.exp(jax.random.uniform(jax.random.fold_in(own, dim), (blocks,), jnp.float32, low / len(pieces), high / len(pieces)))
        gain = gain * jnp.repeat(steps, shape[dim] // blocks).reshape([-1 if axis == dim else 1 for axis in range(len(shape))])
    return gain


def profile(count, total, limit, skew):
    loads = [(1 << 20) // math.isqrt(rank ** skew) + 1 for rank in range(2, count + 1)]
    spare, counts = total - limit - (count - 1), [1] * (count - 1)
    while spare > 0:
        movable = [i for i in range(count - 1) if counts[i] < limit]
        pool, left = sum([loads[i] for i in movable]), spare
        for i in movable:
            extra = min(limit - counts[i], max(1, left * loads[i] // pool), spare)
            counts[i] = counts[i] + extra
            spare = spare - extra
    return np.array([limit] + counts)


def uneven(rng, amount, total, reach, lean):
    if amount == 2:
        one = jax.random.randint(rng, (), max(1, total - reach), min(reach, total - 1) + 1)
        return jnp.stack([one, total - one])
    lengths = jnp.asarray(profile(amount, total, reach, lean), jnp.int32)
    couples = (amount - 1) // 2
    donor, sink = lengths[1:1 + 2 * couples:2], lengths[2:2 + 2 * couples:2]
    room = jnp.minimum(donor - 1, reach - sink)
    passed = jax.random.randint(jax.random.fold_in(rng, 1), (couples,), 0, 1 << 20) % (room + 1)
    lengths = lengths.at[1:1 + 2 * couples:2].set(donor - passed).at[2:2 + 2 * couples:2].set(sink + passed)
    return lengths[jax.random.permutation(jax.random.fold_in(rng, 2), amount)]


def shared_out(rng, own, number, rows, amount, top, most, lean):
    sequence = jax.random.permutation(rng, amount)
    crowded, ordinary = portions_of(amount, rows * top, most, lean, True), portions_of(amount, rows * top, most, lean, False)
    places = jnp.arange(amount)

    def named(sizes, offset_by):
        used = int((sizes > 0).sum())
        fixed = max(1, used // 4)
        passed = fixed + (places - fixed + offset_by * (used - fixed)) % max(1, amount - fixed)
        return jnp.zeros((amount,), jnp.int32).at[sequence[jnp.where(places < fixed, places, passed)]].set(jnp.asarray(sizes, jnp.int32))

    sizes = jnp.where(number % 4 == 0, named(crowded, number // 4), named(ordinary, number - number // 4 - 1))
    mixed = jax.random.permutation(jax.random.fold_in(own, 3), amount)
    source_of, taker = mixed[0:amount // 2 * 2:2], mixed[1:amount // 2 * 2:2]
    slack = jnp.minimum(sizes[source_of] - 1, most - sizes[taker]) // 2
    slack = jnp.where((source_of == sequence[0]) | (taker == sequence[0]) | (sizes[taker] == 0), 0, jnp.maximum(slack, 0))
    passed = jax.random.randint(jax.random.fold_in(own, 4), (amount // 2,), 0, 1 << 20) % (slack + 1)
    sizes = sizes.at[source_of].add(-passed).at[taker].add(passed)
    items = jnp.searchsorted(jnp.cumsum(sizes), jnp.arange(rows * top), side="right").astype(jnp.int32)
    table = items.reshape(top, rows).T
    table = table[jax.random.permutation(jax.random.fold_in(own, 1), rows)]
    offset_by = jax.random.randint(jax.random.fold_in(own, 2), (rows, 1), 0, top)
    return jnp.take_along_axis(table, (jnp.arange(top)[None, :] + offset_by) % top, axis=1)


def portions_of(count, total, limit, slope, full):
    portions = [(1 << 20) // math.isqrt(rank ** slope) + 1 for rank in range(1, count + 1)]
    largest = limit if full else min(limit, max(-(-total // count), total * portions[0] // sum(portions)))
    least = 1 if total - largest >= count - 1 else 0
    given, rest = [largest] + [least] * (count - 1), total - largest - least * (count - 1)
    while rest > 0:
        free = [i for i in range(1, count) if given[i] < largest] or [i for i in range(1, count) if given[i] < limit]
        whole, budget = sum([portions[i] for i in free]), rest
        for i in free:
            addition = min(limit - given[i], max(1, budget * portions[i] // whole), rest)
            given[i] = given[i] + addition
            rest = rest - addition
    return np.array(given)


def noise(key, extent, scale, reach, cuts=(), kind=jnp.bfloat16):
    level = block_levels(key, extent, cuts, -0.22, 0.18) if cuts else 1.0
    values = jax.random.normal(key, extent, jnp.float32) * scale * level
    return jnp.minimum(jnp.maximum(values, -reach), reach).astype(kind)


def setup_inputs(seed: int = 0) -> dict:
    key_of = jax.random.split(jax.random.key(seed), 14)
    hidden_in = noise(key_of[0], (N_REQ, N_EXP, SUF, D), 1.0, 6.0, ((0, 4), (1, 32)))
    queries = draw_queries(jax.random.fold_in(key_of[13], 71), 0)
    suffix_pairs = draw_suffix_pairs(jax.random.fold_in(key_of[13], 71), 0)
    prefix_cache = draw_prefix_cache(jax.random.fold_in(key_of[13], 71), 0)
    suffix_length = jax.vmap(lambda own: uneven(own, N_EXP, N_EXP * SUF * 3 // 4, SUF, 1))(jax.random.split(key_of[4], N_REQ)).reshape((N_REQ, N_EXP)).astype(jnp.int32)
    request_group = place_ends(jax.random.randint(key_of[5], (N_REQ, N_EXP), 0, N_REQ), jax.random.fold_in(key_of[5], 1), 0, N_REQ - 1).astype(jnp.int32)
    prefix_owner = jax.vmap(lambda own: jax.random.permutation(own, N_REQ))(jax.random.split(key_of[6], N_EXP)).reshape((N_EXP, N_REQ)).astype(jnp.int32)
    out_weight = noise(key_of[7], (D, D), 0.15, 0.8984375)
    norm_gain = jnp.clip(1.0 + 0.18 * jax.random.normal(key_of[8], (D,), jnp.float32), 0.1, 1.9)
    routes_keys = jax.random.split(jax.random.fold_in(key_of[9], 1), N_REQ * N_EXP * SUF // SUF)
    routes_turns = jax.random.permutation(jax.random.fold_in(key_of[9], 3), N_REQ * N_EXP * SUF // SUF)
    routes = jax.vmap(lambda own, number: shared_out(jax.random.fold_in(key_of[9], 2), own, number, SUF, EXPERTS, TOP, CAP, 0))(routes_keys, routes_turns).reshape((N_REQ, N_EXP, SUF, TOP))
    gate_values = jnp.clip(0.05 + 0.25 * jax.random.uniform(key_of[10], (N_REQ, N_EXP, SUF, TOP), jnp.float32) ** block_levels(key_of[10], (N_REQ, N_EXP, SUF, TOP), ((0, 4), (1, 32)), -0.2, 0.2), 0.05, 0.3)
    expert_upward = noise(key_of[11], (EXPERTS, D, 2 * FF), D ** -0.5, 0.125, ((0, 32),))
    expert_downward = noise(key_of[12], (EXPERTS, FF, D), FF ** -0.5, 0.1875, ((0, 32),))
    return dict(hidden_in=hidden_in, queries=queries, suffix_pairs=suffix_pairs, prefix_cache=prefix_cache, suffix_length=suffix_length, request_group=request_group, prefix_owner=prefix_owner, out_weight=out_weight, norm_gain=norm_gain, routes=routes, gate_values=gate_values, expert_upward=expert_upward, expert_downward=expert_downward)


def softmax_part(scores, visible, values):
    masked = jnp.where(visible[None], scores, -jnp.inf)
    largest = lax.optimization_barrier(jnp.max(masked, axis=2))
    weights = jnp.exp(masked - largest[:, :, None])
    totals = lax.optimization_barrier(jnp.sum(weights, axis=2))
    rounded = lax.optimization_barrier(weights.astype(jnp.bfloat16)).astype(jnp.float32)
    summed = jnp.einsum('htc,chd->htd', rounded, values)
    return (largest, totals, summed)

def head_split(matrix):
    return matrix.reshape(matrix.shape[0], matrix.shape[1] // HD, HD).astype(jnp.float32)

def merge_parts(first, second):
    largest = jnp.maximum(first[0], second[0])
    scale_first = jnp.exp(first[0] - largest)
    scale_second = jnp.exp(second[0] - largest)
    totals = first[1] * scale_first + second[1] * scale_second
    summed = first[2] * scale_first[:, :, None] + second[2] * scale_second[:, :, None]
    merged = summed / totals[:, :, None]
    head_count = merged.shape[0]
    row_count = merged.shape[1]
    return jnp.transpose(merged, (1, 0, 2)).reshape(row_count, head_count * HD).astype(jnp.bfloat16)

def attend_request(query_rows, pairs, cache):
    row_count = query_rows.shape[0]
    window = cache.shape[1]
    query_heads = head_split(query_rows)
    factor = HD ** (-0.5)
    prefix_scores = jnp.einsum('thd,chd->htc', query_heads, head_split(cache[0])) * factor
    column = lax.broadcasted_iota(jnp.int32, (row_count, window), 1)
    position = lax.broadcasted_iota(jnp.int32, (row_count, window), 0)
    first = softmax_part(prefix_scores, (column < SINK) | (column > position), head_split(cache[1]))
    suffix_scores = jnp.einsum('thd,shd->hts', query_heads, head_split(pairs[0])) * factor
    column_own = lax.broadcasted_iota(jnp.int32, (row_count, row_count), 1)
    position_own = lax.broadcasted_iota(jnp.int32, (row_count, row_count), 0)
    visible_own = column_own <= position_own
    second = softmax_part(suffix_scores, visible_own, head_split(pairs[1]))
    return merge_parts(first, second)

def reference(hidden_in, queries, suffix_pairs, prefix_cache, suffix_length, request_group, prefix_owner, out_weight, norm_gain, routes, gate_values, expert_upward, expert_downward):
    request_count = N_REQ * N_EXP
    row_count = hidden_in.shape[2]
    width = hidden_in.shape[3]
    columns_of = jnp.arange(request_count, dtype=jnp.int32) % N_EXP
    owners_of = prefix_owner[columns_of, request_group.reshape(request_count)].astype(jnp.int32)

    def attend_one(packed):
        query_rows, pairs, column_id, owner_id = packed
        cache = prefix_cache[column_id, owner_id]
        return attend_request(query_rows, pairs, cache)
    attention = lax.map(attend_one, (queries.reshape(request_count, row_count, width), suffix_pairs.reshape(request_count, 2, row_count, width), columns_of, owners_of))
    flat_attention = attention.reshape(request_count * row_count, width)
    residual = hidden_in.reshape(request_count * row_count, width).astype(jnp.float32) + jnp.dot(flat_attention, out_weight, preferred_element_type=jnp.float32)
    scaled = residual * lax.rsqrt(lax.optimization_barrier(jnp.mean(residual * residual, axis=1, keepdims=True)) + 1e-05)
    normed = (scaled * norm_gain[None, :]).astype(jnp.bfloat16)
    flat_routes = routes.reshape(-1).astype(jnp.int32)
    flat_gates = gate_values.reshape(-1)
    list_size = CAP * request_count

    def add_expert(expert, running):
        matches = flat_routes == expert
        picked = jnp.nonzero(matches, size=list_size, fill_value=0)[0].astype(jnp.int32)
        live_entries = jnp.arange(list_size, dtype=jnp.int32) < jnp.sum(matches.astype(jnp.int32))
        token_ids = picked // TOP
        joined = jnp.dot(normed[token_ids], expert_upward[expert], preferred_element_type=jnp.float32)
        hidden_units = (jax.nn.silu(joined[:, :FF]) * joined[:, FF:]).astype(jnp.bfloat16)
        produced = jnp.dot(hidden_units, expert_downward[expert], preferred_element_type=jnp.float32).astype(jnp.bfloat16)
        rounded = lax.optimization_barrier(produced).astype(jnp.float32)
        scaled_rows = rounded * jnp.where(live_entries, flat_gates[picked], 0.0)[:, None]
        return running.at[token_ids].add(scaled_rows)
    mixture = lax.fori_loop(0, EXPERTS, add_expert, jnp.zeros((request_count * row_count, width), jnp.float32))
    combined = residual + mixture
    live_rows = (jnp.arange(row_count, dtype=jnp.int32)[None, :] < suffix_length.reshape(request_count, 1).astype(jnp.int32)).reshape(-1)
    layer_out = jnp.where(live_rows[:, None], combined, 0.0).astype(jnp.bfloat16)
    return layer_out.reshape(N_REQ, N_EXP, row_count, width)
```

```python
import functools

import jax
import jax.numpy as jnp
from jax import lax
from jax.experimental import pallas as pl
from jax.experimental.pallas import tpu as pltpu
from jax.sharding import PartitionSpec as P

HD = 128
SINK = 4
SIDE = 4
CAP = 40
NEG = -1e30
MESH = pl.DeviceIdType.MESH
VMEM_LIMIT = 63 * 1024 * 1024
F32 = jnp.float32
BF16 = jnp.bfloat16
ANY = pl.BlockSpec(memory_space=pl.ANY)
VMEM = pl.BlockSpec(memory_space=pltpu.VMEM)
SMEM = pl.BlockSpec(memory_space=pltpu.SMEM)


def dot_t(a, b):
    return lax.dot_general(a, b, (((1,), (1,)), ((), ())), preferred_element_type=F32)


def dot(a, b):
    return jnp.dot(a, b, preferred_element_type=F32)


def dot_0(a, b):
    return lax.dot_general(a, b, (((0,), (0,)), ((), ())), preferred_element_type=F32)


class Copies:
    def __init__(self, send, recv):
        self.send, self.recv, self.made = send, recv, {}

    def start(self, key, src, dst, device):
        index = len(self.made)
        copy = pltpu.make_async_remote_copy(
            src_ref=src,
            dst_ref=dst,
            send_sem=self.send.at[index],
            recv_sem=self.recv.at[index],
            device_id=device,
            device_id_type=MESH,
        )
        copy.start()
        self.made[key] = copy

    def arrived(self, key):
        self.made[key].wait_recv()

    def drain(self):
        for copy in self.made.values():
            copy.wait_send()


def meet(devices):
    barrier = pltpu.get_barrier_semaphore()
    for device in devices:
        pl.semaphore_signal(barrier, inc=1, device_id=device, device_id_type=MESH)
    pl.semaphore_wait(barrier, len(devices))


def torus(req, e):
    core = lax.rem(e, 2)
    y = lax.rem(e // 2, SIDE)
    z = e // (2 * SIDE)

    def at(dz, dy):
        return (req, (lax.rem(z + dz, SIDE) * SIDE + lax.rem(y + dy, SIDE)) * 2 + core)

    return at(1, 0), at(3, 0), at(0, 1), at(0, 3)


def attend_kernel(
    flag_ref, q_ref, pairs_ref, cache_ref, weight_ref, hidden_ref, gain_ref, up_ref, down_ref, meta_ref,
    residual_ref, normed_ref, up_other, down_other, meta,
    qbuf, flags, cache, weight, part, stat, stat_t, stat_in, own_out, own_stat, relay, back, attn,
    send, recv, local,
):
    x, e = lax.axis_index("req"), lax.axis_index("exp")
    right, left, across = (
        (lax.rem(x + 1, SIDE), e),
        (lax.rem(x + 3, SIDE), e),
        (lax.rem(x + 2, SIDE), e),
    )
    other = (x, e + 1 - 2 * lax.rem(e, 2))
    rows, width = q_ref.shape
    heads = width // HD
    window = cache_ref.shape[1]
    half = rows // 2
    low, high = pl.ds(0, half), pl.ds(half, half)
    copies = Copies(send, recv)

    load_cache = pltpu.make_async_copy(cache_ref, cache, local.at[0])
    load_weight = pltpu.make_async_copy(weight_ref, weight, local.at[1])
    load_cache.start()
    load_weight.start()
    zp, zm, yp, ym = torus(x, e)
    meet([right, left, across, other, zp, zm, yp, ym])

    copies.start("q3", q_ref, qbuf.at[2], right)
    copies.start("q1", q_ref, qbuf.at[0], left)
    copies.start("f3", flag_ref, flags.at[2], right)
    copies.start("f1", flag_ref, flags.at[0], left)
    copies.start("f2", flag_ref, flags.at[1], across)
    copies.start("up", up_ref, up_other, other)
    copies.start("down", down_ref, down_other, other)

    def tell(source, tz, ty, device):
        copies.start(("m", tz, ty), source, meta.at[tz * SIDE + ty], device)

    def told(tz, ty):
        copies.arrived(("m", tz, ty))
        return meta.at[tz * SIDE + ty]

    tell(meta_ref, 3, 0, zp)
    tell(meta_ref, 1, 0, zm)
    tell(meta_ref, 0, 3, yp)
    tell(meta_ref, 0, 1, ym)
    meta[0] = meta_ref[...]

    scale = HD ** (-0.5)
    lane = lax.broadcasted_iota(jnp.int32, (rows, HD), 1)
    stat[...] = jnp.zeros_like(stat)
    own_stat[...] = jnp.zeros_like(own_stat)

    def softmax(scores, visible, values):
        masked = jnp.where(visible, scores, NEG)
        largest = jnp.max(masked, axis=1, keepdims=True)
        weights = jnp.exp(masked - largest)
        totals = jnp.sum(weights, axis=1, keepdims=True)
        return dot(weights.astype(BF16), values) / totals, largest + jnp.log(totals)

    own_c = lax.broadcasted_iota(jnp.int32, (rows, rows), 1)
    own_t = lax.broadcasted_iota(jnp.int32, (rows, rows), 0)

    @pl.loop(0, heads)
    def _(h):
        cols = pl.ds(pl.multiple_of(h * HD, HD), HD)
        out, lse = softmax(dot_t(q_ref[:, cols], pairs_ref[0, :, cols]) * scale, own_c <= own_t, pairs_ref[1, :, cols])
        own_out[:, cols] = out
        own_stat[...] = jnp.where(lane == h, lse, own_stat[...])

    def prefix(slots):
        c = lax.broadcasted_iota(jnp.int32, (rows, window), 1)
        t = lax.broadcasted_iota(jnp.int32, (rows, window), 0)
        visible = (c < SINK) | (c > t)
        valid = {}
        for d in slots:
            flag = flag_ref if d == 0 else flags.at[d - 1]
            valid[d] = flag[pl.ds(x, 1), :]

        @pl.loop(0, heads)
        def _(h):
            cols = pl.ds(pl.multiple_of(h * HD, HD), HD)
            for d in slots:
                q = q_ref[:, cols] if d == 0 else qbuf[d - 1, :, cols]
                out, lse = softmax(dot_t(q, cache[0, :, cols]) * scale, visible, cache[1, :, cols])
                part[d, :, cols] = (out * valid[d]).astype(BF16)
                stat[d] = jnp.where(lane == h, lse * valid[d], stat[d])

        for d in slots:
            stat_t[d] = jnp.transpose(stat[d])[0:heads, :]

    for d in (3, 1):
        source = told(d, 0)
        tell(source, d, 3, yp)
        tell(source, d, 1, ym)
        if d == 3:
            tell(source, 2, 0, zp)
    load_cache.wait()
    prefix([0])
    copies.arrived("q3")
    copies.start("q2a", qbuf.at[2, low], qbuf.at[1, low], right)
    copies.arrived("q1")
    copies.start("q2b", qbuf.at[0, high], qbuf.at[1, high], left)
    source = told(2, 0)
    tell(source, 2, 3, yp)
    tell(source, 2, 1, ym)
    for d in range(SIDE):
        tell(told(d, 3), d, 2, yp)
    copies.arrived("f1")
    copies.arrived("f3")
    prefix([1, 3])
    copies.start("r_high", part.at[1, high], back.at[0, high], right)
    copies.start("l_low", part.at[3, low], back.at[1, low], left)
    copies.start("s1", stat_t.at[1], stat_in.at[0], right)
    copies.start("s3", stat_t.at[3], stat_in.at[1], left)
    copies.arrived("q2a")
    copies.arrived("q2b")
    copies.arrived("f2")
    prefix([2])
    copies.start("relay_r", part.at[2, low], relay.at[0], right)
    copies.start("relay_l", part.at[2, high], relay.at[1], left)
    copies.start("s2", stat_t.at[2], stat_in.at[2], across)
    copies.arrived("relay_r")
    part[1, low, :] = part[1, low, :] + relay[0]
    copies.start("r_low", part.at[1, low], back.at[0, low], right)
    copies.arrived("relay_l")
    part[3, high, :] = part[3, high, :] + relay[1]
    copies.start("l_high", part.at[3, high], back.at[1, high], left)
    for key in ("s1", "s2", "s3", "r_high", "l_low", "r_low", "l_high"):
        copies.arrived(key)
    total_t = stat_t[0] + stat_in[0] + stat_in[1] + stat_in[2]
    stat[0] = jnp.transpose(jnp.concatenate([total_t, jnp.zeros((HD - heads, rows), F32)], axis=0))

    @pl.loop(0, heads)
    def _(h):
        cols = pl.ds(pl.multiple_of(h * HD, HD), HD)
        first = part[0, :, cols].astype(F32) + back[0, :, cols].astype(F32) + back[1, :, cols].astype(F32)
        lse_first = jnp.sum(jnp.where(lane == h, stat[0], 0.0), axis=1, keepdims=True)
        lse_own = jnp.sum(jnp.where(lane == h, own_stat[...], 0.0), axis=1, keepdims=True)
        top = jnp.maximum(lse_first, lse_own)
        a, b = jnp.exp(lse_first - top), jnp.exp(lse_own - top)
        attn[:, cols] = ((a * first + b * own_out[:, cols]) / (a + b)).astype(BF16)

    load_weight.wait()
    tile = min(256, width)

    def project(j, squares):
        cols = pl.ds(pl.multiple_of(j * tile, tile), tile)
        res = hidden_ref[:, cols].astype(F32) + dot(attn[...], weight[:, cols])
        residual_ref[:, cols] = res
        return squares + jnp.sum(res * res, axis=1, keepdims=True)

    squares = lax.fori_loop(0, width // tile, project, jnp.zeros((rows, 1), F32))
    factor = lax.rsqrt(squares / width + 1e-05)

    @pl.loop(0, width // tile)
    def _(j):
        cols = pl.ds(pl.multiple_of(j * tile, tile), tile)
        normed_ref[:, cols] = (residual_ref[:, cols] * factor * gain_ref[:, cols]).astype(BF16)

    for d in range(SIDE):
        told(d, 1)
        told(d, 2)
    copies.arrived("up")
    copies.arrived("down")
    copies.drain()


def attend(flag, queries, pairs, cache, weight, hidden, gain, upward, downward, meta):
    rows, width = queries.shape
    heads = width // HD
    sds = jax.ShapeDtypeStruct
    dma = pltpu.SemaphoreType.DMA
    return pl.pallas_call(
        attend_kernel,
        out_shape=(
            sds((rows, width), F32),
            sds((rows, width), BF16),
            sds(upward.shape, BF16),
            sds(downward.shape, BF16),
            sds((SIDE * SIDE,) + meta.shape, F32),
        ),
        in_specs=[VMEM, VMEM, VMEM, ANY, ANY, VMEM, VMEM, ANY, ANY, VMEM],
        out_specs=(VMEM, VMEM, ANY, ANY, VMEM),
        scratch_shapes=[
            pltpu.VMEM((3, rows, width), BF16),
            pltpu.VMEM((3, 8, HD), F32),
            pltpu.VMEM(cache.shape, BF16),
            pltpu.VMEM(weight.shape, BF16),
            pltpu.VMEM((4, rows, width), BF16),
            pltpu.VMEM((4, rows, HD), F32),
            pltpu.VMEM((4, heads, rows), F32),
            pltpu.VMEM((3, heads, rows), F32),
            pltpu.VMEM((rows, width), F32),
            pltpu.VMEM((rows, HD), F32),
            pltpu.VMEM((2, rows // 2, width), BF16),
            pltpu.VMEM((2, rows, width), BF16),
            pltpu.VMEM((rows, width), BF16),
            dma((36,)),
            dma((36,)),
            dma((2,)),
        ],
        compiler_params=pltpu.CompilerParams(
            collective_id=0, has_side_effects=True, vmem_limit_bytes=VMEM_LIMIT
        ),
        name="attend",
    )(flag, queries, pairs, cache, weight, hidden, gain, upward, downward, meta)


CHUNKS = (
    ((0, 0), (0, 1), (0, 3), (1, 0)),
    ((3, 0), (2, 0), (0, 2), (1, 1)),
    ((1, 3), (3, 1), (3, 3), (1, 2)),
    ((3, 2), (2, 1), (2, 3), (2, 2)),
)


def expert_kernel(
    length_ref, x_ref, meta, residual_ref, up_ref, down_ref, up_other, down_other,
    out_ref,
    tokens, up, down, picked, pmat, gslot, hid, sums, r1, r2, level, r3, r4,
    send, recv, local,
):
    req, e = lax.axis_index("req"), lax.axis_index("exp")
    zp, zm, yp, ym = torus(req, e)
    rows, width = x_ref.shape
    inner = down_ref.shape[0]
    half, quarter = rows // 2, rows // 4
    copies = Copies(send, recv)
    loads = []
    for index, (src, dst) in enumerate(
        ((up_ref, up.at[0]), (up_other, up.at[1]), (down_ref, down.at[0]), (down_other, down.at[1]))
    ):
        loads.append(pltpu.make_async_copy(src, dst, local.at[index]))
        loads[-1].start()
    meet([zp, zm, yp, ym])

    def slot(dz, dy):
        return (dz % SIDE) * SIDE + dy % SIDE

    def view(dz, dy, start, count):
        if dz % SIDE == 0 and dy % SIDE == 0:
            return x_ref.at[pl.ds(start, count)]
        return tokens.at[slot(dz, dy), pl.ds(start, count)]

    def push(kind, dz, dy, axis, step, start, count):
        device = {("z", 1): zp, ("z", -1): zm, ("y", 1): yp, ("y", -1): ym}[axis, step]
        tz, ty = (dz - step, dy) if axis == "z" else (dz, dy - step)
        key = (kind, tz % SIDE, ty % SIDE)
        copies.start(key, view(dz, dy, start, count), tokens.at[slot(tz, ty), pl.ds(start, count)], device)

    def both(kind, dz, dy, axis):
        start = half if kind == "b" else 0
        push(kind, dz, dy, axis, 1, start, half)
        push(kind, dz, dy, axis, -1, start, half)

    def pass_on(kind, dz, dy, axis):
        behind = (dz if axis == "z" else dy) == 3
        start = (half if kind == "b" else 0) + (0 if behind else quarter)
        push(kind + ("0" if behind else "1"), dz, dy, axis, 1 if behind else -1, start, quarter)

    def have(kind, dz, dy):
        far = dy == 2 if kind == "a" else dz == 2
        near_far = dz == 2 if kind == "a" else dy == 2
        split = far or (near_far and (dy == 0 if kind == "a" else dz == 0))
        if (dz, dy) == (0, 0):
            return
        for key in ([kind + "0", kind + "1"] if split else [kind]):
            if (key, dz, dy) not in waited:
                waited.add((key, dz, dy))
                copies.arrived((key, dz, dy))

    waited = set()
    both("a", 0, 0, "z")
    both("b", 0, 0, "y")
    both("a", 0, 0, "y")
    both("b", 0, 0, "z")
    for d in (3, 1):
        have("a", d, 0)
        pass_on("a", d, 0, "z")
        both("a", d, 0, "y")
        have("b", 0, d)
        pass_on("b", 0, d, "y")
        both("b", 0, d, "z")

    def pass_second(d):
        for near in (3, 1):
            have("a", d, near)
            pass_on("a", d, near, "y")
            have("b", near, d)
            pass_on("b", near, d, "z")

    ids = [e.astype(F32), (e + 1 - 2 * lax.rem(e, 2)).astype(F32)]
    span = 2 * CAP
    before = (
        lax.broadcasted_iota(jnp.int32, (rows, rows), 0) < lax.broadcasted_iota(jnp.int32, (rows, rows), 1)
    ).astype(BF16)
    slot_row = lax.broadcasted_iota(jnp.int32, (span, rows), 0).astype(F32)

    def block(dz, dy, cols):
        return x_ref[:, cols] if (dz, dy) == (0, 0) else tokens[slot(dz, dy), :, cols]

    def run_experts(chunk):
        pairs = [chunk[i:i + 2] for i in range(0, len(chunk), 2)]
        for p, pair in enumerate(pairs):
            for k in range(2):
                gates = jnp.zeros((span, 1), F32)
                for i, (dz, dy) in enumerate(pair):
                    source = slot(dz, dy)
                    named = (meta[source, 0:8, :] == ids[k]).astype(F32)
                    mine = jnp.sum(named, axis=0, keepdims=True)
                    gate = jnp.sum(named * meta[source, 8:16, :], axis=0, keepdims=True)
                    rank = dot(jnp.broadcast_to(mine, (8, rows)).astype(BF16), before)[0:1, :]
                    place = jnp.where(mine > 0.0, rank + float(i * CAP), -1.0)
                    chosen = (slot_row == place).astype(F32)
                    pmat[p, k * span:(k + 1) * span, i * rows:(i + 1) * rows] = chosen.astype(BF16)
                    gates = gates + jnp.sum(chosen * gate, axis=1, keepdims=True)
                gslot[k, p * span:(p + 1) * span, :] = jnp.broadcast_to(gates, (span, HD))
        tile = min(512, width)

        @pl.loop(0, width // tile)
        def _(j):
            cols = pl.ds(pl.multiple_of(j * tile, tile), tile)
            for p, pair in enumerate(pairs):
                joint = jnp.concatenate([block(dz, dy, cols) for dz, dy in pair], axis=0)
                rows_out = dot(pmat[p], joint).astype(BF16)
                for k in range(2):
                    picked[k, p * span:(p + 1) * span, cols] = rows_out[k * span:(k + 1) * span, :]

        count = len(pairs) * span
        tile_f = min(256, inner)

        @pl.loop(0, inner // tile_f)
        def _(j):
            start = pl.multiple_of(j * tile_f, tile_f)
            for k in range(2):
                gate = dot(picked[k, 0:count, :], up[k, :, pl.ds(start, tile_f)])
                lift = dot(picked[k, 0:count, :], up[k, :, pl.ds(pl.multiple_of(inner + start, tile_f), tile_f)])
                hid[k, 0:count, pl.ds(start, tile_f)] = (gate / (1.0 + jnp.exp(-gate)) * lift).astype(BF16)

        tile_d = min(256, width)

        @pl.loop(0, width // tile_d)
        def _(j):
            cols = pl.ds(pl.multiple_of(j * tile_d, tile_d), tile_d)
            made = []
            for k in range(2):
                gates = gslot[k, 0:count, 0:1]
                made.append((dot(hid[k, 0:count, :], down[k, :, cols]) * gates).astype(BF16))
            for p, pair in enumerate(pairs):
                joint = jnp.concatenate([m[p * span:(p + 1) * span, :] for m in made], axis=0)
                placed = dot_0(pmat[p], joint).astype(BF16)
                for i, (dz, dy) in enumerate(pair):
                    sums[slot(dz, dy), :, cols] = placed[i * rows:(i + 1) * rows, :]

    def sum_view(h, i, j, start, count):
        dz, dy = (i, j) if h == 0 else (j, i)
        return sums.at[slot(dz, dy), pl.ds(h * half + start, count)]

    first = ((yp, ym), (zp, zm))
    second = ((zp, zm), (yp, ym))

    def far_out(h, i):
        copies.start(("1+", h, i), sum_view(h, i, 2, 0, quarter), r1.at[h, i, pl.ds(0, quarter)], first[h][0])
        copies.start(("1-", h, i), sum_view(h, i, 2, quarter, quarter), r1.at[h, i, pl.ds(quarter, quarter)], first[h][1])

    def add_to(ref, other):
        ref[...] = (ref[...].astype(F32) + other[...].astype(F32)).astype(BF16)

    def near_out(h, i):
        copies.arrived(("1+", h, i))
        add_to(sum_view(h, i, 1, 0, quarter), r1.at[h, i, pl.ds(0, quarter)])
        copies.start(("2+", h, i), sum_view(h, i, 1, 0, half), r2.at[h, i, 0], first[h][0])
        copies.arrived(("1-", h, i))
        add_to(sum_view(h, i, 3, quarter, quarter), r1.at[h, i, pl.ds(quarter, quarter)])
        copies.start(("2-", h, i), sum_view(h, i, 3, 0, half), r2.at[h, i, 1], first[h][1])

    def gathered(h, i, start, count):
        copies_rows = pl.ds(start, count)
        return (
            sum_view(h, i, 0, start, count)[...].astype(F32)
            + r2[h, i, 0, copies_rows, :].astype(F32)
            + r2[h, i, 1, copies_rows, :].astype(F32)
        )

    def arrived_2(h, i):
        copies.arrived(("2+", h, i))
        copies.arrived(("2-", h, i))

    order = (2, 1, 3, 0)
    lo, hi = pl.ds(0, quarter), pl.ds(quarter, quarter)

    loads_waited = False
    for number, chunk in enumerate(CHUNKS):
        if number == 0:
            pass_second(0)
        if number == 1:
            have("a", 2, 0)
            both("a", 2, 0, "y")
            have("b", 0, 2)
            both("b", 0, 2, "z")
            pass_second(1)
        if number == 2:
            pass_second(3)
        if number == 3:
            pass_second(2)
        for dz, dy in chunk:
            have("a", dz, dy)
            have("b", dz, dy)
        if not loads_waited:
            for load in loads:
                load.wait()
            loads_waited = True
        run_experts(chunk)

    for i in order:
        for h in range(2):
            far_out(h, i)
    for i in order:
        for h in range(2):
            near_out(h, i)
    for h in range(2):
        arrived_2(h, 2)
        level[h, 2] = gathered(h, 2, 0, half).astype(BF16)
        copies.start(("3+", h), level.at[h, 2, lo], r3.at[h, lo], second[h][0])
        copies.start(("3-", h), level.at[h, 2, hi], r3.at[h, hi], second[h][1])
    for h in range(2):
        arrived_2(h, 1)
        copies.arrived(("3+", h))
        level[h, 1, lo, :] = (gathered(h, 1, 0, quarter) + r3[h, lo, :].astype(F32)).astype(BF16)
        level[h, 1, hi, :] = gathered(h, 1, quarter, quarter).astype(BF16)
        copies.start(("4+", h), level.at[h, 1], r4.at[h, 0], second[h][0])
        arrived_2(h, 3)
        copies.arrived(("3-", h))
        level[h, 3, lo, :] = gathered(h, 3, 0, quarter).astype(BF16)
        level[h, 3, hi, :] = (gathered(h, 3, quarter, quarter) + r3[h, hi, :].astype(F32)).astype(BF16)
        copies.start(("4-", h), level.at[h, 3], r4.at[h, 1], second[h][1])
    length = length_ref[0]
    for h in range(2):
        arrived_2(h, 0)
        copies.arrived(("4+", h))
        copies.arrived(("4-", h))
        span_rows = pl.ds(h * half, half)
        mixture = gathered(h, 0, 0, half) + r4[h, 0].astype(F32) + r4[h, 1].astype(F32)
        position = lax.broadcasted_iota(jnp.int32, (half, width), 0) + h * half
        out_ref[span_rows, :] = jnp.where(position < length, residual_ref[span_rows, :] + mixture, 0.0).astype(BF16)
    copies.drain()


def experts(length, normed, meta, residual, upward, downward, up_other, down_other):
    rows, width = normed.shape
    inner = downward.shape[0]
    half = rows // 2
    slots = SIDE * SIDE
    pairs = len(CHUNKS[0]) // 2
    dma = pltpu.SemaphoreType.DMA
    return pl.pallas_call(
        expert_kernel,
        out_shape=jax.ShapeDtypeStruct((rows, width), BF16),
        in_specs=[SMEM, VMEM, VMEM, VMEM, ANY, ANY, ANY, ANY],
        out_specs=VMEM,
        scratch_shapes=[
            pltpu.VMEM((slots, rows, width), BF16),
            pltpu.VMEM((2,) + upward.shape, BF16),
            pltpu.VMEM((2,) + downward.shape, BF16),
            pltpu.VMEM((2, pairs * 2 * CAP, width), BF16),
            pltpu.VMEM((pairs, 4 * CAP, 2 * rows), BF16),
            pltpu.VMEM((2, pairs * 2 * CAP, HD), F32),
            pltpu.VMEM((2, pairs * 2 * CAP, inner), BF16),
            pltpu.VMEM((slots, rows, width), BF16),
            pltpu.VMEM((2, SIDE, half, width), BF16),
            pltpu.VMEM((2, SIDE, 2, half, width), BF16),
            pltpu.VMEM((2, SIDE, half, width), BF16),
            pltpu.VMEM((2, half, width), BF16),
            pltpu.VMEM((2, 2, half, width), BF16),
            dma((112,)),
            dma((112,)),
            dma((4,)),
        ],
        compiler_params=pltpu.CompilerParams(
            collective_id=1, has_side_effects=True, vmem_limit_bytes=VMEM_LIMIT
        ),
        name="experts",
    )(length, normed, meta, residual, upward, downward, up_other, down_other)


def on_device(
    hidden_in, queries, suffix_pairs, prefix_cache, suffix_length, request_group, prefix_owner,
    out_weight, norm_gain, routes, gate_values, expert_upward, expert_downward,
):
    rows, width = hidden_in.shape[2:]
    length = suffix_length[0, 0]
    owner = prefix_owner[0, request_group[0, 0]]
    flag = (lax.broadcasted_iota(jnp.int32, (8, HD), 0) == owner).astype(F32)
    live = lax.broadcasted_iota(jnp.int32, (8, rows), 1) < length
    names = jnp.where(live, jnp.transpose(routes[0, 0]), -1).astype(F32)
    meta = jnp.concatenate([names, jnp.transpose(gate_values[0, 0])], axis=0)
    residual, normed, up_other, down_other, everyone = attend(
        flag, queries[0, 0], suffix_pairs[0, 0], prefix_cache[0, 0], out_weight, hidden_in[0, 0],
        norm_gain.reshape(1, width), expert_upward[0], expert_downward[0], meta,
    )
    out = experts(
        length.reshape(1), normed, everyone, residual, expert_upward[0], expert_downward[0], up_other, down_other
    )
    return out.reshape(1, 1, rows, width)


def solution(mesh):
    in_specs = (
        P("req", "exp", None, None),
        P("req", "exp", None, None),
        P("req", "exp", None, None, None),
        P("exp", "req", None, None, None),
        P("req", "exp"),
        P("req", "exp"),
        P("exp", None),
        P(),
        P(),
        P("req", "exp", None, None),
        P("req", "exp", None, None),
        P("exp", None, None),
        P("exp", None, None),
    )
    out_specs = P("req", "exp", None, None)
    return jax.shard_map(
        on_device, mesh=mesh, in_specs=in_specs, out_specs=out_specs, check_vma=False
    )
```

```python
import functools

import jax
import jax.numpy as jnp
from jax import lax
from jax.experimental import pallas as pl
from jax.experimental.pallas import tpu as pltpu
from jax.sharding import PartitionSpec as P

HD = 128
SINK = 4
SIDE = 4
CAP = 40
NEG = -1e30
MESH = pl.DeviceIdType.MESH
VMEM_LIMIT = 63 * 1024 * 1024
F32 = jnp.float32
BF16 = jnp.bfloat16
ANY = pl.BlockSpec(memory_space=pl.ANY)
VMEM = pl.BlockSpec(memory_space=pltpu.VMEM)
SMEM = pl.BlockSpec(memory_space=pltpu.SMEM)


def dot_t(a, b):
    return lax.dot_general(a, b, (((1,), (1,)), ((), ())), preferred_element_type=F32)


def dot(a, b):
    return jnp.dot(a, b, preferred_element_type=F32)


def dot_0(a, b):
    return lax.dot_general(a, b, (((0,), (0,)), ((), ())), preferred_element_type=F32)


class Copies:
    def __init__(self, send, recv):
        self.send, self.recv, self.made, self.gone = send, recv, {}, set()

    def start(self, key, src, dst, device):
        index = len(self.made)
        copy = pltpu.make_async_remote_copy(
            src_ref=src,
            dst_ref=dst,
            send_sem=self.send.at[index],
            recv_sem=self.recv.at[index],
            device_id=device,
            device_id_type=MESH,
        )
        copy.start()
        self.made[key] = copy

    def arrived(self, key):
        self.made[key].wait_recv()

    def left(self, key):
        self.made[key].wait_send()
        self.gone.add(key)

    def drain(self):
        for key, copy in self.made.items():
            if key not in self.gone:
                copy.wait_send()


def meet(devices):
    barrier = pltpu.get_barrier_semaphore()
    for device in devices:
        pl.semaphore_signal(barrier, inc=1, device_id=device, device_id_type=MESH)
    pl.semaphore_wait(barrier, len(devices))


def torus(req, e):
    core = lax.rem(e, 2)
    y = lax.rem(e // 2, SIDE)
    z = e // (2 * SIDE)

    def at(dz, dy):
        return (req, (lax.rem(z + dz, SIDE) * SIDE + lax.rem(y + dy, SIDE)) * 2 + core)

    return at(1, 0), at(3, 0), at(0, 1), at(0, 3)


GROUPS = 2
CHUNKS = (
    ((0, 0), (0, 1), (0, 3), (1, 0)),
    ((3, 0), (2, 0), (0, 2), (1, 1)),
    ((1, 3), (3, 1), (1, 2), (2, 1)),
    ((3, 3), (3, 2), (2, 3), (2, 2)),
)


def slot(dz, dy):
    return (dz % SIDE) * SIDE + dy % SIDE


def layer_kernel(
    length_ref, group_ref, owner_ref, q_ref, pairs_ref, cache_ref, weight_ref, hidden_ref, gain_ref,
    routes_ref, gates_ref, up_ref, down_ref,
    out_ref,
    qrows, flag, flags, cache, part, stat, stat_t, stat_in, own, own_stat, relay, back, attn,
    meta, tokens, up, down, pmat, gslot, hid, sums, r1, r2, r3, r4,
    send, recv, local,
):
    x, e = lax.axis_index("req"), lax.axis_index("exp")
    right, left, across = (
        (lax.rem(x + 1, SIDE), e),
        (lax.rem(x + 3, SIDE), e),
        (lax.rem(x + 2, SIDE), e),
    )
    other = (x, e + 1 - 2 * lax.rem(e, 2))
    zp, zm, yp, ym = torus(x, e)
    rows, width = q_ref.shape
    heads = width // HD
    window = cache_ref.shape[1]
    inner = down_ref.shape[0]
    half, quarter = rows // 2, rows // 4
    size = rows // GROUPS
    part_half = size // 2
    copies = Copies(send, recv)

    loads = {}
    for index, (key, src, dst) in enumerate(
        (
            ("cache", cache_ref, cache),
            ("weight", weight_ref, sums),
            ("up", up_ref, up.at[0]),
            ("down", down_ref, down.at[0]),
        )
    ):
        loads[key] = pltpu.make_async_copy(src, dst, local.at[index])
        loads[key].start()

    length = length_ref[0, 0]
    group = group_ref[0, 0]
    owner = jnp.int32(0)
    for k in range(SIDE):
        owner = jnp.where(group == k, owner_ref[0, k], owner)
    flag[...] = (lax.broadcasted_iota(jnp.int32, (8, HD), 0) == owner).astype(F32)
    live = lax.broadcasted_iota(jnp.int32, (8, rows), 1) < length
    meta[0, 0:8, :] = jnp.where(live, jnp.transpose(routes_ref[...].astype(F32)), -1.0)
    meta[0, 8:16, :] = jnp.transpose(gates_ref[...])
    meet([right, left, across, other, zp, zm, yp, ym])

    def rows_of(g, start=0, count=None):
        return pl.ds(g * size + start, size if count is None else count)

    def q_slot(d, span):
        return qrows.at[pl.ds((d - 1) * rows + span.start, span.size)]

    def q_out(g):
        copies.start(("q", 3, g), q_ref.at[rows_of(g)], q_slot(3, rows_of(g)), right)
        copies.start(("q", 1, g), q_ref.at[rows_of(g)], q_slot(1, rows_of(g)), left)

    def q_on(g):
        low, high = rows_of(g, 0, part_half), rows_of(g, part_half, part_half)
        copies.arrived(("q", 3, g))
        copies.start(("q2+", g), q_slot(3, low), q_slot(2, low), right)
        copies.arrived(("q", 1, g))
        copies.start(("q2-", g), q_slot(1, high), q_slot(2, high), left)

    q_out(0)
    copies.start("f3", flag, flags.at[2], right)
    copies.start("f1", flag, flags.at[0], left)
    copies.start("f2", flag, flags.at[1], across)

    def tell(tz, ty, source, device):
        copies.start(("m", tz, ty), meta.at[source], meta.at[slot(tz, ty)], device)

    def told(tz, ty):
        copies.arrived(("m", tz, ty))
        return slot(tz, ty)

    tell(3, 0, 0, zp)
    tell(1, 0, 0, zm)
    tell(0, 3, 0, yp)
    tell(0, 1, 0, ym)
    copies.start("up", up_ref, up.at[1], other)
    copies.start("down", down_ref, down.at[1], other)

    scale = HD ** (-0.5)
    lane = lax.broadcasted_iota(jnp.int32, (rows, HD), 1)
    lane_g = lax.broadcasted_iota(jnp.int32, (size, HD), 1)
    stat[...] = jnp.zeros_like(stat)
    own_stat[...] = jnp.zeros_like(own_stat)

    def softmax(scores, visible, values):
        masked = jnp.where(visible, scores, NEG)
        largest = jnp.max(masked, axis=1, keepdims=True)
        weights = jnp.exp(masked - largest)
        totals = jnp.sum(weights, axis=1, keepdims=True)
        return dot(weights.astype(BF16), values) * (1.0 / totals), largest + jnp.log(totals)

    def columns(h):
        return pl.ds(pl.multiple_of(h * HD, HD), HD)

    own_c = lax.broadcasted_iota(jnp.int32, (rows, rows), 1)
    own_t = lax.broadcasted_iota(jnp.int32, (rows, rows), 0)
    several = min(2, heads)

    @pl.loop(0, heads // several)
    def _(block):
        stats = own_stat[...]
        for k in range(several):
            h = block * several + k
            cols = columns(h)
            scores = dot_t(q_ref[:, cols], pairs_ref[0, :, cols]) * scale
            out, lse = softmax(scores, own_c <= own_t, pairs_ref[1, :, cols])
            own[:, cols] = out
            stats = jnp.where(lane == h, lse, stats)
        own_stat[...] = stats

    def prefix(g, slots):
        c = lax.broadcasted_iota(jnp.int32, (size, window), 1)
        t = lax.broadcasted_iota(jnp.int32, (size, window), 0) + g * size
        visible = (c < SINK) | (c > t)
        span = rows_of(g)
        valid = {d: (flag if d == 0 else flags.at[d - 1])[pl.ds(x, 1), :] for d in slots}
        several = min(4 // len(slots), heads)

        @pl.loop(0, heads // several)
        def _(block):
            stats = {d: stat[g, d, 0:size, :] for d in slots}
            for k in range(several):
                h = block * several + k
                cols = columns(h)
                for d in slots:
                    q = q_ref[span, cols] if d == 0 else q_slot(d, span)[:, cols]
                    out, lse = softmax(dot_t(q, cache[0, :, cols]) * scale, visible, cache[1, :, cols])
                    part[d, span, cols] = (out * valid[d]).astype(BF16)
                    stats[d] = jnp.where(lane_g == h, lse * valid[d], stats[d])
            for d in slots:
                stat[g, d, 0:size, :] = stats[d]

        for d in slots:
            stat_t[g, d] = jnp.transpose(stat[g, d])[0:heads, :]

    def direct_out(g):
        low, high = rows_of(g, 0, part_half), rows_of(g, part_half, part_half)
        copies.start(("r_high", g), part.at[1, high], back.at[0, high], right)
        copies.start(("l_low", g), part.at[3, low], back.at[1, low], left)
        copies.start(("s1", g), stat_t.at[g, 1], stat_in.at[g, 0], right)
        copies.start(("s3", g), stat_t.at[g, 3], stat_in.at[g, 1], left)

    def relay_out(g):
        low, high = rows_of(g, 0, part_half), rows_of(g, part_half, part_half)
        copies.start(("relay_r", g), part.at[2, low], relay.at[g, 0], right)
        copies.start(("relay_l", g), part.at[2, high], relay.at[g, 1], left)
        copies.start(("s2", g), stat_t.at[g, 2], stat_in.at[g, 2], across)

    def relay_on(g):
        low, high = rows_of(g, 0, part_half), rows_of(g, part_half, part_half)
        copies.arrived(("relay_r", g))
        part[1, low, :] = part[1, low, :] + relay[g, 0]
        copies.start(("r_low", g), part.at[1, low], back.at[0, low], right)
        copies.arrived(("relay_l", g))
        part[3, high, :] = part[3, high, :] + relay[g, 1]
        copies.start(("l_high", g), part.at[3, high], back.at[1, high], left)

    tile = min(256, width)

    def finish(g):
        for key in ("s1", "s2", "s3", "r_high", "l_low", "r_low", "l_high"):
            copies.arrived((key, g))
        span = rows_of(g)
        total_t = stat_t[g, 0] + stat_in[g, 0] + stat_in[g, 1] + stat_in[g, 2]
        stat[g, 0] = jnp.transpose(jnp.concatenate([total_t, jnp.zeros((HD - heads, rows), F32)], axis=0))
        several = min(4, heads)

        @pl.loop(0, heads // several)
        def _(block):
            for k in range(several):
                h = block * several + k
                cols = columns(h)
                first = part[0, span, cols].astype(F32) + back[0, span, cols].astype(F32) + back[1, span, cols].astype(F32)
                lse_first = jnp.sum(jnp.where(lane_g == h, stat[g, 0, 0:size, :], 0.0), axis=1, keepdims=True)
                lse_own = jnp.sum(jnp.where(lane_g == h, own_stat[span, :], 0.0), axis=1, keepdims=True)
                top = jnp.maximum(lse_first, lse_own)
                a, b = jnp.exp(lse_first - top), jnp.exp(lse_own - top)
                attn[:, cols] = ((a * first + b * own[span, cols]) * (1.0 / (a + b))).astype(BF16)

        if g == 0:
            loads["weight"].wait()

        def project(j, squares):
            cols = pl.ds(pl.multiple_of(j * tile, tile), tile)
            weight = sums[:, :, cols].reshape(width, tile)
            res = hidden_ref[span, cols].astype(F32) + dot(attn[...], weight)
            own[span, cols] = res
            return squares + jnp.sum(res * res, axis=1, keepdims=True)

        squares = lax.fori_loop(0, width // tile, project, jnp.zeros((size, 1), F32))
        factor = lax.rsqrt(squares / width + 1e-05)

        @pl.loop(0, width // tile)
        def _(j):
            cols = pl.ds(pl.multiple_of(j * tile, tile), tile)
            tokens[0, span, cols] = (own[span, cols] * factor * gain_ref[:, cols]).astype(BF16)

    def view(dz, dy, start, count):
        return tokens.at[slot(dz, dy), pl.ds(start, count)]

    def start_of(kind):
        return kind[1] * size + (part_half if kind[0] == "b" else 0)

    def push(key, dz, dy, axis, step, start, count):
        device = {("z", 1): zp, ("z", -1): zm, ("y", 1): yp, ("y", -1): ym}[axis, step]
        tz, ty = ((dz - step) % SIDE, dy) if axis == "z" else (dz, (dy - step) % SIDE)
        copies.start((key, tz, ty), view(dz, dy, start, count), view(tz, ty, start, count), device)

    def both(kind, dz, dy, axis):
        push(kind, dz, dy, axis, 1, start_of(kind), part_half)
        push(kind, dz, dy, axis, -1, start_of(kind), part_half)

    def pass_on(kind, dz, dy, axis):
        behind = (dz if axis == "z" else dy) == 3
        start = start_of(kind) + (0 if behind else part_half // 2)
        push((kind, behind), dz, dy, axis, 1 if behind else -1, start, part_half // 2)

    waited = set()

    def have(kind, dz, dy):
        first, last = (dz, dy) if kind[0] == "a" else (dy, dz)
        if first == 0 and last == 0:
            return
        split = last == 2 or (last == 0 and first == 2)
        for key in ([(kind, True), (kind, False)] if split else [kind]):
            if (key, dz, dy) not in waited:
                waited.add((key, dz, dy))
                copies.arrived((key, dz, dy))

    def spread_0(g):
        both(("a", g), 0, 0, "z")
        both(("b", g), 0, 0, "y")
        both(("a", g), 0, 0, "y")
        both(("b", g), 0, 0, "z")

    def spread_1(g):
        for d in (3, 1):
            have(("a", g), d, 0)
            pass_on(("a", g), d, 0, "z")
            both(("a", g), d, 0, "y")
            have(("b", g), 0, d)
            pass_on(("b", g), 0, d, "y")
            both(("b", g), 0, d, "z")

    def spread_far(g):
        have(("a", g), 2, 0)
        both(("a", g), 2, 0, "y")
        have(("b", g), 0, 2)
        both(("b", g), 0, 2, "z")

    def pass_second(g, d):
        for near in (3, 1):
            have(("a", g), d, near)
            pass_on(("a", g), d, near, "y")
            have(("b", g), near, d)
            pass_on(("b", g), near, d, "z")

    ids = [e.astype(F32), (e + 1 - 2 * lax.rem(e, 2)).astype(F32)]
    span2 = 2 * CAP
    count = len(CHUNKS[0]) * CAP
    before = (
        lax.broadcasted_iota(jnp.int32, (rows, rows), 0) < lax.broadcasted_iota(jnp.int32, (rows, rows), 1)
    ).astype(BF16)
    slot_row = lax.broadcasted_iota(jnp.int32, (span2, rows), 0).astype(F32)

    def run_experts(chunk):
        pairs = [chunk[i:i + 2] for i in range(0, len(chunk), 2)]
        for p, pair in enumerate(pairs):
            for k in range(2):
                gates = jnp.zeros((span2, 1), F32)
                for i, (dz, dy) in enumerate(pair):
                    source = slot(dz, dy)
                    named = (meta[source, 0:8, :] == ids[k]).astype(F32)
                    mine = jnp.sum(named, axis=0, keepdims=True)
                    gate = jnp.sum(named * meta[source, 8:16, :], axis=0, keepdims=True)
                    rank = dot(jnp.broadcast_to(mine, (8, rows)).astype(BF16), before)[0:1, :]
                    place = jnp.where(mine > 0.0, rank + float(i * CAP), -1.0)
                    chosen = (slot_row == place).astype(F32)
                    pmat[p, k * span2:(k + 1) * span2, i * rows:(i + 1) * rows] = chosen.astype(BF16)
                    gates = gates + jnp.sum(chosen * gate, axis=1, keepdims=True)
                gslot[k, p * span2:(p + 1) * span2, :] = jnp.broadcast_to(gates, (span2, HD))
        tile = min(512, width)

        @pl.loop(0, width // tile)
        def _(j):
            cols = pl.ds(pl.multiple_of(j * tile, tile), tile)
            for p, pair in enumerate(pairs):
                joint = jnp.concatenate([tokens[slot(dz, dy), :, cols] for dz, dy in pair], axis=0)
                rows_out = dot(pmat[p], joint).astype(BF16)
                for k in range(2):
                    qrows[k * count + p * span2:k * count + (p + 1) * span2, cols] = rows_out[k * span2:(k + 1) * span2, :]

        tile_f = min(256, inner)

        @pl.loop(0, inner // tile_f)
        def _(j):
            start = pl.multiple_of(j * tile_f, tile_f)
            for k in range(2):
                gate = dot(qrows[k * count:(k + 1) * count, :], up[k, :, pl.ds(start, tile_f)])
                lift = dot(qrows[k * count:(k + 1) * count, :], up[k, :, pl.ds(pl.multiple_of(inner + start, tile_f), tile_f)])
                hid[k, :, pl.ds(start, tile_f)] = (gate / (1.0 + jnp.exp(-gate)) * lift).astype(BF16)

        tile_d = min(256, width)

        @pl.loop(0, width // tile_d)
        def _(j):
            cols = pl.ds(pl.multiple_of(j * tile_d, tile_d), tile_d)
            made = []
            for k in range(2):
                made.append((dot(hid[k], down[k, :, cols]) * gslot[k, :, 0:1]).astype(BF16))
            for p, pair in enumerate(pairs):
                joint = jnp.concatenate([m[p * span2:(p + 1) * span2, :] for m in made], axis=0)
                placed = dot_0(pmat[p], joint).astype(BF16)
                for i, (dz, dy) in enumerate(pair):
                    sums[slot(dz, dy), :, cols] = placed[i * rows:(i + 1) * rows, :]

    def sum_view(h, i, j, start, count):
        dz, dy = (i, j) if h == 0 else (j, i)
        return sums.at[slot(dz, dy), pl.ds(h * half + start, count)]

    first = ((yp, ym), (zp, zm))
    second = ((zp, zm), (yp, ym))

    def far_out(h, i):
        copies.start(("1+", h, i), sum_view(h, i, 2, 0, quarter), r1.at[h, i, pl.ds(0, quarter)], first[h][0])
        copies.start(("1-", h, i), sum_view(h, i, 2, quarter, quarter), r1.at[h, i, pl.ds(quarter, quarter)], first[h][1])

    def add_to(ref, more):
        ref[...] = (ref[...].astype(F32) + more[...].astype(F32)).astype(BF16)

    def near_out(h, i):
        copies.arrived(("1+", h, i))
        add_to(sum_view(h, i, 1, 0, quarter), r1.at[h, i, pl.ds(0, quarter)])
        copies.start(("2+", h, i), sum_view(h, i, 1, 0, half), r2.at[h, i, 0], first[h][0])
        copies.arrived(("1-", h, i))
        add_to(sum_view(h, i, 3, quarter, quarter), r1.at[h, i, pl.ds(quarter, quarter)])
        copies.start(("2-", h, i), sum_view(h, i, 3, 0, half), r2.at[h, i, 1], first[h][1])

    def gathered(h, i, start, count):
        span = pl.ds(start, count)
        return (
            sum_view(h, i, 0, start, count)[...].astype(F32)
            + r2[h, i, 0, span, :].astype(F32)
            + r2[h, i, 1, span, :].astype(F32)
        )

    def arrived_2(h, i):
        copies.arrived(("2+", h, i))
        copies.arrived(("2-", h, i))

    loads["cache"].wait()
    prefix(0, [0])
    q_on(0)
    q_out(1)
    copies.arrived("f1")
    copies.arrived("f3")
    prefix(0, [1, 3])
    direct_out(0)
    copies.arrived(("q2+", 0))
    copies.arrived(("q2-", 0))
    copies.arrived("f2")
    prefix(0, [2])
    relay_out(0)
    for d in (3, 1):
        source = told(d, 0)
        tell(d, 3, source, yp)
        tell(d, 1, source, ym)
        if d == 3:
            tell(2, 0, source, zp)
    prefix(1, [0])
    relay_on(0)
    q_on(1)
    source = told(2, 0)
    tell(2, 3, source, yp)
    tell(2, 1, source, ym)
    prefix(1, [1, 3])
    direct_out(1)
    finish(0)
    spread_0(0)
    for d in range(SIDE):
        tell(d, 2, told(d, 3), yp)
    copies.arrived(("q2+", 1))
    copies.arrived(("q2-", 1))
    prefix(1, [2])
    relay_out(1)
    spread_1(0)
    relay_on(1)
    pass_second(0, 0)
    spread_far(0)
    for d in range(SIDE):
        told(d, 1)
        told(d, 2)
    finish(1)
    spread_0(1)
    pass_second(0, 1)
    pass_second(0, 3)
    spread_1(1)
    pass_second(0, 2)
    pass_second(1, 0)
    for key in ("up", "down"):
        loads[key].wait()
        copies.arrived(key)
    for g in range(GROUPS):
        for key in ("q2+", "q2-", "r_high", "l_low", "relay_r", "relay_l", "r_low", "l_high"):
            copies.left((key, g))

    def run(chunk):
        for dz, dy in chunk:
            for g in range(GROUPS):
                have(("a", g), dz, dy)
                have(("b", g), dz, dy)
        run_experts(chunk)

    run(CHUNKS[0])
    spread_far(1)
    pass_second(1, 1)
    run(CHUNKS[1])
    pass_second(1, 3)
    pass_second(1, 2)
    run(CHUNKS[2])
    for i in (0, 1):
        for h in range(2):
            far_out(h, i)
    run(CHUNKS[3])
    for i in (2, 3):
        for h in range(2):
            far_out(h, i)

    level = part
    lo, hi = pl.ds(0, quarter), pl.ds(quarter, quarter)

    def level_rows(h, start, count):
        return pl.ds(h * half + start, count)

    for i in (2, 1, 3, 0):
        for h in range(2):
            near_out(h, i)
    for h in range(2):
        arrived_2(h, 2)
        level[2, level_rows(h, 0, half), :] = gathered(h, 2, 0, half).astype(BF16)
        copies.start(("3+", h), level.at[2, level_rows(h, 0, quarter)], r3.at[h, lo], second[h][0])
        copies.start(("3-", h), level.at[2, level_rows(h, quarter, quarter)], r3.at[h, hi], second[h][1])
    for h in range(2):
        arrived_2(h, 1)
        copies.arrived(("3+", h))
        level[1, level_rows(h, 0, quarter), :] = (gathered(h, 1, 0, quarter) + r3[h, lo, :].astype(F32)).astype(BF16)
        level[1, level_rows(h, quarter, quarter), :] = gathered(h, 1, quarter, quarter).astype(BF16)
        copies.start(("4+", h), level.at[1, level_rows(h, 0, half)], r4.at[h, 0], second[h][0])
        arrived_2(h, 3)
        copies.arrived(("3-", h))
        level[3, level_rows(h, 0, quarter), :] = gathered(h, 3, 0, quarter).astype(BF16)
        level[3, level_rows(h, quarter, quarter), :] = (gathered(h, 3, quarter, quarter) + r3[h, hi, :].astype(F32)).astype(BF16)
        copies.start(("4-", h), level.at[3, level_rows(h, 0, half)], r4.at[h, 1], second[h][1])
    for h in range(2):
        arrived_2(h, 0)
        copies.arrived(("4+", h))
        copies.arrived(("4-", h))
        span = pl.ds(h * half, half)
        mixture = gathered(h, 0, 0, half) + r4[h, 0].astype(F32) + r4[h, 1].astype(F32)
        position = lax.broadcasted_iota(jnp.int32, (half, width), 0) + h * half
        out_ref[span, :] = jnp.where(position < length, own[span, :] + mixture, 0.0).astype(BF16)
    copies.drain()


def layer(length, group, owner, queries, pairs, cache, weight, hidden, gain, routes, gates, upward, downward):
    rows, width = queries.shape
    heads = width // HD
    inner = downward.shape[0]
    half = rows // 2
    slots = SIDE * SIDE
    count = len(CHUNKS[0]) * CAP
    dma = pltpu.SemaphoreType.DMA
    return pl.pallas_call(
        layer_kernel,
        out_shape=jax.ShapeDtypeStruct((rows, width), BF16),
        in_specs=[SMEM, SMEM, SMEM, VMEM, VMEM, ANY, ANY, VMEM, VMEM, VMEM, VMEM, ANY, ANY],
        out_specs=VMEM,
        scratch_shapes=[
            pltpu.VMEM((3 * rows, width), BF16),
            pltpu.VMEM((8, HD), F32),
            pltpu.VMEM((3, 8, HD), F32),
            pltpu.VMEM(cache.shape, BF16),
            pltpu.VMEM((4, rows, width), BF16),
            pltpu.VMEM((GROUPS, 4, rows, HD), F32),
            pltpu.VMEM((GROUPS, 4, heads, rows), F32),
            pltpu.VMEM((GROUPS, 3, heads, rows), F32),
            pltpu.VMEM((rows, width), F32),
            pltpu.VMEM((rows, HD), F32),
            pltpu.VMEM((GROUPS, 2, rows // GROUPS // 2, width), BF16),
            pltpu.VMEM((2, rows, width), BF16),
            pltpu.VMEM((rows // GROUPS, width), BF16),
            pltpu.VMEM((slots, 16, rows), F32),
            pltpu.VMEM((slots, rows, width), BF16),
            pltpu.VMEM((2,) + upward.shape, BF16),
            pltpu.VMEM((2,) + downward.shape, BF16),
            pltpu.VMEM((len(CHUNKS[0]) // 2, 4 * CAP, 2 * rows), BF16),
            pltpu.VMEM((2, count, HD), F32),
            pltpu.VMEM((2, count, inner), BF16),
            pltpu.VMEM((slots, width // slots, width), BF16),
            pltpu.VMEM((2, SIDE, half, width), BF16),
            pltpu.VMEM((2, SIDE, 2, half, width), BF16),
            pltpu.VMEM((2, half, width), BF16),
            pltpu.VMEM((2, 2, half, width), BF16),
            dma((180,)),
            dma((180,)),
            dma((4,)),
        ],
        compiler_params=pltpu.CompilerParams(
            collective_id=0, has_side_effects=True, vmem_limit_bytes=VMEM_LIMIT
        ),
        name="layer",
    )(
        length, group, owner, queries, pairs, cache, weight.reshape(slots, width // slots, width), hidden, gain,
        routes, gates, upward, downward,
    )


def on_device(
    hidden_in, queries, suffix_pairs, prefix_cache, suffix_length, request_group, prefix_owner,
    out_weight, norm_gain, routes, gate_values, expert_upward, expert_downward,
):
    rows, width = hidden_in.shape[2:]
    out = layer(
        suffix_length, request_group, prefix_owner, queries[0, 0], suffix_pairs[0, 0], prefix_cache[0, 0], out_weight,
        hidden_in[0, 0], norm_gain.reshape(1, width), routes[0, 0], gate_values[0, 0], expert_upward[0], expert_downward[0],
    )
    return out.reshape(1, 1, rows, width)


def solution(mesh):
    in_specs = (
        P("req", "exp", None, None),
        P("req", "exp", None, None),
        P("req", "exp", None, None, None),
        P("exp", "req", None, None, None),
        P("req", "exp"),
        P("req", "exp"),
        P("exp", None),
        P(),
        P(),
        P("req", "exp", None, None),
        P("req", "exp", None, None),
        P("exp", None, None),
        P("exp", None, None),
    )
    out_specs = P("req", "exp", None, None)
    return jax.shard_map(
        on_device, mesh=mesh, in_specs=in_specs, out_specs=out_specs, check_vma=False
    )
```

```python
import functools

import jax
import jax.numpy as jnp
from jax import lax
from jax.experimental import pallas as pl
from jax.experimental.pallas import tpu as pltpu
from jax.sharding import PartitionSpec as P

HD = 128
SINK = 4
SIDE = 4
CAP = 40
NEG = -1e30
MESH = pl.DeviceIdType.MESH
VMEM_LIMIT = 63 * 1024 * 1024
F32 = jnp.float32
BF16 = jnp.bfloat16
ANY = pl.BlockSpec(memory_space=pl.ANY)
VMEM = pl.BlockSpec(memory_space=pltpu.VMEM)
SMEM = pl.BlockSpec(memory_space=pltpu.SMEM)


def dot_t(a, b):
    return lax.dot_general(a, b, (((1,), (1,)), ((), ())), preferred_element_type=F32)


def dot(a, b):
    return jnp.dot(a, b, preferred_element_type=F32)


def dot_0(a, b):
    return lax.dot_general(a, b, (((0,), (0,)), ((), ())), preferred_element_type=F32)


class Copies:
    def __init__(self, send, recv):
        self.send, self.recv, self.made, self.gone = send, recv, {}, set()

    def start(self, key, src, dst, device):
        index = len(self.made)
        copy = pltpu.make_async_remote_copy(
            src_ref=src,
            dst_ref=dst,
            send_sem=self.send.at[index],
            recv_sem=self.recv.at[index],
            device_id=device,
            device_id_type=MESH,
        )
        copy.start()
        self.made[key] = copy

    def arrived(self, key):
        self.made[key].wait_recv()

    def left(self, key):
        self.made[key].wait_send()
        self.gone.add(key)

    def drain(self):
        for key, copy in self.made.items():
            if key not in self.gone:
                copy.wait_send()


def meet(devices):
    barrier = pltpu.get_barrier_semaphore()
    for device in devices:
        pl.semaphore_signal(barrier, inc=1, device_id=device, device_id_type=MESH)
    pl.semaphore_wait(barrier, len(devices))


def torus(req, e):
    core = lax.rem(e, 2)
    y = lax.rem(e // 2, SIDE)
    z = e // (2 * SIDE)

    def at(dz, dy):
        return (req, (lax.rem(z + dz, SIDE) * SIDE + lax.rem(y + dy, SIDE)) * 2 + core)

    return at(1, 0), at(3, 0), at(0, 1), at(0, 3)


GROUPS = 2
CHUNKS = (
    ((0, 0), (0, 1), (0, 3), (1, 0)),
    ((0, 2), (2, 0), (1, 2), (2, 1)),
    ((2, 2), (3, 2), (2, 3), (3, 0)),
    ((1, 1), (1, 3), (3, 1), (3, 3)),
)


def slot(dz, dy):
    return (dz % SIDE) * SIDE + dy % SIDE


def layer_kernel(
    length_ref, group_ref, owner_ref, q_ref, pairs_ref, cache_ref, weight_ref, hidden_ref, gain_ref,
    routes_ref, gates_ref, up_ref, down_ref,
    out_ref,
    qrows, flag, flags, cache, part, stat, stat_t, stat_in, own, own_stat, relay, back, attn,
    meta, tokens, up, down, pmat, gslot, hid, sums, r1, r2, r3, r4,
    send, recv, local,
):
    x, e = lax.axis_index("req"), lax.axis_index("exp")
    right, left, across = (
        (lax.rem(x + 1, SIDE), e),
        (lax.rem(x + 3, SIDE), e),
        (lax.rem(x + 2, SIDE), e),
    )
    other = (x, e + 1 - 2 * lax.rem(e, 2))
    zp, zm, yp, ym = torus(x, e)
    rows, width = q_ref.shape
    heads = width // HD
    window = cache_ref.shape[1]
    inner = down_ref.shape[0]
    half, quarter = rows // 2, rows // 4
    size = rows // GROUPS
    part_half = size // 2
    copies = Copies(send, recv)

    loads = {}
    for index, (key, src, dst) in enumerate(
        (
            ("cache", cache_ref, cache),
            ("weight", weight_ref, sums),
            ("up", up_ref, up.at[0]),
            ("down", down_ref, down.at[0]),
        )
    ):
        loads[key] = pltpu.make_async_copy(src, dst, local.at[index])
        loads[key].start()

    length = length_ref[0, 0]
    group = group_ref[0, 0]
    owner = jnp.int32(0)
    for k in range(SIDE):
        owner = jnp.where(group == k, owner_ref[0, k], owner)
    flag[...] = (lax.broadcasted_iota(jnp.int32, (8, HD), 0) == owner).astype(F32)
    live = lax.broadcasted_iota(jnp.int32, (8, rows), 1) < length
    meta[0, 0:8, :] = jnp.where(live, jnp.transpose(routes_ref[...].astype(F32)), -1.0)
    meta[0, 8:16, :] = jnp.transpose(gates_ref[...])
    meet([right, left, across, other, zp, zm, yp, ym])

    def rows_of(g, start=0, count=None):
        return pl.ds(g * size + start, size if count is None else count)

    def q_slot(d, span):
        return qrows.at[pl.ds((d - 1) * rows + span.start, span.size)]

    def q_out(g):
        copies.start(("q", 3, g), q_ref.at[rows_of(g)], q_slot(3, rows_of(g)), right)
        copies.start(("q", 1, g), q_ref.at[rows_of(g)], q_slot(1, rows_of(g)), left)

    def q_on(g):
        low, high = rows_of(g, 0, part_half), rows_of(g, part_half, part_half)
        copies.arrived(("q", 3, g))
        copies.start(("q2+", g), q_slot(3, low), q_slot(2, low), right)
        copies.arrived(("q", 1, g))
        copies.start(("q2-", g), q_slot(1, high), q_slot(2, high), left)

    q_out(0)
    copies.start("f3", flag, flags.at[2], right)
    copies.start("f1", flag, flags.at[0], left)
    copies.start("f2", flag, flags.at[1], across)

    def tell(tz, ty, source, device):
        copies.start(("m", tz, ty), meta.at[source], meta.at[slot(tz, ty)], device)

    def told(tz, ty):
        copies.arrived(("m", tz, ty))
        return slot(tz, ty)

    tell(3, 0, 0, zp)
    tell(1, 0, 0, zm)
    tell(0, 3, 0, yp)
    tell(0, 1, 0, ym)
    copies.start("up", up_ref, up.at[1], other)
    copies.start("down", down_ref, down.at[1], other)

    scale = HD ** (-0.5)
    lane = lax.broadcasted_iota(jnp.int32, (rows, HD), 1)
    lane_g = lax.broadcasted_iota(jnp.int32, (size, HD), 1)
    stat[...] = jnp.zeros_like(stat)
    own_stat[...] = jnp.zeros_like(own_stat)

    def softmax(scores, visible, values):
        masked = jnp.where(visible, scores, NEG)
        largest = jnp.max(masked, axis=1, keepdims=True)
        weights = jnp.exp(masked - largest)
        totals = jnp.sum(weights, axis=1, keepdims=True)
        return dot(weights.astype(BF16), values) * (1.0 / totals), largest + jnp.log(totals)

    def columns(h):
        return pl.ds(pl.multiple_of(h * HD, HD), HD)

    own_c = lax.broadcasted_iota(jnp.int32, (rows, rows), 1)
    own_t = lax.broadcasted_iota(jnp.int32, (rows, rows), 0)

    def own_part():
        several = min(2, heads)

        @pl.loop(0, heads // several)
        def _(block):
            stats = own_stat[...]
            for k in range(several):
                h = block * several + k
                cols = columns(h)
                scores = dot_t(q_ref[:, cols], pairs_ref[0, :, cols]) * scale
                out, lse = softmax(scores, own_c <= own_t, pairs_ref[1, :, cols])
                own[:, cols] = out
                stats = jnp.where(lane == h, lse, stats)
            own_stat[...] = stats

    def prefix(g, slots):
        c = lax.broadcasted_iota(jnp.int32, (size, window), 1)
        t = lax.broadcasted_iota(jnp.int32, (size, window), 0) + g * size
        visible = (c < SINK) | (c > t)
        span = rows_of(g)
        valid = {d: (flag if d == 0 else flags.at[d - 1])[pl.ds(x, 1), :] for d in slots}
        several = min(4 // len(slots), heads)

        @pl.loop(0, heads // several)
        def _(block):
            stats = {d: stat[g, d, 0:size, :] for d in slots}
            for k in range(several):
                h = block * several + k
                cols = columns(h)
                for d in slots:
                    q = q_ref[span, cols] if d == 0 else q_slot(d, span)[:, cols]
                    out, lse = softmax(dot_t(q, cache[0, :, cols]) * scale, visible, cache[1, :, cols])
                    part[d, span, cols] = (out * valid[d]).astype(BF16)
                    stats[d] = jnp.where(lane_g == h, lse * valid[d], stats[d])
            for d in slots:
                stat[g, d, 0:size, :] = stats[d]

        for d in slots:
            stat_t[g, d] = jnp.transpose(stat[g, d])[0:heads, :]

    def direct_out(g):
        low, high = rows_of(g, 0, part_half), rows_of(g, part_half, part_half)
        copies.start(("r_high", g), part.at[1, high], back.at[0, high], right)
        copies.start(("l_low", g), part.at[3, low], back.at[1, low], left)
        copies.start(("s1", g), stat_t.at[g, 1], stat_in.at[g, 0], right)
        copies.start(("s3", g), stat_t.at[g, 3], stat_in.at[g, 1], left)

    def relay_out(g):
        low, high = rows_of(g, 0, part_half), rows_of(g, part_half, part_half)
        copies.start(("relay_r", g), part.at[2, low], relay.at[g, 0], right)
        copies.start(("relay_l", g), part.at[2, high], relay.at[g, 1], left)
        copies.start(("s2", g), stat_t.at[g, 2], stat_in.at[g, 2], across)

    def relay_on(g):
        low, high = rows_of(g, 0, part_half), rows_of(g, part_half, part_half)
        copies.arrived(("relay_r", g))
        part[1, low, :] = part[1, low, :] + relay[g, 0]
        copies.start(("r_low", g), part.at[1, low], back.at[0, low], right)
        copies.arrived(("relay_l", g))
        part[3, high, :] = part[3, high, :] + relay[g, 1]
        copies.start(("l_high", g), part.at[3, high], back.at[1, high], left)

    tile = min(256, width)

    def finish(g):
        for key in ("s1", "s2", "s3", "r_high", "l_low", "r_low", "l_high"):
            copies.arrived((key, g))
        span = rows_of(g)
        total_t = stat_t[g, 0] + stat_in[g, 0] + stat_in[g, 1] + stat_in[g, 2]
        stat[g, 0] = jnp.transpose(jnp.concatenate([total_t, jnp.zeros((HD - heads, rows), F32)], axis=0))
        several = min(4, heads)

        @pl.loop(0, heads // several)
        def _(block):
            for k in range(several):
                h = block * several + k
                cols = columns(h)
                first = part[0, span, cols].astype(F32) + back[0, span, cols].astype(F32) + back[1, span, cols].astype(F32)
                lse_first = jnp.sum(jnp.where(lane_g == h, stat[g, 0, 0:size, :], 0.0), axis=1, keepdims=True)
                lse_own = jnp.sum(jnp.where(lane_g == h, own_stat[span, :], 0.0), axis=1, keepdims=True)
                top = jnp.maximum(lse_first, lse_own)
                a, b = jnp.exp(lse_first - top), jnp.exp(lse_own - top)
                attn[:, cols] = ((a * first + b * own[span, cols]) * (1.0 / (a + b))).astype(BF16)

        if g == 0:
            loads["weight"].wait()

        def project(j, squares):
            cols = pl.ds(pl.multiple_of(j * tile, tile), tile)
            weight = sums[:, :, cols].reshape(width, tile)
            res = hidden_ref[span, cols].astype(F32) + dot(attn[...], weight)
            own[span, cols] = res
            return squares + jnp.sum(res * res, axis=1, keepdims=True)

        squares = lax.fori_loop(0, width // tile, project, jnp.zeros((size, 1), F32))
        factor = lax.rsqrt(squares / width + 1e-05)

        @pl.loop(0, width // tile)
        def _(j):
            cols = pl.ds(pl.multiple_of(j * tile, tile), tile)
            tokens[0, span, cols] = (own[span, cols] * factor * gain_ref[:, cols]).astype(BF16)

    def view(dz, dy, start, count):
        return tokens.at[slot(dz, dy), pl.ds(start, count)]

    def start_of(kind):
        return kind[1] * size + (part_half if kind[0] == "b" else 0)

    def push(key, dz, dy, axis, step, start, count):
        device = {("z", 1): zp, ("z", -1): zm, ("y", 1): yp, ("y", -1): ym}[axis, step]
        tz, ty = ((dz - step) % SIDE, dy) if axis == "z" else (dz, (dy - step) % SIDE)
        copies.start((key, tz, ty), view(dz, dy, start, count), view(tz, ty, start, count), device)

    def both(kind, dz, dy, axis):
        push(kind, dz, dy, axis, 1, start_of(kind), part_half)
        push(kind, dz, dy, axis, -1, start_of(kind), part_half)

    def pass_on(kind, dz, dy, axis):
        behind = (dz if axis == "z" else dy) == 3
        start = start_of(kind) + (0 if behind else part_half // 2)
        push((kind, behind), dz, dy, axis, 1 if behind else -1, start, part_half // 2)

    waited = set()

    def have(kind, dz, dy):
        first, last = (dz, dy) if kind[0] == "a" else (dy, dz)
        if first == 0 and last == 0:
            return
        split = last == 2 or (last == 0 and first == 2)
        for key in ([(kind, True), (kind, False)] if split else [kind]):
            if (key, dz, dy) not in waited:
                waited.add((key, dz, dy))
                copies.arrived((key, dz, dy))

    def spread_0(g):
        both(("a", g), 0, 0, "z")
        both(("b", g), 0, 0, "y")
        both(("a", g), 0, 0, "y")
        both(("b", g), 0, 0, "z")

    def spread_1(g):
        for d in (3, 1):
            have(("a", g), d, 0)
            pass_on(("a", g), d, 0, "z")
            both(("a", g), d, 0, "y")
            have(("b", g), 0, d)
            pass_on(("b", g), 0, d, "y")
            both(("b", g), 0, d, "z")

    def spread_far(g):
        have(("a", g), 2, 0)
        both(("a", g), 2, 0, "y")
        have(("b", g), 0, 2)
        both(("b", g), 0, 2, "z")

    def pass_second(g, d):
        for near in (3, 1):
            have(("a", g), d, near)
            pass_on(("a", g), d, near, "y")
            have(("b", g), near, d)
            pass_on(("b", g), near, d, "z")

    ids = [e.astype(F32), (e + 1 - 2 * lax.rem(e, 2)).astype(F32)]
    span2 = 2 * CAP
    count = len(CHUNKS[0]) * CAP
    before = (
        lax.broadcasted_iota(jnp.int32, (rows, rows), 0) < lax.broadcasted_iota(jnp.int32, (rows, rows), 1)
    ).astype(BF16)
    slot_row = lax.broadcasted_iota(jnp.int32, (span2, rows), 0).astype(F32)

    def run_experts(chunk):
        pairs = [chunk[i:i + 2] for i in range(0, len(chunk), 2)]
        for p, pair in enumerate(pairs):
            for k in range(2):
                gates = jnp.zeros((span2, 1), F32)
                for i, (dz, dy) in enumerate(pair):
                    source = slot(dz, dy)
                    named = (meta[source, 0:8, :] == ids[k]).astype(F32)
                    mine = jnp.sum(named, axis=0, keepdims=True)
                    gate = jnp.sum(named * meta[source, 8:16, :], axis=0, keepdims=True)
                    rank = dot(jnp.broadcast_to(mine, (8, rows)).astype(BF16), before)[0:1, :]
                    place = jnp.where(mine > 0.0, rank + float(i * CAP), -1.0)
                    chosen = (slot_row == place).astype(F32)
                    pmat[p, k * span2:(k + 1) * span2, i * rows:(i + 1) * rows] = chosen.astype(BF16)
                    gates = gates + jnp.sum(chosen * gate, axis=1, keepdims=True)
                gslot[k, p * span2:(p + 1) * span2, :] = jnp.broadcast_to(gates, (span2, HD))
        tile = min(512, width)

        @pl.loop(0, width // tile)
        def _(j):
            cols = pl.ds(pl.multiple_of(j * tile, tile), tile)
            for p, pair in enumerate(pairs):
                joint = jnp.concatenate([tokens[slot(dz, dy), :, cols] for dz, dy in pair], axis=0)
                rows_out = dot(pmat[p], joint).astype(BF16)
                for k in range(2):
                    qrows[k * count + p * span2:k * count + (p + 1) * span2, cols] = rows_out[k * span2:(k + 1) * span2, :]

        tile_f = min(256, inner)

        @pl.loop(0, inner // tile_f)
        def _(j):
            start = pl.multiple_of(j * tile_f, tile_f)
            for k in range(2):
                gate = dot(qrows[k * count:(k + 1) * count, :], up[k, :, pl.ds(start, tile_f)])
                lift = dot(qrows[k * count:(k + 1) * count, :], up[k, :, pl.ds(pl.multiple_of(inner + start, tile_f), tile_f)])
                hid[k, :, pl.ds(start, tile_f)] = (gate / (1.0 + jnp.exp(-gate)) * lift).astype(BF16)

        tile_d = min(256, width)

        @pl.loop(0, width // tile_d)
        def _(j):
            cols = pl.ds(pl.multiple_of(j * tile_d, tile_d), tile_d)
            made = []
            for k in range(2):
                made.append((dot(hid[k], down[k, :, cols]) * gslot[k, :, 0:1]).astype(BF16))
            for p, pair in enumerate(pairs):
                joint = jnp.concatenate([m[p * span2:(p + 1) * span2, :] for m in made], axis=0)
                placed = dot_0(pmat[p], joint).astype(BF16)
                for i, (dz, dy) in enumerate(pair):
                    sums[slot(dz, dy), :, cols] = placed[i * rows:(i + 1) * rows, :]

    def sum_view(h, i, j, start, count):
        dz, dy = (i, j) if h == 0 else (j, i)
        return sums.at[slot(dz, dy), pl.ds(h * half + start, count)]

    first = ((yp, ym), (zp, zm))
    second = ((zp, zm), (yp, ym))

    def far_out(h, i):
        copies.start(("1+", h, i), sum_view(h, i, 2, 0, quarter), r1.at[h, i, pl.ds(0, quarter)], first[h][0])
        copies.start(("1-", h, i), sum_view(h, i, 2, quarter, quarter), r1.at[h, i, pl.ds(quarter, quarter)], first[h][1])

    def add_to(ref, more):
        ref[...] = (ref[...].astype(F32) + more[...].astype(F32)).astype(BF16)

    def near_out(h, i):
        copies.arrived(("1+", h, i))
        add_to(sum_view(h, i, 1, 0, quarter), r1.at[h, i, pl.ds(0, quarter)])
        copies.start(("2+", h, i), sum_view(h, i, 1, 0, half), r2.at[h, i, 0], first[h][0])
        copies.arrived(("1-", h, i))
        add_to(sum_view(h, i, 3, quarter, quarter), r1.at[h, i, pl.ds(quarter, quarter)])
        copies.start(("2-", h, i), sum_view(h, i, 3, 0, half), r2.at[h, i, 1], first[h][1])

    def gathered(h, i, start, count):
        span = pl.ds(start, count)
        return (
            sum_view(h, i, 0, start, count)[...].astype(F32)
            + r2[h, i, 0, span, :].astype(F32)
            + r2[h, i, 1, span, :].astype(F32)
        )

    def arrived_2(h, i):
        copies.arrived(("2+", h, i))
        copies.arrived(("2-", h, i))

    loads["cache"].wait()
    prefix(0, [0])
    own_part()
    q_on(0)
    copies.arrived("f1")
    copies.arrived("f3")
    prefix(0, [1, 3])
    direct_out(0)
    copies.arrived(("q2+", 0))
    copies.arrived(("q2-", 0))
    copies.arrived("f2")
    prefix(0, [2])
    relay_out(0)
    q_out(1)
    prefix(1, [0])
    relay_on(0)
    for d in (3, 1):
        source = told(d, 0)
        tell(d, 3, source, yp)
        tell(d, 1, source, ym)
        if d == 3:
            tell(2, 0, source, zp)
    q_on(1)
    finish(0)
    spread_0(0)
    prefix(1, [1, 3])
    direct_out(1)
    spread_1(0)
    copies.arrived(("q2+", 1))
    copies.arrived(("q2-", 1))
    prefix(1, [2])
    relay_out(1)
    source = told(2, 0)
    tell(2, 3, source, yp)
    tell(2, 1, source, ym)
    pass_second(0, 0)
    relay_on(1)
    spread_far(0)
    finish(1)
    spread_0(1)
    for d in range(SIDE):
        tell(d, 2, told(d, 3), yp)
    pass_second(0, 1)
    pass_second(0, 3)
    spread_1(1)
    pass_second(0, 2)
    pass_second(1, 0)
    for d in range(SIDE):
        told(d, 1)
        told(d, 2)
    for key in ("up", "down"):
        loads[key].wait()
        copies.arrived(key)
    for g in range(GROUPS):
        for key in ("q2+", "q2-", "r_high", "l_low", "relay_r", "relay_l", "r_low", "l_high"):
            copies.left((key, g))

    def run(chunk):
        for dz, dy in chunk:
            for g in range(GROUPS):
                have(("a", g), dz, dy)
                have(("b", g), dz, dy)
        run_experts(chunk)

    level = part
    lo, hi = pl.ds(0, quarter), pl.ds(quarter, quarter)

    def level_rows(h, start, count):
        return pl.ds(h * half + start, count)

    def level_far(h):
        arrived_2(h, 2)
        level[2, level_rows(h, 0, half), :] = gathered(h, 2, 0, half).astype(BF16)
        copies.start(("3+", h), level.at[2, level_rows(h, 0, quarter)], r3.at[h, lo], second[h][0])
        copies.start(("3-", h), level.at[2, level_rows(h, quarter, quarter)], r3.at[h, hi], second[h][1])

    run(CHUNKS[0])
    spread_far(1)
    pass_second(1, 1)
    pass_second(1, 3)
    pass_second(1, 2)
    run(CHUNKS[1])
    for h, i in ((0, 0), (1, 0), (0, 1), (1, 1)):
        far_out(h, i)
    run(CHUNKS[2])
    for h, i in ((0, 2), (1, 2), (0, 3), (1, 3)):
        far_out(h, i)
    for h, i in ((0, 0), (1, 0)):
        near_out(h, i)
    run(CHUNKS[3])
    for h, i in ((0, 2), (1, 2), (0, 1), (1, 1)):
        near_out(h, i)
    level_far(0)
    level_far(1)
    for h, i in ((0, 3), (1, 3)):
        near_out(h, i)
    for h in range(2):
        arrived_2(h, 1)
        copies.arrived(("3+", h))
        level[1, level_rows(h, 0, quarter), :] = (gathered(h, 1, 0, quarter) + r3[h, lo, :].astype(F32)).astype(BF16)
        level[1, level_rows(h, quarter, quarter), :] = gathered(h, 1, quarter, quarter).astype(BF16)
        copies.start(("4+", h), level.at[1, level_rows(h, 0, half)], r4.at[h, 0], second[h][0])
        arrived_2(h, 3)
        copies.arrived(("3-", h))
        level[3, level_rows(h, 0, quarter), :] = gathered(h, 3, 0, quarter).astype(BF16)
        level[3, level_rows(h, quarter, quarter), :] = (gathered(h, 3, quarter, quarter) + r3[h, hi, :].astype(F32)).astype(BF16)
        copies.start(("4-", h), level.at[3, level_rows(h, 0, half)], r4.at[h, 1], second[h][1])
    for h in range(2):
        arrived_2(h, 0)
        copies.arrived(("4+", h))
        copies.arrived(("4-", h))
        span = pl.ds(h * half, half)
        mixture = gathered(h, 0, 0, half) + r4[h, 0].astype(F32) + r4[h, 1].astype(F32)
        position = lax.broadcasted_iota(jnp.int32, (half, width), 0) + h * half
        out_ref[span, :] = jnp.where(position < length, own[span, :] + mixture, 0.0).astype(BF16)
    copies.drain()


def layer(length, group, owner, queries, pairs, cache, weight, hidden, gain, routes, gates, upward, downward):
    rows, width = queries.shape
    heads = width // HD
    inner = downward.shape[0]
    half = rows // 2
    slots = SIDE * SIDE
    count = len(CHUNKS[0]) * CAP
    dma = pltpu.SemaphoreType.DMA
    return pl.pallas_call(
        layer_kernel,
        out_shape=jax.ShapeDtypeStruct((rows, width), BF16),
        in_specs=[SMEM, SMEM, SMEM, VMEM, VMEM, ANY, ANY, VMEM, VMEM, VMEM, VMEM, ANY, ANY],
        out_specs=VMEM,
        scratch_shapes=[
            pltpu.VMEM((3 * rows, width), BF16),
            pltpu.VMEM((8, HD), F32),
            pltpu.VMEM((3, 8, HD), F32),
            pltpu.VMEM(cache.shape, BF16),
            pltpu.VMEM((4, rows, width), BF16),
            pltpu.VMEM((GROUPS, 4, rows, HD), F32),
            pltpu.VMEM((GROUPS, 4, heads, rows), F32),
            pltpu.VMEM((GROUPS, 3, heads, rows), F32),
            pltpu.VMEM((rows, width), F32),
            pltpu.VMEM((rows, HD), F32),
            pltpu.VMEM((GROUPS, 2, rows // GROUPS // 2, width), BF16),
            pltpu.VMEM((2, rows, width), BF16),
            pltpu.VMEM((rows // GROUPS, width), BF16),
            pltpu.VMEM((slots, 16, rows), F32),
            pltpu.VMEM((slots, rows, width), BF16),
            pltpu.VMEM((2,) + upward.shape, BF16),
            pltpu.VMEM((2,) + downward.shape, BF16),
            pltpu.VMEM((len(CHUNKS[0]) // 2, 4 * CAP, 2 * rows), BF16),
            pltpu.VMEM((2, count, HD), F32),
            pltpu.VMEM((2, count, inner), BF16),
            pltpu.VMEM((slots, width // slots, width), BF16),
            pltpu.VMEM((2, SIDE, half, width), BF16),
            pltpu.VMEM((2, SIDE, 2, half, width), BF16),
            pltpu.VMEM((2, half, width), BF16),
            pltpu.VMEM((2, 2, half, width), BF16),
            dma((180,)),
            dma((180,)),
            dma((4,)),
        ],
        compiler_params=pltpu.CompilerParams(
            collective_id=0, has_side_effects=True, vmem_limit_bytes=VMEM_LIMIT
        ),
        name="layer",
    )(
        length, group, owner, queries, pairs, cache, weight.reshape(slots, width // slots, width), hidden, gain,
        routes, gates, upward, downward,
    )


def on_device(
    hidden_in, queries, suffix_pairs, prefix_cache, suffix_length, request_group, prefix_owner,
    out_weight, norm_gain, routes, gate_values, expert_upward, expert_downward,
):
    rows, width = hidden_in.shape[2:]
    out = layer(
        suffix_length, request_group, prefix_owner, queries[0, 0], suffix_pairs[0, 0], prefix_cache[0, 0], out_weight,
        hidden_in[0, 0], norm_gain.reshape(1, width), routes[0, 0], gate_values[0, 0], expert_upward[0], expert_downward[0],
    )
    return out.reshape(1, 1, rows, width)


def solution(mesh):
    in_specs = (
        P("req", "exp", None, None),
        P("req", "exp", None, None),
        P("req", "exp", None, None, None),
        P("exp", "req", None, None, None),
        P("req", "exp"),
        P("req", "exp"),
        P("exp", None),
        P(),
        P(),
        P("req", "exp", None, None),
        P("req", "exp", None, None),
        P("exp", None, None),
        P("exp", None, None),
    )
    out_specs = P("req", "exp", None, None)
    return jax.shard_map(
        on_device, mesh=mesh, in_specs=in_specs, out_specs=out_specs, check_vma=False
    )
```

```python
import functools

import jax
import jax.numpy as jnp
from jax import lax
from jax.experimental import pallas as pl
from jax.experimental.pallas import tpu as pltpu
from jax.sharding import PartitionSpec as P

HD = 128
SINK = 4
SIDE = 4
CAP = 40
NEG = -1e30
MESH = pl.DeviceIdType.MESH
VMEM_LIMIT = 63 * 1024 * 1024
F32 = jnp.float32
BF16 = jnp.bfloat16
ANY = pl.BlockSpec(memory_space=pl.ANY)
VMEM = pl.BlockSpec(memory_space=pltpu.VMEM)
SMEM = pl.BlockSpec(memory_space=pltpu.SMEM)


def dot_t(a, b):
    return lax.dot_general(a, b, (((1,), (1,)), ((), ())), preferred_element_type=F32)


def dot(a, b):
    return jnp.dot(a, b, preferred_element_type=F32)


class Copies:
    def __init__(self, send, recv):
        self.send, self.recv, self.made, self.gone = send, recv, {}, set()

    def start(self, key, src, dst, device):
        index = len(self.made)
        copy = pltpu.make_async_remote_copy(
            src_ref=src,
            dst_ref=dst,
            send_sem=self.send.at[index],
            recv_sem=self.recv.at[index],
            device_id=device,
            device_id_type=MESH,
        )
        copy.start()
        self.made[key] = copy

    def arrived(self, key):
        self.made[key].wait_recv()

    def left(self, key):
        self.made[key].wait_send()
        self.gone.add(key)

    def drain(self):
        for key, copy in self.made.items():
            if key not in self.gone:
                copy.wait_send()


def meet(devices):
    barrier = pltpu.get_barrier_semaphore()
    for device in devices:
        pl.semaphore_signal(barrier, inc=1, device_id=device, device_id_type=MESH)
    pl.semaphore_wait(barrier, len(devices))


def torus(req, e):
    core = lax.rem(e, 2)
    y = lax.rem(e // 2, SIDE)
    z = e // (2 * SIDE)

    def at(dz, dy):
        return (req, (lax.rem(z + dz, SIDE) * SIDE + lax.rem(y + dy, SIDE)) * 2 + core)

    return at(1, 0), at(3, 0), at(0, 1), at(0, 3)


GROUPS = 2
LOG2E = 1.4426950408889634
CHUNKS = (
    ((0, 0), (0, 1), (0, 3), (1, 0)),
    ((0, 2), (2, 0), (1, 2), (2, 1)),
    ((2, 2), (3, 2), (2, 3), (3, 0)),
    ((1, 1), (1, 3), (3, 1), (3, 3)),
)


def slot(dz, dy):
    return (dz % SIDE) * SIDE + dy % SIDE


def layer_kernel(
    length_ref, group_ref, owner_ref, q_ref, pairs_ref, cache_ref, weight_ref, hidden_ref, gain_ref,
    routes_ref, gates_ref, up_ref, down_ref,
    out_ref,
    qrows, flag, flags, cache, part, stat, stat_t, stat_in, own, own_stat, relay, back, attn,
    bias, meta, tokens, up, down, pmat, pmat_t, gslot, hid, sums, r1, r2, r3, r4,
    send, recv, local,
):
    x, e = lax.axis_index("req"), lax.axis_index("exp")
    right, left, across = (
        (lax.rem(x + 1, SIDE), e),
        (lax.rem(x + 3, SIDE), e),
        (lax.rem(x + 2, SIDE), e),
    )
    other = (x, e + 1 - 2 * lax.rem(e, 2))
    zp, zm, yp, ym = torus(x, e)
    rows, width = q_ref.shape
    heads = width // HD
    window = cache_ref.shape[1]
    inner = down_ref.shape[0]
    half, quarter = rows // 2, rows // 4
    size = rows // GROUPS
    part_half = size // 2
    copies = Copies(send, recv)

    loads = {}
    for index, (key, src, dst) in enumerate(
        (
            ("cache", cache_ref, cache),
            ("weight", weight_ref, sums),
            ("up", up_ref, up.at[0]),
            ("down", down_ref, down.at[0]),
        )
    ):
        loads[key] = pltpu.make_async_copy(src, dst, local.at[index])
        loads[key].start()

    length = length_ref[0, 0]
    group = group_ref[0, 0]
    owner = jnp.int32(0)
    for k in range(SIDE):
        owner = jnp.where(group == k, owner_ref[0, k], owner)
    flag[...] = (lax.broadcasted_iota(jnp.int32, (8, HD), 0) == owner).astype(F32)
    live = lax.broadcasted_iota(jnp.int32, (8, rows), 1) < length
    meta[0, 0:8, :] = jnp.where(live, jnp.transpose(routes_ref[...].astype(F32)), -1.0)
    meta[0, 8:16, :] = jnp.transpose(gates_ref[...])
    meet([right, left, across, other, zp, zm, yp, ym])

    def rows_of(g, start=0, count=None):
        return pl.ds(g * size + start, size if count is None else count)

    def q_slot(d, span):
        return qrows.at[pl.ds((d - 1) * rows + span.start, span.size)]

    def q_out(g):
        copies.start(("q", 3, g), q_ref.at[rows_of(g)], q_slot(3, rows_of(g)), right)
        copies.start(("q", 1, g), q_ref.at[rows_of(g)], q_slot(1, rows_of(g)), left)

    def q_on(g):
        low, high = rows_of(g, 0, part_half), rows_of(g, part_half, part_half)
        copies.arrived(("q", 3, g))
        copies.start(("q2+", g), q_slot(3, low), q_slot(2, low), right)
        copies.arrived(("q", 1, g))
        copies.start(("q2-", g), q_slot(1, high), q_slot(2, high), left)

    q_out(0)
    copies.start("f3", flag, flags.at[2], right)
    copies.start("f1", flag, flags.at[0], left)
    copies.start("f2", flag, flags.at[1], across)

    def tell(tz, ty, source, device):
        copies.start(("m", tz, ty), meta.at[source], meta.at[slot(tz, ty)], device)

    def told(tz, ty):
        copies.arrived(("m", tz, ty))
        return slot(tz, ty)

    tell(3, 0, 0, zp)
    tell(1, 0, 0, zm)
    tell(0, 3, 0, yp)
    tell(0, 1, 0, ym)
    copies.start("up", up_ref, up.at[1], other)
    copies.start("down", down_ref, down.at[1], other)

    scale = HD ** (-0.5)
    lane = lax.broadcasted_iota(jnp.int32, (rows, HD), 1)
    lane_g = lax.broadcasted_iota(jnp.int32, (size, HD), 1)
    stat[...] = jnp.zeros_like(stat)
    own_stat[...] = jnp.zeros_like(own_stat)

    def softmax(masked):
        largest = jnp.max(masked, axis=1, keepdims=True)
        weights = jnp.exp2((masked - largest) * (scale * LOG2E))
        totals = jnp.sum(weights, axis=1, keepdims=True)
        return weights.astype(BF16), 1.0 / totals, largest * scale + jnp.log(totals)

    def in_turn(jobs, scores, values, store):
        made, soft = {}, {}
        for step in range(len(jobs) + 2):
            if step < len(jobs):
                made[step] = scores(jobs[step])
            if 0 <= step - 1 < len(jobs):
                soft[step - 1] = softmax(made.pop(step - 1))
            if step >= 2:
                weights, inverse, lse = soft.pop(step - 2)
                store(jobs[step - 2], dot(weights, values(jobs[step - 2])) * inverse, lse)

    def columns(h):
        return pl.ds(pl.multiple_of(h * HD, HD), HD)

    own_c = lax.broadcasted_iota(jnp.int32, (rows, rows), 1)
    own_t = lax.broadcasted_iota(jnp.int32, (rows, rows), 0)

    def own_part():
        several = min(4, heads)
        own_bias = jnp.where(own_c <= own_t, 0.0, NEG)

        @pl.loop(0, heads // several)
        def _(block):
            stats = [own_stat[...]]

            def scores(k):
                cols = columns(block * several + k)
                return dot_t(q_ref[:, cols], pairs_ref[0, :, cols]) + own_bias

            def store(k, out, lse):
                own[:, columns(block * several + k)] = out
                stats[0] = jnp.where(lane == block * several + k, lse, stats[0])

            in_turn(
                list(range(several)), scores, lambda k: pairs_ref[1, :, columns(block * several + k)], store
            )
            own_stat[...] = stats[0]

    for g in range(GROUPS):
        c = lax.broadcasted_iota(jnp.int32, (size, window), 1)
        t = lax.broadcasted_iota(jnp.int32, (size, window), 0) + g * size
        bias[g] = jnp.where((c < SINK) | (c > t), 0.0, NEG)

    def prefix(g, slots):
        span = rows_of(g)
        valid = {d: (flag if d == 0 else flags.at[d - 1])[pl.ds(x, 1), :] for d in slots}
        several = min(8 // len(slots), heads)

        @pl.loop(0, heads // several)
        def _(block):
            stats = {d: stat[g, d, 0:size, :] for d in slots}

            def scores(job):
                k, d = job
                cols = columns(block * several + k)
                q = q_ref[span, cols] if d == 0 else q_slot(d, span)[:, cols]
                return dot_t(q, cache[0, :, cols]) + bias[g]

            def store(job, out, lse):
                k, d = job
                h = block * several + k
                part[d, span, columns(h)] = (out * valid[d]).astype(BF16)
                stats[d] = jnp.where(lane_g == h, lse * valid[d], stats[d])

            in_turn(
                [(k, d) for k in range(several) for d in slots], scores,
                lambda job: cache[1, :, columns(block * several + job[0])], store,
            )
            for d in slots:
                stat[g, d, 0:size, :] = stats[d]

        for d in slots:
            stat_t[g, d] = jnp.transpose(stat[g, d])[0:heads, :]

    def direct_out(g):
        low, high = rows_of(g, 0, part_half), rows_of(g, part_half, part_half)
        copies.start(("r_high", g), part.at[1, high], back.at[0, high], right)
        copies.start(("l_low", g), part.at[3, low], back.at[1, low], left)
        copies.start(("s1", g), stat_t.at[g, 1], stat_in.at[g, 0], right)
        copies.start(("s3", g), stat_t.at[g, 3], stat_in.at[g, 1], left)

    def relay_out(g):
        low, high = rows_of(g, 0, part_half), rows_of(g, part_half, part_half)
        copies.start(("relay_r", g), part.at[2, low], relay.at[g, 0], right)
        copies.start(("relay_l", g), part.at[2, high], relay.at[g, 1], left)
        copies.start(("s2", g), stat_t.at[g, 2], stat_in.at[g, 2], across)

    def relay_on(g):
        low, high = rows_of(g, 0, part_half), rows_of(g, part_half, part_half)
        copies.arrived(("relay_r", g))
        part[1, low, :] = part[1, low, :] + relay[g, 0]
        copies.start(("r_low", g), part.at[1, low], back.at[0, low], right)
        copies.arrived(("relay_l", g))
        part[3, high, :] = part[3, high, :] + relay[g, 1]
        copies.start(("l_high", g), part.at[3, high], back.at[1, high], left)

    tile = min(512, width)

    def finish(g):
        for key in ("s1", "s2", "s3", "r_high", "l_low", "r_low", "l_high"):
            copies.arrived((key, g))
        span = rows_of(g)
        total_t = stat_t[g, 0] + stat_in[g, 0] + stat_in[g, 1] + stat_in[g, 2]
        stat[g, 0] = jnp.transpose(jnp.concatenate([total_t, jnp.zeros((HD - heads, rows), F32)], axis=0))
        several = min(4, heads)

        @pl.loop(0, heads // several)
        def _(block):
            for k in range(several):
                h = block * several + k
                cols = columns(h)
                first = part[0, span, cols].astype(F32) + back[0, span, cols].astype(F32) + back[1, span, cols].astype(F32)
                lse_first = jnp.sum(jnp.where(lane_g == h, stat[g, 0, 0:size, :], 0.0), axis=1, keepdims=True)
                lse_own = jnp.sum(jnp.where(lane_g == h, own_stat[span, :], 0.0), axis=1, keepdims=True)
                top = jnp.maximum(lse_first, lse_own)
                a, b = jnp.exp(lse_first - top), jnp.exp(lse_own - top)
                attn[:, cols] = ((a * first + b * own[span, cols]) * (1.0 / (a + b))).astype(BF16)

        if g == 0:
            loads["weight"].wait()

        def project(j, squares):
            cols = pl.ds(pl.multiple_of(j * tile, tile), tile)
            weight = sums[:, :, cols].reshape(width, tile)
            res = hidden_ref[span, cols].astype(F32) + dot(attn[...], weight)
            own[span, cols] = res
            return squares + jnp.sum(res * res, axis=1, keepdims=True)

        squares = lax.fori_loop(0, width // tile, project, jnp.zeros((size, 1), F32))
        factor = lax.rsqrt(squares / width + 1e-05)

        @pl.loop(0, width // tile)
        def _(j):
            cols = pl.ds(pl.multiple_of(j * tile, tile), tile)
            tokens[0, span, cols] = (own[span, cols] * factor * gain_ref[:, cols]).astype(BF16)

    def view(dz, dy, start, count):
        return tokens.at[slot(dz, dy), pl.ds(start, count)]

    def start_of(kind):
        return kind[1] * size + (part_half if kind[0] == "b" else 0)

    def push(key, dz, dy, axis, step, start, count):
        device = {("z", 1): zp, ("z", -1): zm, ("y", 1): yp, ("y", -1): ym}[axis, step]
        tz, ty = ((dz - step) % SIDE, dy) if axis == "z" else (dz, (dy - step) % SIDE)
        copies.start((key, tz, ty), view(dz, dy, start, count), view(tz, ty, start, count), device)

    def both(kind, dz, dy, axis):
        push(kind, dz, dy, axis, 1, start_of(kind), part_half)
        push(kind, dz, dy, axis, -1, start_of(kind), part_half)

    def pass_on(kind, dz, dy, axis):
        behind = (dz if axis == "z" else dy) == 3
        start = start_of(kind) + (0 if behind else part_half // 2)
        push((kind, behind), dz, dy, axis, 1 if behind else -1, start, part_half // 2)

    waited = set()

    def have(kind, dz, dy):
        first, last = (dz, dy) if kind[0] == "a" else (dy, dz)
        if first == 0 and last == 0:
            return
        split = last == 2 or (last == 0 and first == 2)
        for key in ([(kind, True), (kind, False)] if split else [kind]):
            if (key, dz, dy) not in waited:
                waited.add((key, dz, dy))
                copies.arrived((key, dz, dy))

    def spread_0(g):
        both(("a", g), 0, 0, "z")
        both(("b", g), 0, 0, "y")
        both(("a", g), 0, 0, "y")
        both(("b", g), 0, 0, "z")

    def spread_1(g):
        for d in (3, 1):
            have(("a", g), d, 0)
            pass_on(("a", g), d, 0, "z")
            both(("a", g), d, 0, "y")
            have(("b", g), 0, d)
            pass_on(("b", g), 0, d, "y")
            both(("b", g), 0, d, "z")

    def spread_far(g):
        have(("a", g), 2, 0)
        both(("a", g), 2, 0, "y")
        have(("b", g), 0, 2)
        both(("b", g), 0, 2, "z")

    def pass_second(g, d):
        for near in (3, 1):
            have(("a", g), d, near)
            pass_on(("a", g), d, near, "y")
            have(("b", g), near, d)
            pass_on(("b", g), near, d, "z")

    ids = [e.astype(F32), (e + 1 - 2 * lax.rem(e, 2)).astype(F32)]
    span2 = 2 * CAP
    count = len(CHUNKS[0]) * CAP
    before = (
        lax.broadcasted_iota(jnp.int32, (rows, rows), 0) < lax.broadcasted_iota(jnp.int32, (rows, rows), 1)
    ).astype(BF16)
    slot_row = lax.broadcasted_iota(jnp.int32, (span2, rows), 0).astype(F32)

    def run_experts(chunk):
        pairs = [chunk[i:i + 2] for i in range(0, len(chunk), 2)]
        for p, pair in enumerate(pairs):
            gates = [jnp.zeros((span2, 1), F32)] * 2
            for i, (dz, dy) in enumerate(pair):
                source = slot(dz, dy)
                both_chosen = []
                for k in range(2):
                    named = (meta[source, 0:8, :] == ids[k]).astype(F32)
                    mine = jnp.sum(named, axis=0, keepdims=True)
                    gate = jnp.sum(named * meta[source, 8:16, :], axis=0, keepdims=True)
                    rank = dot(jnp.broadcast_to(mine, (8, rows)).astype(BF16), before)[0:1, :]
                    place = jnp.where(mine > 0.0, rank + float(i * CAP), -1.0)
                    chosen = (slot_row == place).astype(F32)
                    gates[k] = gates[k] + jnp.sum(chosen * gate, axis=1, keepdims=True)
                    both_chosen.append(chosen)
                chosen = jnp.concatenate(both_chosen, axis=0)
                pmat[p, :, i * rows:(i + 1) * rows] = chosen.astype(BF16)
                pmat_t[p, i * rows:(i + 1) * rows, :] = jnp.transpose(chosen).astype(BF16)
            for k in range(2):
                gslot[k, p * span2:(p + 1) * span2, :] = jnp.broadcast_to(gates[k], (span2, HD))
        tile = min(512, width)

        @pl.loop(0, width // tile)
        def _(j):
            cols = pl.ds(pl.multiple_of(j * tile, tile), tile)
            for p, pair in enumerate(pairs):
                joint = jnp.concatenate([tokens[slot(dz, dy), :, cols] for dz, dy in pair], axis=0)
                rows_out = dot(pmat[p], joint).astype(BF16)
                for k in range(2):
                    qrows[k * count + p * span2:k * count + (p + 1) * span2, cols] = rows_out[k * span2:(k + 1) * span2, :]

        tile_f = min(256, inner)

        @pl.loop(0, inner // tile_f)
        def _(j):
            start = pl.multiple_of(j * tile_f, tile_f)
            for k in range(2):
                gate = dot(qrows[k * count:(k + 1) * count, :], up[k, :, pl.ds(start, tile_f)])
                lift = dot(qrows[k * count:(k + 1) * count, :], up[k, :, pl.ds(pl.multiple_of(inner + start, tile_f), tile_f)])
                hid[k, :, pl.ds(start, tile_f)] = (gate / (1.0 + jnp.exp(-gate)) * lift).astype(BF16)

        tile_d = min(256, width)
        turns = min(2, width // tile_d)

        @pl.loop(0, width // (turns * tile_d))
        def _(block):
            joint = []
            for turn in range(turns):
                cols = pl.ds(pl.multiple_of((block * turns + turn) * tile_d, tile_d), tile_d)
                made = [(dot(hid[k], down[k, :, cols]) * gslot[k, :, 0:1]).astype(BF16) for k in range(2)]
                joint.append([
                    jnp.concatenate([m[p * span2:(p + 1) * span2, :] for m in made], axis=0) for p in range(len(pairs))
                ])
            for turn in range(turns):
                cols = pl.ds(pl.multiple_of((block * turns + turn) * tile_d, tile_d), tile_d)
                for p, pair in enumerate(pairs):
                    placed = dot(pmat_t[p], joint[turn][p]).astype(BF16)
                    for i, (dz, dy) in enumerate(pair):
                        sums[slot(dz, dy), :, cols] = placed[i * rows:(i + 1) * rows, :]

    def sum_view(h, i, j, start, count):
        dz, dy = (i, j) if h == 0 else (j, i)
        return sums.at[slot(dz, dy), pl.ds(h * half + start, count)]

    first = ((yp, ym), (zp, zm))
    second = ((zp, zm), (yp, ym))

    def far_out(h, i):
        copies.start(("1+", h, i), sum_view(h, i, 2, 0, quarter), r1.at[h, i, pl.ds(0, quarter)], first[h][0])
        copies.start(("1-", h, i), sum_view(h, i, 2, quarter, quarter), r1.at[h, i, pl.ds(quarter, quarter)], first[h][1])

    def add_to(ref, more):
        ref[...] = (ref[...].astype(F32) + more[...].astype(F32)).astype(BF16)

    def near_out(h, i):
        copies.arrived(("1+", h, i))
        add_to(sum_view(h, i, 1, 0, quarter), r1.at[h, i, pl.ds(0, quarter)])
        copies.start(("2+", h, i), sum_view(h, i, 1, 0, half), r2.at[h, i, 0], first[h][0])
        copies.arrived(("1-", h, i))
        add_to(sum_view(h, i, 3, quarter, quarter), r1.at[h, i, pl.ds(quarter, quarter)])
        copies.start(("2-", h, i), sum_view(h, i, 3, 0, half), r2.at[h, i, 1], first[h][1])

    def gathered(h, i, start, count):
        span = pl.ds(start, count)
        return (
            sum_view(h, i, 0, start, count)[...].astype(F32)
            + r2[h, i, 0, span, :].astype(F32)
            + r2[h, i, 1, span, :].astype(F32)
        )

    def arrived_2(h, i):
        copies.arrived(("2+", h, i))
        copies.arrived(("2-", h, i))

    loads["cache"].wait()
    prefix(0, [0])
    own_part()
    q_on(0)
    copies.arrived("f1")
    copies.arrived("f3")
    prefix(0, [1, 3])
    direct_out(0)
    copies.arrived(("q2+", 0))
    copies.arrived(("q2-", 0))
    copies.arrived("f2")
    prefix(0, [2])
    relay_out(0)
    q_out(1)
    prefix(1, [0])
    relay_on(0)
    for d in (3, 1):
        source = told(d, 0)
        tell(d, 3, source, yp)
        tell(d, 1, source, ym)
        if d == 3:
            tell(2, 0, source, zp)
    q_on(1)
    finish(0)
    spread_0(0)
    prefix(1, [1, 3])
    direct_out(1)
    spread_1(0)
    copies.arrived(("q2+", 1))
    copies.arrived(("q2-", 1))
    prefix(1, [2])
    relay_out(1)
    source = told(2, 0)
    tell(2, 3, source, yp)
    tell(2, 1, source, ym)
    pass_second(0, 0)
    relay_on(1)
    spread_far(0)
    finish(1)
    spread_0(1)
    for d in range(SIDE):
        tell(d, 2, told(d, 3), yp)
    pass_second(0, 1)
    pass_second(0, 3)
    spread_1(1)
    pass_second(0, 2)
    pass_second(1, 0)
    for d in range(SIDE):
        told(d, 1)
        told(d, 2)
    for key in ("up", "down"):
        loads[key].wait()
        copies.arrived(key)
    for g in range(GROUPS):
        for key in ("q2+", "q2-", "r_high", "l_low", "relay_r", "relay_l", "r_low", "l_high"):
            copies.left((key, g))

    def run(chunk):
        for dz, dy in chunk:
            for g in range(GROUPS):
                have(("a", g), dz, dy)
                have(("b", g), dz, dy)
        run_experts(chunk)

    level = part
    lo, hi = pl.ds(0, quarter), pl.ds(quarter, quarter)

    def level_rows(h, start, count):
        return pl.ds(h * half + start, count)

    def level_far(h):
        arrived_2(h, 2)
        level[2, level_rows(h, 0, half), :] = gathered(h, 2, 0, half).astype(BF16)
        copies.start(("3+", h), level.at[2, level_rows(h, 0, quarter)], r3.at[h, lo], second[h][0])
        copies.start(("3-", h), level.at[2, level_rows(h, quarter, quarter)], r3.at[h, hi], second[h][1])

    run(CHUNKS[0])
    spread_far(1)
    pass_second(1, 1)
    pass_second(1, 3)
    pass_second(1, 2)
    run(CHUNKS[1])
    for h, i in ((0, 0), (1, 0), (0, 1), (1, 1)):
        far_out(h, i)
    run(CHUNKS[2])
    for h, i in ((0, 2), (1, 2), (0, 3), (1, 3)):
        far_out(h, i)
    for h, i in ((0, 0), (1, 0)):
        near_out(h, i)
    run(CHUNKS[3])
    for h, i in ((0, 2), (1, 2), (0, 1), (1, 1)):
        near_out(h, i)
    level_far(0)
    level_far(1)
    for h, i in ((0, 3), (1, 3)):
        near_out(h, i)
    for h in range(2):
        arrived_2(h, 1)
        copies.arrived(("3+", h))
        level[1, level_rows(h, 0, quarter), :] = (gathered(h, 1, 0, quarter) + r3[h, lo, :].astype(F32)).astype(BF16)
        level[1, level_rows(h, quarter, quarter), :] = gathered(h, 1, quarter, quarter).astype(BF16)
        copies.start(("4+", h), level.at[1, level_rows(h, 0, half)], r4.at[h, 0], second[h][0])
        arrived_2(h, 3)
        copies.arrived(("3-", h))
        level[3, level_rows(h, 0, quarter), :] = gathered(h, 3, 0, quarter).astype(BF16)
        level[3, level_rows(h, quarter, quarter), :] = (gathered(h, 3, quarter, quarter) + r3[h, hi, :].astype(F32)).astype(BF16)
        copies.start(("4-", h), level.at[3, level_rows(h, 0, half)], r4.at[h, 1], second[h][1])
    for h in range(2):
        arrived_2(h, 0)
        copies.arrived(("4+", h))
        copies.arrived(("4-", h))
        span = pl.ds(h * half, half)
        mixture = gathered(h, 0, 0, half) + r4[h, 0].astype(F32) + r4[h, 1].astype(F32)
        position = lax.broadcasted_iota(jnp.int32, (half, width), 0) + h * half
        out_ref[span, :] = jnp.where(position < length, own[span, :] + mixture, 0.0).astype(BF16)
    copies.drain()


def layer(length, group, owner, queries, pairs, cache, weight, hidden, gain, routes, gates, upward, downward):
    rows, width = queries.shape
    heads = width // HD
    inner = downward.shape[0]
    half = rows // 2
    slots = SIDE * SIDE
    count = len(CHUNKS[0]) * CAP
    dma = pltpu.SemaphoreType.DMA
    return pl.pallas_call(
        layer_kernel,
        out_shape=jax.ShapeDtypeStruct((rows, width), BF16),
        in_specs=[SMEM, SMEM, SMEM, VMEM, VMEM, ANY, ANY, VMEM, VMEM, VMEM, VMEM, ANY, ANY],
        out_specs=VMEM,
        scratch_shapes=[
            pltpu.VMEM((3 * rows, width), BF16),
            pltpu.VMEM((8, HD), F32),
            pltpu.VMEM((3, 8, HD), F32),
            pltpu.VMEM(cache.shape, BF16),
            pltpu.VMEM((4, rows, width), BF16),
            pltpu.VMEM((GROUPS, 4, rows, HD), F32),
            pltpu.VMEM((GROUPS, 4, heads, rows), F32),
            pltpu.VMEM((GROUPS, 3, heads, rows), F32),
            pltpu.VMEM((rows, width), F32),
            pltpu.VMEM((rows, HD), F32),
            pltpu.VMEM((GROUPS, 2, rows // GROUPS // 2, width), BF16),
            pltpu.VMEM((2, rows, width), BF16),
            pltpu.VMEM((rows // GROUPS, width), BF16),
            pltpu.VMEM((GROUPS, rows // GROUPS, cache.shape[1]), F32),
            pltpu.VMEM((slots, 16, rows), F32),
            pltpu.VMEM((slots, rows, width), BF16),
            pltpu.VMEM((2,) + upward.shape, BF16),
            pltpu.VMEM((2,) + downward.shape, BF16),
            pltpu.VMEM((len(CHUNKS[0]) // 2, 4 * CAP, 2 * rows), BF16),
            pltpu.VMEM((len(CHUNKS[0]) // 2, 2 * rows, 4 * CAP), BF16),
            pltpu.VMEM((2, count, HD), F32),
            pltpu.VMEM((2, count, inner), BF16),
            pltpu.VMEM((slots, width // slots, width), BF16),
            pltpu.VMEM((2, SIDE, half, width), BF16),
            pltpu.VMEM((2, SIDE, 2, half, width), BF16),
            pltpu.VMEM((2, half, width), BF16),
            pltpu.VMEM((2, 2, half, width), BF16),
            dma((180,)),
            dma((180,)),
            dma((4,)),
        ],
        compiler_params=pltpu.CompilerParams(
            collective_id=0, has_side_effects=True, vmem_limit_bytes=VMEM_LIMIT
        ),
        name="layer",
    )(
        length, group, owner, queries, pairs, cache, weight.reshape(slots, width // slots, width), hidden, gain,
        routes, gates, upward, downward,
    )


def on_device(
    hidden_in, queries, suffix_pairs, prefix_cache, suffix_length, request_group, prefix_owner,
    out_weight, norm_gain, routes, gate_values, expert_upward, expert_downward,
):
    rows, width = hidden_in.shape[2:]
    out = layer(
        suffix_length, request_group, prefix_owner, queries[0, 0], suffix_pairs[0, 0], prefix_cache[0, 0], out_weight,
        hidden_in[0, 0], norm_gain.reshape(1, width), routes[0, 0], gate_values[0, 0], expert_upward[0], expert_downward[0],
    )
    return out.reshape(1, 1, rows, width)


def solution(mesh):
    in_specs = (
        P("req", "exp", None, None),
        P("req", "exp", None, None),
        P("req", "exp", None, None, None),
        P("exp", "req", None, None, None),
        P("req", "exp"),
        P("req", "exp"),
        P("exp", None),
        P(),
        P(),
        P("req", "exp", None, None),
        P("req", "exp", None, None),
        P("exp", None, None),
        P("exp", None, None),
    )
    out_specs = P("req", "exp", None, None)
    return jax.shard_map(
        on_device, mesh=mesh, in_specs=in_specs, out_specs=out_specs, check_vma=False
    )
```

```python
import functools

import jax
import jax.numpy as jnp
from jax import lax
from jax.experimental import pallas as pl
from jax.experimental.pallas import tpu as pltpu
from jax.sharding import PartitionSpec as P

HD = 128
SINK = 4
SIDE = 4
CAP = 40
NEG = -1e30
MESH = pl.DeviceIdType.MESH
VMEM_LIMIT = 63 * 1024 * 1024
F32 = jnp.float32
BF16 = jnp.bfloat16
ANY = pl.BlockSpec(memory_space=pl.ANY)
VMEM = pl.BlockSpec(memory_space=pltpu.VMEM)
SMEM = pl.BlockSpec(memory_space=pltpu.SMEM)


def dot_t(a, b):
    return lax.dot_general(a, b, (((1,), (1,)), ((), ())), preferred_element_type=F32)


def dot(a, b):
    return jnp.dot(a, b, preferred_element_type=F32)


class Copies:
    def __init__(self, send, recv):
        self.send, self.recv, self.made, self.gone = send, recv, {}, set()

    def start(self, key, src, dst, device):
        index = len(self.made)
        copy = pltpu.make_async_remote_copy(
            src_ref=src,
            dst_ref=dst,
            send_sem=self.send.at[index],
            recv_sem=self.recv.at[index],
            device_id=device,
            device_id_type=MESH,
        )
        copy.start()
        self.made[key] = copy

    def arrived(self, key):
        self.made[key].wait_recv()

    def left(self, key):
        self.made[key].wait_send()
        self.gone.add(key)

    def drain(self):
        for key, copy in self.made.items():
            if key not in self.gone:
                copy.wait_send()


def meet(devices):
    barrier = pltpu.get_barrier_semaphore()
    for device in devices:
        pl.semaphore_signal(barrier, inc=1, device_id=device, device_id_type=MESH)
    pl.semaphore_wait(barrier, len(devices))


def torus(req, e):
    core = lax.rem(e, 2)
    y = lax.rem(e // 2, SIDE)
    z = e // (2 * SIDE)

    def at(dz, dy):
        return (req, (lax.rem(z + dz, SIDE) * SIDE + lax.rem(y + dy, SIDE)) * 2 + core)

    return at(1, 0), at(3, 0), at(0, 1), at(0, 3)


GROUPS = 2
LOG2E = 1.4426950408889634
CHUNKS = (
    ((0, 0), (0, 1), (0, 3), (1, 0)),
    ((0, 2), (2, 0)),
    ((1, 2), (2, 1), (3, 0), (1, 1)),
    ((2, 2), (3, 2), (2, 3), (1, 3)),
    ((3, 1), (3, 3)),
)


def slot(dz, dy):
    return (dz % SIDE) * SIDE + dy % SIDE


def layer_kernel(
    length_ref, group_ref, owner_ref, q_ref, pairs_ref, cache_ref, weight_ref, hidden_ref, gain_ref,
    routes_ref, gates_ref, up_ref, down_ref,
    out_ref,
    qrows, flag, flags, cache, part, stat, stat_t, stat_in, own, own_stat, relay, back, attn,
    bias, meta, tokens, up, down, pmat, pmat_t, gslot, hid, sums, r1, r2, r3, r4,
    send, recv, local,
):
    x, e = lax.axis_index("req"), lax.axis_index("exp")
    right, left, across = (
        (lax.rem(x + 1, SIDE), e),
        (lax.rem(x + 3, SIDE), e),
        (lax.rem(x + 2, SIDE), e),
    )
    other = (x, e + 1 - 2 * lax.rem(e, 2))
    zp, zm, yp, ym = torus(x, e)
    rows, width = q_ref.shape
    heads = width // HD
    window = cache_ref.shape[1]
    inner = down_ref.shape[0]
    half, quarter = rows // 2, rows // 4
    size = rows // GROUPS
    part_half = size // 2
    copies = Copies(send, recv)

    loads = {}
    for index, (key, src, dst) in enumerate(
        (
            ("cache", cache_ref, cache),
            ("weight", weight_ref, sums),
            ("up", up_ref, up.at[0]),
            ("down", down_ref, down.at[0]),
        )
    ):
        loads[key] = pltpu.make_async_copy(src, dst, local.at[index])
        loads[key].start()

    length = length_ref[0, 0]
    group = group_ref[0, 0]
    owner = jnp.int32(0)
    for k in range(SIDE):
        owner = jnp.where(group == k, owner_ref[0, k], owner)
    flag[...] = (lax.broadcasted_iota(jnp.int32, (8, HD), 0) == owner).astype(F32)
    live = lax.broadcasted_iota(jnp.int32, (8, rows), 1) < length
    meta[0, 0:8, :] = jnp.where(live, jnp.transpose(routes_ref[...].astype(F32)), -1.0)
    meta[0, 8:16, :] = jnp.transpose(gates_ref[...])
    meet([right, left, across, other, zp, zm, yp, ym])

    def rows_of(g, start=0, count=None):
        return pl.ds(g * size + start, size if count is None else count)

    def q_slot(d, span):
        return qrows.at[pl.ds((d - 1) * rows + span.start, span.size)]

    def q_piece(g, hop, piece):
        span = rows_of(g, piece * part_half, part_half)
        copies.start(("q", hop, g, piece), q_ref.at[span], q_slot(hop, span), right if hop == 3 else left)

    def q_first(g):
        q_piece(g, 3, 0)
        q_piece(g, 1, 1)

    def q_rest(g):
        q_piece(g, 3, 1)
        q_piece(g, 1, 0)

    def q_on(g):
        low, high = rows_of(g, 0, part_half), rows_of(g, part_half, part_half)
        copies.arrived(("q", 3, g, 0))
        copies.start(("q2+", g), q_slot(3, low), q_slot(2, low), right)
        copies.arrived(("q", 1, g, 1))
        copies.start(("q2-", g), q_slot(1, high), q_slot(2, high), left)

    def q_near(g):
        copies.arrived(("q", 3, g, 1))
        copies.arrived(("q", 1, g, 0))

    q_first(0)
    q_rest(0)
    copies.start("f3", flag, flags.at[2], right)
    copies.start("f1", flag, flags.at[0], left)
    copies.start("f2", flag, flags.at[1], across)

    def tell(tz, ty, source, device):
        copies.start(("m", tz, ty), meta.at[source], meta.at[slot(tz, ty)], device)

    def told(tz, ty):
        copies.arrived(("m", tz, ty))
        return slot(tz, ty)

    tell(3, 0, 0, zp)
    tell(1, 0, 0, zm)
    tell(0, 3, 0, yp)
    tell(0, 1, 0, ym)
    copies.start("up", up_ref, up.at[1], other)
    copies.start("down", down_ref, down.at[1], other)

    scale = HD ** (-0.5)
    lane = lax.broadcasted_iota(jnp.int32, (rows, HD), 1)
    lane_g = lax.broadcasted_iota(jnp.int32, (size, HD), 1)
    stat[...] = jnp.zeros_like(stat)
    own_stat[...] = jnp.zeros_like(own_stat)

    def softmax(masked):
        largest = jnp.max(masked, axis=1, keepdims=True)
        weights = jnp.exp2((masked - largest) * (scale * LOG2E))
        totals = jnp.sum(weights, axis=1, keepdims=True)
        return weights.astype(BF16), 1.0 / totals, largest * scale + jnp.log(totals)

    def in_turn(jobs, scores, values, store):
        made, soft = {}, {}
        for step in range(len(jobs) + 2):
            if step < len(jobs):
                made[step] = scores(jobs[step])
            if 0 <= step - 1 < len(jobs):
                soft[step - 1] = softmax(made.pop(step - 1))
            if step >= 2:
                weights, inverse, lse = soft.pop(step - 2)
                store(jobs[step - 2], dot(weights, values(jobs[step - 2])) * inverse, lse)

    def columns(h):
        return pl.ds(pl.multiple_of(h * HD, HD), HD)

    own_c = lax.broadcasted_iota(jnp.int32, (rows, rows), 1)
    own_t = lax.broadcasted_iota(jnp.int32, (rows, rows), 0)

    def own_part():
        several = min(4, heads)
        own_bias = jnp.where(own_c <= own_t, 0.0, NEG)

        @pl.loop(0, heads // several)
        def _(block):
            stats = [own_stat[...]]

            def scores(k):
                cols = columns(block * several + k)
                return dot_t(q_ref[:, cols], pairs_ref[0, :, cols]) + own_bias

            def store(k, out, lse):
                own[:, columns(block * several + k)] = out
                stats[0] = jnp.where(lane == block * several + k, lse, stats[0])

            in_turn(
                list(range(several)), scores, lambda k: pairs_ref[1, :, columns(block * several + k)], store
            )
            own_stat[...] = stats[0]

    for g in range(GROUPS):
        c = lax.broadcasted_iota(jnp.int32, (size, window), 1)
        t = lax.broadcasted_iota(jnp.int32, (size, window), 0) + g * size
        bias[g] = jnp.where((c < SINK) | (c > t), 0.0, NEG)

    def prefix(g, slots):
        span = rows_of(g)
        valid = {d: (flag if d == 0 else flags.at[d - 1])[pl.ds(x, 1), :] for d in slots}
        several = min(8 // len(slots), heads)

        @pl.loop(0, heads // several)
        def _(block):
            stats = {d: stat[g, d, 0:size, :] for d in slots}

            def scores(job):
                k, d = job
                cols = columns(block * several + k)
                q = q_ref[span, cols] if d == 0 else q_slot(d, span)[:, cols]
                return dot_t(q, cache[0, :, cols]) + bias[g]

            def store(job, out, lse):
                k, d = job
                h = block * several + k
                part[d, span, columns(h)] = (out * valid[d]).astype(BF16)
                stats[d] = jnp.where(lane_g == h, lse * valid[d], stats[d])

            in_turn(
                [(k, d) for k in range(several) for d in slots], scores,
                lambda job: cache[1, :, columns(block * several + job[0])], store,
            )
            for d in slots:
                stat[g, d, 0:size, :] = stats[d]

        for d in slots:
            stat_t[g, d] = jnp.transpose(stat[g, d])[0:heads, :]

    def direct_out(g):
        low, high = rows_of(g, 0, part_half), rows_of(g, part_half, part_half)
        copies.start(("r_high", g), part.at[1, high], back.at[0, high], right)
        copies.start(("l_low", g), part.at[3, low], back.at[1, low], left)
        copies.start(("s1", g), stat_t.at[g, 1], stat_in.at[g, 0], right)
        copies.start(("s3", g), stat_t.at[g, 3], stat_in.at[g, 1], left)

    def relay_out(g):
        low, high = rows_of(g, 0, part_half), rows_of(g, part_half, part_half)
        copies.start(("relay_r", g), part.at[2, low], relay.at[g, 0], right)
        copies.start(("relay_l", g), part.at[2, high], relay.at[g, 1], left)
        copies.start(("s2", g), stat_t.at[g, 2], stat_in.at[g, 2], across)

    def relay_on(g):
        low, high = rows_of(g, 0, part_half), rows_of(g, part_half, part_half)
        copies.arrived(("relay_r", g))
        part[1, low, :] = part[1, low, :] + relay[g, 0]
        copies.start(("r_low", g), part.at[1, low], back.at[0, low], right)
        copies.arrived(("relay_l", g))
        part[3, high, :] = part[3, high, :] + relay[g, 1]
        copies.start(("l_high", g), part.at[3, high], back.at[1, high], left)

    tile = min(512, width)

    def finish(g):
        for key in ("s1", "s2", "s3", "r_high", "l_low", "r_low", "l_high"):
            copies.arrived((key, g))
        span = rows_of(g)
        total_t = stat_t[g, 0] + stat_in[g, 0] + stat_in[g, 1] + stat_in[g, 2]
        stat[g, 0] = jnp.transpose(jnp.concatenate([total_t, jnp.zeros((HD - heads, rows), F32)], axis=0))
        several = min(4, heads)

        @pl.loop(0, heads // several)
        def _(block):
            for k in range(several):
                h = block * several + k
                cols = columns(h)
                first = part[0, span, cols].astype(F32) + back[0, span, cols].astype(F32) + back[1, span, cols].astype(F32)
                lse_first = jnp.sum(jnp.where(lane_g == h, stat[g, 0, 0:size, :], 0.0), axis=1, keepdims=True)
                lse_own = jnp.sum(jnp.where(lane_g == h, own_stat[span, :], 0.0), axis=1, keepdims=True)
                top = jnp.maximum(lse_first, lse_own)
                a, b = jnp.exp(lse_first - top), jnp.exp(lse_own - top)
                attn[:, cols] = ((a * first + b * own[span, cols]) * (1.0 / (a + b))).astype(BF16)

        if g == 0:
            loads["weight"].wait()

        def project(j, squares):
            cols = pl.ds(pl.multiple_of(j * tile, tile), tile)
            weight = sums[:, :, cols].reshape(width, tile)
            res = hidden_ref[span, cols].astype(F32) + dot(attn[...], weight)
            own[span, cols] = res
            return squares + jnp.sum(res * res, axis=1, keepdims=True)

        squares = lax.fori_loop(0, width // tile, project, jnp.zeros((size, 1), F32))
        factor = lax.rsqrt(squares / width + 1e-05)

        @pl.loop(0, width // tile)
        def _(j):
            cols = pl.ds(pl.multiple_of(j * tile, tile), tile)
            tokens[0, span, cols] = (own[span, cols] * factor * gain_ref[:, cols]).astype(BF16)

    def view(dz, dy, start, count):
        return tokens.at[slot(dz, dy), pl.ds(start, count)]

    def start_of(kind):
        return kind[1] * size + (part_half if kind[0] == "b" else 0)

    def push(key, dz, dy, axis, step, start, count):
        device = {("z", 1): zp, ("z", -1): zm, ("y", 1): yp, ("y", -1): ym}[axis, step]
        tz, ty = ((dz - step) % SIDE, dy) if axis == "z" else (dz, (dy - step) % SIDE)
        copies.start((key, tz, ty), view(dz, dy, start, count), view(tz, ty, start, count), device)

    def both(kind, dz, dy, axis):
        push(kind, dz, dy, axis, 1, start_of(kind), part_half)
        push(kind, dz, dy, axis, -1, start_of(kind), part_half)

    def pass_on(kind, dz, dy, axis):
        behind = (dz if axis == "z" else dy) == 3
        start = start_of(kind) + (0 if behind else part_half // 2)
        push((kind, behind), dz, dy, axis, 1 if behind else -1, start, part_half // 2)

    waited = set()

    def have(kind, dz, dy):
        first, last = (dz, dy) if kind[0] == "a" else (dy, dz)
        if first == 0 and last == 0:
            return
        split = last == 2 or (last == 0 and first == 2)
        for key in ([(kind, True), (kind, False)] if split else [kind]):
            if (key, dz, dy) not in waited:
                waited.add((key, dz, dy))
                copies.arrived((key, dz, dy))

    def spread_0(g):
        both(("a", g), 0, 0, "z")
        both(("b", g), 0, 0, "y")
        both(("a", g), 0, 0, "y")
        both(("b", g), 0, 0, "z")

    def spread_1(g):
        for d in (3, 1):
            have(("a", g), d, 0)
            pass_on(("a", g), d, 0, "z")
            both(("a", g), d, 0, "y")
            have(("b", g), 0, d)
            pass_on(("b", g), 0, d, "y")
            both(("b", g), 0, d, "z")

    def spread_far(g):
        have(("a", g), 2, 0)
        both(("a", g), 2, 0, "y")
        have(("b", g), 0, 2)
        both(("b", g), 0, 2, "z")

    def pass_second(g, d):
        for near in (3, 1):
            have(("a", g), d, near)
            pass_on(("a", g), d, near, "y")
            have(("b", g), near, d)
            pass_on(("b", g), near, d, "z")

    ids = [e.astype(F32), (e + 1 - 2 * lax.rem(e, 2)).astype(F32)]
    span2 = 2 * CAP
    count = len(CHUNKS[0]) * CAP
    before = (
        lax.broadcasted_iota(jnp.int32, (rows, rows), 0) < lax.broadcasted_iota(jnp.int32, (rows, rows), 1)
    ).astype(BF16)
    slot_row = lax.broadcasted_iota(jnp.int32, (span2, rows), 0).astype(F32)

    def run_experts(chunk):
        pairs = [chunk[i:i + 2] for i in range(0, len(chunk), 2)]
        held = len(chunk) * CAP
        for p, pair in enumerate(pairs):
            gates = [jnp.zeros((span2, 1), F32)] * 2
            for i, (dz, dy) in enumerate(pair):
                source = slot(dz, dy)
                both_chosen = []
                for k in range(2):
                    named = (meta[source, 0:8, :] == ids[k]).astype(F32)
                    mine = jnp.sum(named, axis=0, keepdims=True)
                    gate = jnp.sum(named * meta[source, 8:16, :], axis=0, keepdims=True)
                    rank = dot(jnp.broadcast_to(mine, (8, rows)).astype(BF16), before)[0:1, :]
                    place = jnp.where(mine > 0.0, rank + float(i * CAP), -1.0)
                    chosen = (slot_row == place).astype(F32)
                    gates[k] = gates[k] + jnp.sum(chosen * gate, axis=1, keepdims=True)
                    both_chosen.append(chosen)
                chosen = jnp.concatenate(both_chosen, axis=0)
                pmat[p, :, i * rows:(i + 1) * rows] = chosen.astype(BF16)
                pmat_t[p, i * rows:(i + 1) * rows, :] = jnp.transpose(chosen).astype(BF16)
            for k in range(2):
                gslot[k, p * span2:(p + 1) * span2, :] = jnp.broadcast_to(gates[k], (span2, HD))
        tile = min(512, width)

        @pl.loop(0, width // tile)
        def _(j):
            cols = pl.ds(pl.multiple_of(j * tile, tile), tile)
            for p, pair in enumerate(pairs):
                joint = jnp.concatenate([tokens[slot(dz, dy), :, cols] for dz, dy in pair], axis=0)
                rows_out = dot(pmat[p], joint).astype(BF16)
                for k in range(2):
                    qrows[k * count + p * span2:k * count + (p + 1) * span2, cols] = rows_out[k * span2:(k + 1) * span2, :]

        tile_f = min(256, inner)

        @pl.loop(0, inner // tile_f)
        def _(j):
            start = pl.multiple_of(j * tile_f, tile_f)
            for k in range(2):
                gate = dot(qrows[k * count:k * count + held, :], up[k, :, pl.ds(start, tile_f)])
                lift = dot(qrows[k * count:k * count + held, :], up[k, :, pl.ds(pl.multiple_of(inner + start, tile_f), tile_f)])
                hid[k, 0:held, pl.ds(start, tile_f)] = (gate / (1.0 + jnp.exp(-gate)) * lift).astype(BF16)

        tile_d = min(256, width)
        turns = min(2, width // tile_d)

        @pl.loop(0, width // (turns * tile_d))
        def _(block):
            joint = []
            for turn in range(turns):
                cols = pl.ds(pl.multiple_of((block * turns + turn) * tile_d, tile_d), tile_d)
                made = [(dot(hid[k, 0:held, :], down[k, :, cols]) * gslot[k, 0:held, 0:1]).astype(BF16) for k in range(2)]
                joint.append([
                    jnp.concatenate([m[p * span2:(p + 1) * span2, :] for m in made], axis=0) for p in range(len(pairs))
                ])
            for turn in range(turns):
                cols = pl.ds(pl.multiple_of((block * turns + turn) * tile_d, tile_d), tile_d)
                for p, pair in enumerate(pairs):
                    placed = dot(pmat_t[p], joint[turn][p]).astype(BF16)
                    for i, (dz, dy) in enumerate(pair):
                        sums[slot(dz, dy), :, cols] = placed[i * rows:(i + 1) * rows, :]

    def sum_view(h, i, j, start, count):
        dz, dy = (i, j) if h == 0 else (j, i)
        return sums.at[slot(dz, dy), pl.ds(h * half + start, count)]

    first = ((yp, ym), (zp, zm))
    second = ((zp, zm), (yp, ym))

    def far_out(h, i):
        copies.start(("1+", h, i), sum_view(h, i, 2, 0, quarter), r1.at[h, i, pl.ds(0, quarter)], first[h][0])
        copies.start(("1-", h, i), sum_view(h, i, 2, quarter, quarter), r1.at[h, i, pl.ds(quarter, quarter)], first[h][1])

    def add_to(ref, more):
        ref[...] = (ref[...].astype(F32) + more[...].astype(F32)).astype(BF16)

    def near_out(h, i):
        copies.arrived(("1+", h, i))
        add_to(sum_view(h, i, 1, 0, quarter), r1.at[h, i, pl.ds(0, quarter)])
        copies.start(("2+", h, i), sum_view(h, i, 1, 0, half), r2.at[h, i, 0], first[h][0])
        copies.arrived(("1-", h, i))
        add_to(sum_view(h, i, 3, quarter, quarter), r1.at[h, i, pl.ds(quarter, quarter)])
        copies.start(("2-", h, i), sum_view(h, i, 3, 0, half), r2.at[h, i, 1], first[h][1])

    def gathered(h, i, start, count):
        span = pl.ds(start, count)
        return (
            sum_view(h, i, 0, start, count)[...].astype(F32)
            + r2[h, i, 0, span, :].astype(F32)
            + r2[h, i, 1, span, :].astype(F32)
        )

    def arrived_2(h, i):
        copies.arrived(("2+", h, i))
        copies.arrived(("2-", h, i))

    loads["cache"].wait()
    prefix(0, [0])
    q_on(0)
    own_part()
    copies.arrived("f1")
    copies.arrived("f3")
    q_near(0)
    prefix(0, [1, 3])
    direct_out(0)
    q_first(1)
    copies.arrived(("q2+", 0))
    copies.arrived(("q2-", 0))
    copies.arrived("f2")
    prefix(0, [2])
    relay_out(0)
    prefix(1, [0])
    relay_on(0)
    q_rest(1)
    for d in (3, 1):
        source = told(d, 0)
        tell(d, 3, source, yp)
        tell(d, 1, source, ym)
        if d == 3:
            tell(2, 0, source, zp)
    q_on(1)
    finish(0)
    spread_0(0)
    q_near(1)
    prefix(1, [1, 3])
    direct_out(1)
    spread_1(0)
    copies.arrived(("q2+", 1))
    copies.arrived(("q2-", 1))
    prefix(1, [2])
    relay_out(1)
    source = told(2, 0)
    tell(2, 3, source, yp)
    tell(2, 1, source, ym)
    pass_second(0, 0)
    relay_on(1)
    spread_far(0)
    finish(1)
    spread_0(1)
    for d in range(SIDE):
        tell(d, 2, told(d, 3), yp)
    pass_second(0, 1)
    pass_second(0, 3)
    spread_1(1)
    pass_second(0, 2)
    pass_second(1, 0)
    for d in range(SIDE):
        told(d, 1)
        told(d, 2)
    for key in ("up", "down"):
        loads[key].wait()
        copies.arrived(key)
    for g in range(GROUPS):
        for key in ("q2+", "q2-", "r_high", "l_low", "relay_r", "relay_l", "r_low", "l_high"):
            copies.left((key, g))

    def run(chunk):
        for dz, dy in chunk:
            for g in range(GROUPS):
                have(("a", g), dz, dy)
                have(("b", g), dz, dy)
        run_experts(chunk)

    level = part
    lo, hi = pl.ds(0, quarter), pl.ds(quarter, quarter)

    def level_rows(h, start, count):
        return pl.ds(h * half + start, count)

    def level_far(h):
        arrived_2(h, 2)
        level[2, level_rows(h, 0, half), :] = gathered(h, 2, 0, half).astype(BF16)
        copies.start(("3+", h), level.at[2, level_rows(h, 0, quarter)], r3.at[h, lo], second[h][0])
        copies.start(("3-", h), level.at[2, level_rows(h, quarter, quarter)], r3.at[h, hi], second[h][1])

    run(CHUNKS[0])
    spread_far(1)
    pass_second(1, 1)
    pass_second(1, 3)
    run(CHUNKS[1])
    pass_second(1, 2)
    for h, i in ((0, 0), (1, 0)):
        far_out(h, i)
    run(CHUNKS[2])
    for h, i in ((0, 1), (1, 1)):
        far_out(h, i)
    for h, i in ((0, 0), (1, 0)):
        near_out(h, i)
    run(CHUNKS[3])
    for h, i in ((0, 2), (1, 2), (0, 3), (1, 3)):
        far_out(h, i)
    run(CHUNKS[4])
    for h, i in ((0, 2), (1, 2), (0, 1), (1, 1)):
        near_out(h, i)
    level_far(0)
    level_far(1)
    for h, i in ((0, 3), (1, 3)):
        near_out(h, i)
    for h in range(2):
        arrived_2(h, 1)
        copies.arrived(("3+", h))
        level[1, level_rows(h, 0, quarter), :] = (gathered(h, 1, 0, quarter) + r3[h, lo, :].astype(F32)).astype(BF16)
        level[1, level_rows(h, quarter, quarter), :] = gathered(h, 1, quarter, quarter).astype(BF16)
        copies.start(("4+", h), level.at[1, level_rows(h, 0, half)], r4.at[h, 0], second[h][0])
        arrived_2(h, 3)
        copies.arrived(("3-", h))
        level[3, level_rows(h, 0, quarter), :] = gathered(h, 3, 0, quarter).astype(BF16)
        level[3, level_rows(h, quarter, quarter), :] = (gathered(h, 3, quarter, quarter) + r3[h, hi, :].astype(F32)).astype(BF16)
        copies.start(("4-", h), level.at[3, level_rows(h, 0, half)], r4.at[h, 1], second[h][1])
    for h in range(2):
        arrived_2(h, 0)
        copies.arrived(("4+", h))
        copies.arrived(("4-", h))
        span = pl.ds(h * half, half)
        mixture = gathered(h, 0, 0, half) + r4[h, 0].astype(F32) + r4[h, 1].astype(F32)
        position = lax.broadcasted_iota(jnp.int32, (half, width), 0) + h * half
        out_ref[span, :] = jnp.where(position < length, own[span, :] + mixture, 0.0).astype(BF16)
    copies.drain()


def layer(length, group, owner, queries, pairs, cache, weight, hidden, gain, routes, gates, upward, downward):
    rows, width = queries.shape
    heads = width // HD
    inner = downward.shape[0]
    half = rows // 2
    slots = SIDE * SIDE
    count = len(CHUNKS[0]) * CAP
    dma = pltpu.SemaphoreType.DMA
    return pl.pallas_call(
        layer_kernel,
        out_shape=jax.ShapeDtypeStruct((rows, width), BF16),
        in_specs=[SMEM, SMEM, SMEM, VMEM, VMEM, ANY, ANY, VMEM, VMEM, VMEM, VMEM, ANY, ANY],
        out_specs=VMEM,
        scratch_shapes=[
            pltpu.VMEM((3 * rows, width), BF16),
            pltpu.VMEM((8, HD), F32),
            pltpu.VMEM((3, 8, HD), F32),
            pltpu.VMEM(cache.shape, BF16),
            pltpu.VMEM((4, rows, width), BF16),
            pltpu.VMEM((GROUPS, 4, rows, HD), F32),
            pltpu.VMEM((GROUPS, 4, heads, rows), F32),
            pltpu.VMEM((GROUPS, 3, heads, rows), F32),
            pltpu.VMEM((rows, width), F32),
            pltpu.VMEM((rows, HD), F32),
            pltpu.VMEM((GROUPS, 2, rows // GROUPS // 2, width), BF16),
            pltpu.VMEM((2, rows, width), BF16),
            pltpu.VMEM((rows // GROUPS, width), BF16),
            pltpu.VMEM((GROUPS, rows // GROUPS, cache.shape[1]), F32),
            pltpu.VMEM((slots, 16, rows), F32),
            pltpu.VMEM((slots, rows, width), BF16),
            pltpu.VMEM((2,) + upward.shape, BF16),
            pltpu.VMEM((2,) + downward.shape, BF16),
            pltpu.VMEM((len(CHUNKS[0]) // 2, 4 * CAP, 2 * rows), BF16),
            pltpu.VMEM((len(CHUNKS[0]) // 2, 2 * rows, 4 * CAP), BF16),
            pltpu.VMEM((2, count, HD), F32),
            pltpu.VMEM((2, count, inner), BF16),
            pltpu.VMEM((slots, width // slots, width), BF16),
            pltpu.VMEM((2, SIDE, half, width), BF16),
            pltpu.VMEM((2, SIDE, 2, half, width), BF16),
            pltpu.VMEM((2, half, width), BF16),
            pltpu.VMEM((2, 2, half, width), BF16),
            dma((180,)),
            dma((180,)),
            dma((4,)),
        ],
        compiler_params=pltpu.CompilerParams(
            collective_id=0, has_side_effects=True, vmem_limit_bytes=VMEM_LIMIT
        ),
        name="layer",
    )(
        length, group, owner, queries, pairs, cache, weight.reshape(slots, width // slots, width), hidden, gain,
        routes, gates, upward, downward,
    )


def on_device(
    hidden_in, queries, suffix_pairs, prefix_cache, suffix_length, request_group, prefix_owner,
    out_weight, norm_gain, routes, gate_values, expert_upward, expert_downward,
):
    rows, width = hidden_in.shape[2:]
    out = layer(
        suffix_length, request_group, prefix_owner, queries[0, 0], suffix_pairs[0, 0], prefix_cache[0, 0], out_weight,
        hidden_in[0, 0], norm_gain.reshape(1, width), routes[0, 0], gate_values[0, 0], expert_upward[0], expert_downward[0],
    )
    return out.reshape(1, 1, rows, width)


def solution(mesh):
    in_specs = (
        P("req", "exp", None, None),
        P("req", "exp", None, None),
        P("req", "exp", None, None, None),
        P("exp", "req", None, None, None),
        P("req", "exp"),
        P("req", "exp"),
        P("exp", None),
        P(),
        P(),
        P("req", "exp", None, None),
        P("req", "exp", None, None),
        P("exp", None, None),
        P("exp", None, None),
    )
    out_specs = P("req", "exp", None, None)
    return jax.shard_map(
        on_device, mesh=mesh, in_specs=in_specs, out_specs=out_specs, check_vma=False
    )
```

```python
import functools

import jax
import jax.numpy as jnp
from jax import lax
from jax.experimental import pallas as pl
from jax.experimental.pallas import tpu as pltpu
from jax.sharding import PartitionSpec as P

HD = 128
SINK = 4
SIDE = 4
CAP = 40
NEG = -1e30
MESH = pl.DeviceIdType.MESH
VMEM_LIMIT = 67043328
F32 = jnp.float32
BF16 = jnp.bfloat16
ANY = pl.BlockSpec(memory_space=pl.ANY)
VMEM = pl.BlockSpec(memory_space=pltpu.VMEM)
SMEM = pl.BlockSpec(memory_space=pltpu.SMEM)


def dot_t(a, b):
    return lax.dot_general(a, b, (((1,), (1,)), ((), ())), preferred_element_type=F32)


def dot(a, b):
    return jnp.dot(a, b, preferred_element_type=F32)


class Copies:
    def __init__(self, send, recv):
        self.send, self.recv, self.made, self.gone = send, recv, {}, set()

    def start(self, key, src, dst, device):
        index = len(self.made)
        copy = pltpu.make_async_remote_copy(
            src_ref=src,
            dst_ref=dst,
            send_sem=self.send.at[index],
            recv_sem=self.recv.at[index],
            device_id=device,
            device_id_type=MESH,
        )
        copy.start()
        self.made[key] = copy

    def arrived(self, key):
        self.made[key].wait_recv()

    def left(self, key):
        self.made[key].wait_send()
        self.gone.add(key)

    def drain(self):
        for key, copy in self.made.items():
            if key not in self.gone:
                copy.wait_send()


def meet(devices):
    barrier = pltpu.get_barrier_semaphore()
    for device in devices:
        pl.semaphore_signal(barrier, inc=1, device_id=device, device_id_type=MESH)
    pl.semaphore_wait(barrier, len(devices))


def torus(req, e):
    core = lax.rem(e, 2)
    y = lax.rem(e // 2, SIDE)
    z = e // (2 * SIDE)

    def at(dz, dy):
        return (req, (lax.rem(z + dz, SIDE) * SIDE + lax.rem(y + dy, SIDE)) * 2 + core)

    return at(1, 0), at(3, 0), at(0, 1), at(0, 3)


GROUPS = 2
LOG2E = 1.4426950408889634
CHUNKS = (
    ((0, 0), (0, 1), (0, 3), (1, 0)),
    ((0, 2), (2, 0)),
    ((1, 2), (2, 1), (3, 0), (1, 1)),
    ((2, 2), (3, 2), (2, 3), (1, 3)),
    ((3, 1), (3, 3)),
)


def slot(dz, dy):
    return (dz % SIDE) * SIDE + dy % SIDE


def layer_kernel(
    length_ref, group_ref, owner_ref, q_ref, pairs_ref, cache_ref, weight_ref, hidden_ref, gain_ref,
    routes_ref, gates_ref, up_ref, down_ref,
    out_ref,
    qrows, flag, flags, cache, part, stat, stat_t, stat_in, own, own_stat, relay, back, attn,
    bias, meta, tokens, up, down, pmat, pmat_t, gslot, hid, sums, r1, r2, r3, r4,
    send, recv, local,
):
    x, e = lax.axis_index("req"), lax.axis_index("exp")
    right, left, across = (
        (lax.rem(x + 1, SIDE), e),
        (lax.rem(x + 3, SIDE), e),
        (lax.rem(x + 2, SIDE), e),
    )
    other = (x, e + 1 - 2 * lax.rem(e, 2))
    zp, zm, yp, ym = torus(x, e)
    rows, width = q_ref.shape
    heads = width // HD
    window = cache_ref.shape[1]
    inner = down_ref.shape[0]
    half, quarter = rows // 2, rows // 4
    size = rows // GROUPS
    part_half = size // 2
    copies = Copies(send, recv)

    loads = {}
    for index, (key, src, dst) in enumerate(
        (
            ("cache", cache_ref, cache),
            ("weight", weight_ref, sums),
            ("up", up_ref, up.at[0]),
            ("down", down_ref, down.at[0]),
        )
    ):
        loads[key] = pltpu.make_async_copy(src, dst, local.at[index])
        loads[key].start()

    length = length_ref[0, 0]
    group = group_ref[0, 0]
    owner = jnp.int32(0)
    for k in range(SIDE):
        owner = jnp.where(group == k, owner_ref[0, k], owner)
    flag[...] = (lax.broadcasted_iota(jnp.int32, (8, HD), 0) == owner).astype(F32)
    live = lax.broadcasted_iota(jnp.int32, (8, rows), 1) < length
    meta[0, 0:8, :] = jnp.where(live, jnp.transpose(routes_ref[...].astype(F32)), -1.0)
    meta[0, 8:16, :] = jnp.transpose(gates_ref[...])
    meet([right, left, across, other, zp, zm, yp, ym])

    def rows_of(g, start=0, count=None):
        return pl.ds(g * size + start, size if count is None else count)

    def q_slot(d, span):
        return qrows.at[pl.ds((d - 1) * rows + span.start, span.size)]

    def q_piece(g, hop, piece):
        span = rows_of(g, piece * part_half, part_half)
        copies.start(("q", hop, g, piece), q_ref.at[span], q_slot(hop, span), right if hop == 3 else left)

    def q_first(g):
        q_piece(g, 3, 0)
        q_piece(g, 1, 1)

    def q_rest(g):
        q_piece(g, 3, 1)
        q_piece(g, 1, 0)

    def q_on(g):
        low, high = rows_of(g, 0, part_half), rows_of(g, part_half, part_half)
        copies.arrived(("q", 3, g, 0))
        copies.start(("q2+", g), q_slot(3, low), q_slot(2, low), right)
        copies.arrived(("q", 1, g, 1))
        copies.start(("q2-", g), q_slot(1, high), q_slot(2, high), left)

    def q_near(g):
        copies.arrived(("q", 3, g, 1))
        copies.arrived(("q", 1, g, 0))

    q_first(0)
    q_rest(0)
    copies.start("f3", flag, flags.at[2], right)
    copies.start("f1", flag, flags.at[0], left)
    copies.start("f2", flag, flags.at[1], across)

    def tell(tz, ty, source, device):
        copies.start(("m", tz, ty), meta.at[source], meta.at[slot(tz, ty)], device)

    def told(tz, ty):
        copies.arrived(("m", tz, ty))
        return slot(tz, ty)

    tell(3, 0, 0, zp)
    tell(1, 0, 0, zm)
    tell(0, 3, 0, yp)
    tell(0, 1, 0, ym)
    copies.start("up", up_ref, up.at[1], other)
    copies.start("down", down_ref, down.at[1], other)

    scale = HD ** (-0.5)
    lane = lax.broadcasted_iota(jnp.int32, (rows, HD), 1)
    lane_g = lax.broadcasted_iota(jnp.int32, (size, HD), 1)
    stat[...] = jnp.zeros_like(stat)
    own_stat[...] = jnp.zeros_like(own_stat)

    def softmax(masked):
        largest = jnp.max(masked, axis=1, keepdims=True)
        weights = jnp.exp2((masked - largest) * (scale * LOG2E))
        totals = jnp.sum(weights, axis=1, keepdims=True)
        return weights.astype(BF16), 1.0 / totals, largest * scale + jnp.log(totals)

    def in_turn(jobs, scores, values, store):
        made, soft = {}, {}
        for step in range(len(jobs) + 2):
            if step < len(jobs):
                made[step] = scores(jobs[step])
            if 0 <= step - 1 < len(jobs):
                soft[step - 1] = softmax(made.pop(step - 1))
            if step >= 2:
                weights, inverse, lse = soft.pop(step - 2)
                store(jobs[step - 2], dot(weights, values(jobs[step - 2])) * inverse, lse)

    def columns(h):
        return pl.ds(pl.multiple_of(h * HD, HD), HD)

    own_c = lax.broadcasted_iota(jnp.int32, (rows, rows), 1)
    own_t = lax.broadcasted_iota(jnp.int32, (rows, rows), 0)

    def own_part():
        several = min(4, heads)
        own_bias = jnp.where(own_c <= own_t, 0.0, NEG)

        @pl.loop(0, heads // several)
        def _(block):
            stats = [own_stat[...]]

            def scores(k):
                cols = columns(block * several + k)
                return dot_t(q_ref[:, cols], pairs_ref[0, :, cols]) + own_bias

            def store(k, out, lse):
                own[:, columns(block * several + k)] = out
                stats[0] = jnp.where(lane == block * several + k, lse, stats[0])

            in_turn(
                list(range(several)), scores, lambda k: pairs_ref[1, :, columns(block * several + k)], store
            )
            own_stat[...] = stats[0]

    for g in range(GROUPS):
        c = lax.broadcasted_iota(jnp.int32, (size, window), 1)
        t = lax.broadcasted_iota(jnp.int32, (size, window), 0) + g * size
        bias[g] = jnp.where((c < SINK) | (c > t), 0.0, NEG)

    def prefix(g, slots):
        span = rows_of(g)
        valid = {d: (flag if d == 0 else flags.at[d - 1])[pl.ds(x, 1), :] for d in slots}
        several = min(8 // len(slots), heads)

        @pl.loop(0, heads // several)
        def _(block):
            stats = {d: stat[g, d, 0:size, :] for d in slots}

            def scores(job):
                k, d = job
                cols = columns(block * several + k)
                q = q_ref[span, cols] if d == 0 else q_slot(d, span)[:, cols]
                return dot_t(q, cache[0, :, cols]) + bias[g]

            def store(job, out, lse):
                k, d = job
                h = block * several + k
                part[d, span, columns(h)] = (out * valid[d]).astype(BF16)
                stats[d] = jnp.where(lane_g == h, lse * valid[d], stats[d])

            in_turn(
                [(k, d) for k in range(several) for d in slots], scores,
                lambda job: cache[1, :, columns(block * several + job[0])], store,
            )
            for d in slots:
                stat[g, d, 0:size, :] = stats[d]

        for d in slots:
            stat_t[g, d] = jnp.transpose(jnp.concatenate([stat[g, d], jnp.zeros((rows - size, HD), F32)], axis=0))[0:heads, :]

    def direct_out(g):
        low, high = rows_of(g, 0, part_half), rows_of(g, part_half, part_half)
        copies.start(("r_high", g), part.at[1, high], back.at[0, high], right)
        copies.start(("l_low", g), part.at[3, low], back.at[1, low], left)
        copies.start(("s1", g), stat_t.at[g, 1], stat_in.at[g, 0], right)
        copies.start(("s3", g), stat_t.at[g, 3], stat_in.at[g, 1], left)

    def relay_out(g):
        low, high = rows_of(g, 0, part_half), rows_of(g, part_half, part_half)
        copies.start(("relay_r", g), part.at[2, low], relay.at[g, 0], right)
        copies.start(("relay_l", g), part.at[2, high], relay.at[g, 1], left)
        copies.start(("s2", g), stat_t.at[g, 2], stat_in.at[g, 2], across)

    def relay_on(g):
        low, high = rows_of(g, 0, part_half), rows_of(g, part_half, part_half)
        copies.arrived(("relay_r", g))
        part[1, low, :] = part[1, low, :] + relay[g, 0]
        copies.start(("r_low", g), part.at[1, low], back.at[0, low], right)
        copies.arrived(("relay_l", g))
        part[3, high, :] = part[3, high, :] + relay[g, 1]
        copies.start(("l_high", g), part.at[3, high], back.at[1, high], left)

    tile = min(512, width)

    def finish(g):
        for key in ("s1", "s2", "s3", "r_high", "l_low", "r_low", "l_high"):
            copies.arrived((key, g))
        span = rows_of(g)
        total_t = stat_t[g, 0] + stat_in[g, 0] + stat_in[g, 1] + stat_in[g, 2]
        stat[g, 0] = jnp.transpose(jnp.concatenate([total_t, jnp.zeros((HD - heads, rows), F32)], axis=0))[0:size, :]
        several = min(4, heads)

        @pl.loop(0, heads // several)
        def _(block):
            for k in range(several):
                h = block * several + k
                cols = columns(h)
                first = part[0, span, cols].astype(F32) + back[0, span, cols].astype(F32) + back[1, span, cols].astype(F32)
                lse_first = jnp.sum(jnp.where(lane_g == h, stat[g, 0, 0:size, :], 0.0), axis=1, keepdims=True)
                lse_own = jnp.sum(jnp.where(lane_g == h, own_stat[span, :], 0.0), axis=1, keepdims=True)
                top = jnp.maximum(lse_first, lse_own)
                a, b = jnp.exp(lse_first - top), jnp.exp(lse_own - top)
                attn[:, cols] = ((a * first + b * own[span, cols]) * (1.0 / (a + b))).astype(BF16)

        if g == 0:
            loads["weight"].wait()

        def project(j, squares):
            cols = pl.ds(pl.multiple_of(j * tile, tile), tile)
            weight = sums[:, :, cols].reshape(width, tile)
            res = hidden_ref[span, cols].astype(F32) + dot(attn[...], weight)
            own[span, cols] = res
            return squares + jnp.sum(res * res, axis=1, keepdims=True)

        squares = lax.fori_loop(0, width // tile, project, jnp.zeros((size, 1), F32))
        factor = lax.rsqrt(squares / width + 1e-05)

        @pl.loop(0, width // tile)
        def _(j):
            cols = pl.ds(pl.multiple_of(j * tile, tile), tile)
            tokens[0, span, cols] = (own[span, cols] * factor * gain_ref[:, cols]).astype(BF16)

    def view(dz, dy, start, count):
        return tokens.at[slot(dz, dy), pl.ds(start, count)]

    def start_of(kind):
        return kind[1] * size + (part_half if kind[0] == "b" else 0)

    def push(key, dz, dy, axis, step, start, count):
        device = {("z", 1): zp, ("z", -1): zm, ("y", 1): yp, ("y", -1): ym}[axis, step]
        tz, ty = ((dz - step) % SIDE, dy) if axis == "z" else (dz, (dy - step) % SIDE)
        copies.start((key, tz, ty), view(dz, dy, start, count), view(tz, ty, start, count), device)

    def both(kind, dz, dy, axis):
        push(kind, dz, dy, axis, 1, start_of(kind), part_half)
        push(kind, dz, dy, axis, -1, start_of(kind), part_half)

    def pass_on(kind, dz, dy, axis):
        behind = (dz if axis == "z" else dy) == 3
        start = start_of(kind) + (0 if behind else part_half // 2)
        push((kind, behind), dz, dy, axis, 1 if behind else -1, start, part_half // 2)

    waited = set()

    def have(kind, dz, dy):
        first, last = (dz, dy) if kind[0] == "a" else (dy, dz)
        if first == 0 and last == 0:
            return
        split = last == 2 or (last == 0 and first == 2)
        for key in ([(kind, True), (kind, False)] if split else [kind]):
            if (key, dz, dy) not in waited:
                waited.add((key, dz, dy))
                copies.arrived((key, dz, dy))

    def spread_0(g):
        both(("a", g), 0, 0, "z")
        both(("b", g), 0, 0, "y")
        both(("a", g), 0, 0, "y")
        both(("b", g), 0, 0, "z")

    def spread_1(g):
        for d in (3, 1):
            have(("a", g), d, 0)
            pass_on(("a", g), d, 0, "z")
            both(("a", g), d, 0, "y")
            have(("b", g), 0, d)
            pass_on(("b", g), 0, d, "y")
            both(("b", g), 0, d, "z")

    def spread_far(g):
        have(("a", g), 2, 0)
        both(("a", g), 2, 0, "y")
        have(("b", g), 0, 2)
        both(("b", g), 0, 2, "z")

    def pass_second(g, d):
        for near in (3, 1):
            have(("a", g), d, near)
            pass_on(("a", g), d, near, "y")
            have(("b", g), near, d)
            pass_on(("b", g), near, d, "z")

    ids = [e.astype(F32), (e + 1 - 2 * lax.rem(e, 2)).astype(F32)]
    span2 = 2 * CAP
    count = len(CHUNKS[0]) * CAP
    before = (
        lax.broadcasted_iota(jnp.int32, (rows, rows), 0) < lax.broadcasted_iota(jnp.int32, (rows, rows), 1)
    ).astype(BF16)
    slot_row = lax.broadcasted_iota(jnp.int32, (span2, rows), 0).astype(F32)

    pairs_of, total = {}, 0
    for chunk in CHUNKS:
        pairs_of[chunk] = [(total + i // 2, chunk[i:i + 2]) for i in range(0, len(chunk), 2)]
        total += len(chunk) // 2

    def place_tokens(chunk):
        for p, pair in pairs_of[chunk]:
            gates = [jnp.zeros((span2, 1), F32)] * 2
            for i, (dz, dy) in enumerate(pair):
                source = slot(dz, dy)
                both_chosen = []
                for k in range(2):
                    named = (meta[source, 0:8, :] == ids[k]).astype(F32)
                    mine = jnp.sum(named, axis=0, keepdims=True)
                    gate = jnp.sum(named * meta[source, 8:16, :], axis=0, keepdims=True)
                    rank = dot(jnp.broadcast_to(mine, (8, rows)).astype(BF16), before)[0:1, :]
                    place = jnp.where(mine > 0.0, rank + float(i * CAP), -1.0)
                    chosen = (slot_row == place).astype(F32)
                    gates[k] = gates[k] + jnp.sum(chosen * gate, axis=1, keepdims=True)
                    both_chosen.append(chosen)
                chosen = jnp.concatenate(both_chosen, axis=0)
                pmat[p, :, i * rows:(i + 1) * rows] = chosen.astype(BF16)
                pmat_t[p, i * rows:(i + 1) * rows, :] = jnp.transpose(chosen).astype(BF16)
            for k in range(2):
                gslot[:, 2 * p + k:2 * p + k + 1] = gates[k]

    def run_experts(chunk):
        pairs = pairs_of[chunk]
        held = len(chunk) * CAP
        tile = min(1024, width)
        for start in range(0, width, tile):
            cols = pl.ds(start, tile)
            for n, (p, pair) in enumerate(pairs):
                joint = jnp.concatenate([tokens[slot(dz, dy), :, cols] for dz, dy in pair], axis=0)
                rows_out = dot(pmat[p], joint).astype(BF16)
                for k in range(2):
                    qrows[k * count + n * span2:k * count + (n + 1) * span2, cols] = rows_out[k * span2:(k + 1) * span2, :]

        tile_f = min(256, inner)

        @pl.loop(0, inner // tile_f)
        def _(j):
            start = pl.multiple_of(j * tile_f, tile_f)
            for k in range(2):
                gate = dot(qrows[k * count:k * count + held, :], up[k, :, pl.ds(start, tile_f)])
                lift = dot(qrows[k * count:k * count + held, :], up[k, :, pl.ds(pl.multiple_of(inner + start, tile_f), tile_f)])
                hid[k, 0:held, pl.ds(start, tile_f)] = (gate / (1.0 + jnp.exp(-gate)) * lift).astype(BF16)

        tile_d = min(256, width)
        turns = min(2, width // tile_d)

        @pl.loop(0, width // (turns * tile_d))
        def _(block):
            joint = []
            for turn in range(turns):
                cols = pl.ds(pl.multiple_of((block * turns + turn) * tile_d, tile_d), tile_d)
                made = []
                for k in range(2):
                    gates = jnp.concatenate([gslot[:, 2 * p + k:2 * p + k + 1] for p, _ in pairs], axis=0)
                    made.append((dot(hid[k, 0:held, :], down[k, :, cols]) * gates).astype(BF16))
                joint.append([
                    jnp.concatenate([m[n * span2:(n + 1) * span2, :] for m in made], axis=0) for n in range(len(pairs))
                ])
            for turn in range(turns):
                cols = pl.ds(pl.multiple_of((block * turns + turn) * tile_d, tile_d), tile_d)
                for n, (p, pair) in enumerate(pairs):
                    placed = dot(pmat_t[p], joint[turn][n]).astype(BF16)
                    for i, (dz, dy) in enumerate(pair):
                        sums[slot(dz, dy), :, cols] = placed[i * rows:(i + 1) * rows, :]

    def sum_view(h, i, j, start, count):
        dz, dy = (i, j) if h == 0 else (j, i)
        return sums.at[slot(dz, dy), pl.ds(h * half + start, count)]

    first = ((yp, ym), (zp, zm))
    second = ((zp, zm), (yp, ym))

    def far_out(h, i):
        copies.start(("1+", h, i), sum_view(h, i, 2, 0, quarter), r1.at[h, i, pl.ds(0, quarter)], first[h][0])
        copies.start(("1-", h, i), sum_view(h, i, 2, quarter, quarter), r1.at[h, i, pl.ds(quarter, quarter)], first[h][1])

    def add_to(ref, more):
        ref[...] = (ref[...].astype(F32) + more[...].astype(F32)).astype(BF16)

    def near_out(h, i):
        copies.arrived(("1+", h, i))
        add_to(sum_view(h, i, 1, 0, quarter), r1.at[h, i, pl.ds(0, quarter)])
        copies.start(("2+", h, i), sum_view(h, i, 1, 0, half), r2.at[h, i, 0], first[h][0])
        copies.arrived(("1-", h, i))
        add_to(sum_view(h, i, 3, quarter, quarter), r1.at[h, i, pl.ds(quarter, quarter)])
        copies.start(("2-", h, i), sum_view(h, i, 3, 0, half), r2.at[h, i, 1], first[h][1])

    def gathered(h, i, start, count):
        span = pl.ds(start, count)
        return (
            sum_view(h, i, 0, start, count)[...].astype(F32)
            + r2[h, i, 0, span, :].astype(F32)
            + r2[h, i, 1, span, :].astype(F32)
        )

    def arrived_2(h, i):
        copies.arrived(("2+", h, i))
        copies.arrived(("2-", h, i))

    loads["cache"].wait()
    prefix(0, [0])
    q_on(0)
    own_part()
    copies.arrived("f1")
    copies.arrived("f3")
    q_near(0)
    prefix(0, [1, 3])
    direct_out(0)
    copies.arrived(("q2+", 0))
    copies.arrived(("q2-", 0))
    copies.arrived("f2")
    prefix(0, [2])
    relay_out(0)
    q_first(1)
    prefix(1, [0])
    relay_on(0)
    q_rest(1)
    for d in (3, 1):
        source = told(d, 0)
        tell(d, 3, source, yp)
        tell(d, 1, source, ym)
        if d == 3:
            tell(2, 0, source, zp)
    q_on(1)
    finish(0)
    spread_0(0)
    q_near(1)
    prefix(1, [1, 3])
    direct_out(1)
    spread_1(0)
    copies.arrived(("q2+", 1))
    copies.arrived(("q2-", 1))
    prefix(1, [2])
    relay_out(1)
    source = told(2, 0)
    tell(2, 3, source, yp)
    tell(2, 1, source, ym)
    pass_second(0, 0)
    relay_on(1)
    spread_far(0)
    for d in range(SIDE):
        tell(d, 2, told(d, 3), yp)
    finish(1)
    spread_0(1)
    pass_second(0, 1)
    pass_second(0, 3)
    for d in range(SIDE):
        told(d, 1)
        told(d, 2)
    place_tokens(CHUNKS[0])
    place_tokens(CHUNKS[1])
    place_tokens(CHUNKS[2])
    spread_1(1)
    pass_second(0, 2)
    place_tokens(CHUNKS[3])
    place_tokens(CHUNKS[4])
    pass_second(1, 0)
    for key in ("up", "down"):
        loads[key].wait()
        copies.arrived(key)
    for g in range(GROUPS):
        for key in ("q2+", "q2-", "r_high", "l_low", "relay_r", "relay_l", "r_low", "l_high"):
            copies.left((key, g))

    def run(chunk):
        for dz, dy in chunk:
            for g in range(GROUPS):
                have(("a", g), dz, dy)
                have(("b", g), dz, dy)
        run_experts(chunk)

    level = part
    lo, hi = pl.ds(0, quarter), pl.ds(quarter, quarter)

    def level_rows(h, start, count):
        return pl.ds(h * half + start, count)

    def level_far(h):
        arrived_2(h, 2)
        level[2, level_rows(h, 0, half), :] = gathered(h, 2, 0, half).astype(BF16)
        copies.start(("3+", h), level.at[2, level_rows(h, 0, quarter)], r3.at[h, lo], second[h][0])
        copies.start(("3-", h), level.at[2, level_rows(h, quarter, quarter)], r3.at[h, hi], second[h][1])

    run(CHUNKS[0])
    spread_far(1)
    pass_second(1, 1)
    pass_second(1, 3)
    run(CHUNKS[1])
    pass_second(1, 2)
    for h, i in ((0, 0), (1, 0)):
        far_out(h, i)
    run(CHUNKS[2])
    for h, i in ((0, 1), (1, 1)):
        far_out(h, i)
    for h, i in ((0, 0), (1, 0)):
        near_out(h, i)
    run(CHUNKS[3])
    for h, i in ((0, 2), (1, 2), (0, 3), (1, 3)):
        far_out(h, i)
    run(CHUNKS[4])
    for h, i in ((0, 2), (1, 2), (0, 1), (1, 1)):
        near_out(h, i)
    level_far(0)
    level_far(1)
    for h, i in ((0, 3), (1, 3)):
        near_out(h, i)
    for h in range(2):
        arrived_2(h, 1)
        copies.arrived(("3+", h))
        level[1, level_rows(h, 0, quarter), :] = (gathered(h, 1, 0, quarter) + r3[h, lo, :].astype(F32)).astype(BF16)
        level[1, level_rows(h, quarter, quarter), :] = gathered(h, 1, quarter, quarter).astype(BF16)
        copies.start(("4+", h), level.at[1, level_rows(h, 0, half)], r4.at[h, 0], second[h][0])
        arrived_2(h, 3)
        copies.arrived(("3-", h))
        level[3, level_rows(h, 0, quarter), :] = gathered(h, 3, 0, quarter).astype(BF16)
        level[3, level_rows(h, quarter, quarter), :] = (gathered(h, 3, quarter, quarter) + r3[h, hi, :].astype(F32)).astype(BF16)
        copies.start(("4-", h), level.at[3, level_rows(h, 0, half)], r4.at[h, 1], second[h][1])
    for h in range(2):
        arrived_2(h, 0)
        copies.arrived(("4+", h))
        copies.arrived(("4-", h))
        span = pl.ds(h * half, half)
        mixture = gathered(h, 0, 0, half) + r4[h, 0].astype(F32) + r4[h, 1].astype(F32)
        position = lax.broadcasted_iota(jnp.int32, (half, width), 0) + h * half
        out_ref[span, :] = jnp.where(position < length, own[span, :] + mixture, 0.0).astype(BF16)
    copies.drain()


def layer(length, group, owner, queries, pairs, cache, weight, hidden, gain, routes, gates, upward, downward):
    rows, width = queries.shape
    heads = width // HD
    inner = downward.shape[0]
    half = rows // 2
    slots = SIDE * SIDE
    count = len(CHUNKS[0]) * CAP
    dma = pltpu.SemaphoreType.DMA
    return pl.pallas_call(
        layer_kernel,
        out_shape=jax.ShapeDtypeStruct((rows, width), BF16),
        in_specs=[SMEM, SMEM, SMEM, VMEM, VMEM, ANY, ANY, VMEM, VMEM, VMEM, VMEM, ANY, ANY],
        out_specs=VMEM,
        scratch_shapes=[
            pltpu.VMEM((3 * rows, width), BF16),
            pltpu.VMEM((8, HD), F32),
            pltpu.VMEM((3, 8, HD), F32),
            pltpu.VMEM(cache.shape, BF16),
            pltpu.VMEM((4, rows, width), BF16),
            pltpu.VMEM((GROUPS, 4, rows // GROUPS, HD), F32),
            pltpu.VMEM((GROUPS, 4, heads, rows), F32),
            pltpu.VMEM((GROUPS, 3, heads, rows), F32),
            pltpu.VMEM((rows, width), F32),
            pltpu.VMEM((rows, HD), F32),
            pltpu.VMEM((GROUPS, 2, rows // GROUPS // 2, width), BF16),
            pltpu.VMEM((2, rows, width), BF16),
            pltpu.VMEM((rows // GROUPS, width), BF16),
            pltpu.VMEM((GROUPS, rows // GROUPS, cache.shape[1]), F32),
            pltpu.VMEM((slots, 16, rows), F32),
            pltpu.VMEM((slots, rows, width), BF16),
            pltpu.VMEM((2,) + upward.shape, BF16),
            pltpu.VMEM((2,) + downward.shape, BF16),
            pltpu.VMEM((slots // 2, 4 * CAP, 2 * rows), BF16),
            pltpu.VMEM((slots // 2, 2 * rows, 4 * CAP), BF16),
            pltpu.VMEM((2 * CAP, HD), F32),
            pltpu.VMEM((2, count, inner), BF16),
            pltpu.VMEM((slots, width // slots, width), BF16),
            pltpu.VMEM((2, SIDE, half, width), BF16),
            pltpu.VMEM((2, SIDE, 2, half, width), BF16),
            pltpu.VMEM((2, half, width), BF16),
            pltpu.VMEM((2, 2, half, width), BF16),
            dma((180,)),
            dma((180,)),
            dma((4,)),
        ],
        compiler_params=pltpu.CompilerParams(
            collective_id=0, has_side_effects=True, vmem_limit_bytes=VMEM_LIMIT
        ),
        name="layer",
    )(
        length, group, owner, queries, pairs, cache, weight.reshape(slots, width // slots, width), hidden, gain,
        routes, gates, upward, downward,
    )


def on_device(
    hidden_in, queries, suffix_pairs, prefix_cache, suffix_length, request_group, prefix_owner,
    out_weight, norm_gain, routes, gate_values, expert_upward, expert_downward,
):
    rows, width = hidden_in.shape[2:]
    out = layer(
        suffix_length, request_group, prefix_owner, queries[0, 0], suffix_pairs[0, 0], prefix_cache[0, 0], out_weight,
        hidden_in[0, 0], norm_gain.reshape(1, width), routes[0, 0], gate_values[0, 0], expert_upward[0], expert_downward[0],
    )
    return out.reshape(1, 1, rows, width)


def solution(mesh):
    in_specs = (
        P("req", "exp", None, None),
        P("req", "exp", None, None),
        P("req", "exp", None, None, None),
        P("exp", "req", None, None, None),
        P("req", "exp"),
        P("req", "exp"),
        P("exp", None),
        P(),
        P(),
        P("req", "exp", None, None),
        P("req", "exp", None, None),
        P("exp", None, None),
        P("exp", None, None),
    )
    out_specs = P("req", "exp", None, None)
    return jax.shard_map(
        on_device, mesh=mesh, in_specs=in_specs, out_specs=out_specs, check_vma=False
    )
```

```python
import functools

import jax
import jax.numpy as jnp
from jax import lax
from jax.experimental import pallas as pl
from jax.experimental.pallas import tpu as pltpu
from jax.sharding import PartitionSpec as P

HD = 128
SINK = 4
SIDE = 4
CAP = 40
NEG = -1e30
MESH = pl.DeviceIdType.MESH
VMEM_LIMIT = 67043328
F32 = jnp.float32
BF16 = jnp.bfloat16
ANY = pl.BlockSpec(memory_space=pl.ANY)
VMEM = pl.BlockSpec(memory_space=pltpu.VMEM)
SMEM = pl.BlockSpec(memory_space=pltpu.SMEM)


def dot_t(a, b):
    return lax.dot_general(a, b, (((1,), (1,)), ((), ())), preferred_element_type=F32)


def dot(a, b):
    return jnp.dot(a, b, preferred_element_type=F32)


class Copies:
    def __init__(self, send, recv):
        self.send, self.recv, self.made, self.gone = send, recv, {}, set()

    def start(self, key, src, dst, device):
        index = len(self.made)
        copy = pltpu.make_async_remote_copy(
            src_ref=src,
            dst_ref=dst,
            send_sem=self.send.at[index],
            recv_sem=self.recv.at[index],
            device_id=device,
            device_id_type=MESH,
        )
        copy.start()
        self.made[key] = copy

    def arrived(self, key):
        self.made[key].wait_recv()

    def left(self, key):
        self.made[key].wait_send()
        self.gone.add(key)

    def drain(self):
        for key, copy in self.made.items():
            if key not in self.gone:
                copy.wait_send()


def meet(devices):
    barrier = pltpu.get_barrier_semaphore()
    for device in devices:
        pl.semaphore_signal(barrier, inc=1, device_id=device, device_id_type=MESH)
    pl.semaphore_wait(barrier, len(devices))


def torus(req, e):
    core = lax.rem(e, 2)
    y = lax.rem(e // 2, SIDE)
    z = e // (2 * SIDE)

    def at(dz, dy):
        return (req, (lax.rem(z + dz, SIDE) * SIDE + lax.rem(y + dy, SIDE)) * 2 + core)

    return at(1, 0), at(3, 0), at(0, 1), at(0, 3)


GROUPS = 2
LOG2E = 1.4426950408889634
CHUNKS = (
    ((0, 0), (0, 1), (0, 3), (1, 0)),
    ((0, 2), (2, 0)),
    ((1, 2), (2, 1), (3, 0), (1, 1)),
    ((2, 2), (3, 2), (2, 3), (1, 3)),
    ((3, 1), (3, 3)),
)


def slot(dz, dy):
    return (dz % SIDE) * SIDE + dy % SIDE


def layer_kernel(
    length_ref, group_ref, owner_ref, q_ref, pairs_ref, cache_ref, weight_ref, hidden_ref, gain_ref,
    routes_ref, gates_ref, up_ref, down_ref,
    out_ref,
    qrows, flag, flags, cache, part, stat, stat_t, stat_in, own, own_stat, relay, back, attn,
    bias, meta, tokens, up, down, pmat, pmat_t, gslot, hid, sums, r1, r2, r3, r4,
    send, recv, local,
):
    x, e = lax.axis_index("req"), lax.axis_index("exp")
    right, left, across = (
        (lax.rem(x + 1, SIDE), e),
        (lax.rem(x + 3, SIDE), e),
        (lax.rem(x + 2, SIDE), e),
    )
    other = (x, e + 1 - 2 * lax.rem(e, 2))
    zp, zm, yp, ym = torus(x, e)
    rows, width = q_ref.shape
    heads = width // HD
    window = cache_ref.shape[1]
    inner = down_ref.shape[0]
    half, quarter = rows // 2, rows // 4
    size = rows // GROUPS
    part_half = size // 2
    copies = Copies(send, recv)

    loads = {}
    for index, (key, src, dst) in enumerate(
        (
            ("cache", cache_ref, cache),
            ("weight", weight_ref, sums),
            ("up", up_ref, up.at[0]),
            ("down", down_ref, down.at[0]),
        )
    ):
        loads[key] = pltpu.make_async_copy(src, dst, local.at[index])
        loads[key].start()

    length = length_ref[0, 0]
    group = group_ref[0, 0]
    owner = jnp.int32(0)
    for k in range(SIDE):
        owner = jnp.where(group == k, owner_ref[0, k], owner)
    flag[...] = (lax.broadcasted_iota(jnp.int32, (8, HD), 0) == owner).astype(F32)
    live = lax.broadcasted_iota(jnp.int32, (8, rows), 1) < length
    meta[0, 0:8, :] = jnp.where(live, jnp.transpose(routes_ref[...].astype(F32)), -1.0)
    meta[0, 8:16, :] = jnp.transpose(gates_ref[...])
    meet([right, left, across, other, zp, zm, yp, ym])

    def rows_of(g, start=0, count=None):
        return pl.ds(g * size + start, size if count is None else count)

    def q_slot(d, span):
        return qrows.at[pl.ds((d - 1) * rows + span.start, span.size)]

    def q_piece(g, hop, piece):
        span = rows_of(g, piece * part_half, part_half)
        copies.start(("q", hop, g, piece), q_ref.at[span], q_slot(hop, span), right if hop == 3 else left)

    def q_first(g):
        q_piece(g, 3, 0)
        q_piece(g, 1, 1)

    def q_rest(g):
        q_piece(g, 3, 1)
        q_piece(g, 1, 0)

    def q_on(g):
        low, high = rows_of(g, 0, part_half), rows_of(g, part_half, part_half)
        copies.arrived(("q", 3, g, 0))
        copies.start(("q2+", g), q_slot(3, low), q_slot(2, low), right)
        copies.arrived(("q", 1, g, 1))
        copies.start(("q2-", g), q_slot(1, high), q_slot(2, high), left)

    def q_near(g):
        copies.arrived(("q", 3, g, 1))
        copies.arrived(("q", 1, g, 0))

    q_first(0)
    q_rest(0)
    copies.start("f3", flag, flags.at[2], right)
    copies.start("f1", flag, flags.at[0], left)
    copies.start("f2", flag, flags.at[1], across)

    def tell(tz, ty, source, device):
        copies.start(("m", tz, ty), meta.at[source], meta.at[slot(tz, ty)], device)

    def told(tz, ty):
        copies.arrived(("m", tz, ty))
        return slot(tz, ty)

    tell(3, 0, 0, zp)
    tell(1, 0, 0, zm)
    tell(0, 3, 0, yp)
    tell(0, 1, 0, ym)
    copies.start("up", up_ref, up.at[1], other)
    copies.start("down", down_ref, down.at[1], other)

    scale = HD ** (-0.5)
    lane = lax.broadcasted_iota(jnp.int32, (rows, HD), 1)
    lane_g = lax.broadcasted_iota(jnp.int32, (size, HD), 1)
    stat[...] = jnp.zeros_like(stat)
    own_stat[...] = jnp.zeros_like(own_stat)

    def softmax(masked):
        largest = jnp.max(masked, axis=1, keepdims=True)
        weights = jnp.exp2((masked - largest) * (scale * LOG2E))
        totals = jnp.sum(weights, axis=1, keepdims=True)
        return weights.astype(BF16), 1.0 / totals, largest * scale + jnp.log(totals)

    def in_turn(jobs, scores, values, store):
        made, soft = {}, {}
        for step in range(len(jobs) + 2):
            if step < len(jobs):
                made[step] = scores(jobs[step])
            if 0 <= step - 1 < len(jobs):
                soft[step - 1] = softmax(made.pop(step - 1))
            if step >= 2:
                weights, inverse, lse = soft.pop(step - 2)
                store(jobs[step - 2], dot(weights, values(jobs[step - 2])) * inverse, lse)

    def columns(h):
        return pl.ds(pl.multiple_of(h * HD, HD), HD)

    own_c = lax.broadcasted_iota(jnp.int32, (rows, rows), 1)
    own_t = lax.broadcasted_iota(jnp.int32, (rows, rows), 0)

    def own_part():
        several = min(4, heads)
        own_bias = jnp.where(own_c <= own_t, 0.0, NEG)

        @pl.loop(0, heads // several)
        def _(block):
            stats = [own_stat[...]]

            def scores(k):
                cols = columns(block * several + k)
                return dot_t(q_ref[:, cols], pairs_ref[0, :, cols]) + own_bias

            def store(k, out, lse):
                own[:, columns(block * several + k)] = out
                stats[0] = jnp.where(lane == block * several + k, lse, stats[0])

            in_turn(
                list(range(several)), scores, lambda k: pairs_ref[1, :, columns(block * several + k)], store
            )
            own_stat[...] = stats[0]

    for g in range(GROUPS):
        c = lax.broadcasted_iota(jnp.int32, (size, window), 1)
        t = lax.broadcasted_iota(jnp.int32, (size, window), 0) + g * size
        bias[g] = jnp.where((c < SINK) | (c > t), 0.0, NEG)

    def prefix(g, slots):
        span = rows_of(g)
        valid = {d: (flag if d == 0 else flags.at[d - 1])[pl.ds(x, 1), :] for d in slots}
        several = min(8 // len(slots), heads)

        @pl.loop(0, heads // several)
        def _(block):
            stats = {d: stat[g, d, 0:size, :] for d in slots}

            def scores(job):
                k, d = job
                cols = columns(block * several + k)
                q = q_ref[span, cols] if d == 0 else q_slot(d, span)[:, cols]
                return dot_t(q, cache[0, :, cols]) + bias[g]

            def store(job, out, lse):
                k, d = job
                h = block * several + k
                part[d, span, columns(h)] = (out * valid[d]).astype(BF16)
                stats[d] = jnp.where(lane_g == h, lse * valid[d], stats[d])

            in_turn(
                [(k, d) for k in range(several) for d in slots], scores,
                lambda job: cache[1, :, columns(block * several + job[0])], store,
            )
            for d in slots:
                stat[g, d, 0:size, :] = stats[d]

        for d in slots:
            stat_t[g, d] = jnp.transpose(jnp.concatenate([stat[g, d], jnp.zeros((rows - size, HD), F32)], axis=0))[0:heads, :]

    def direct_out(g):
        low, high = rows_of(g, 0, part_half), rows_of(g, part_half, part_half)
        copies.start(("r_high", g), part.at[1, high], back.at[0, high], right)
        copies.start(("l_low", g), part.at[3, low], back.at[1, low], left)
        copies.start(("s1", g), stat_t.at[g, 1], stat_in.at[g, 0], right)
        copies.start(("s3", g), stat_t.at[g, 3], stat_in.at[g, 1], left)

    def relay_out(g):
        low, high = rows_of(g, 0, part_half), rows_of(g, part_half, part_half)
        copies.start(("relay_r", g), part.at[2, low], relay.at[g, 0], right)
        copies.start(("relay_l", g), part.at[2, high], relay.at[g, 1], left)
        copies.start(("s2", g), stat_t.at[g, 2], stat_in.at[g, 2], across)

    def relay_on(g):
        low, high = rows_of(g, 0, part_half), rows_of(g, part_half, part_half)
        copies.arrived(("relay_r", g))
        part[1, low, :] = part[1, low, :] + relay[g, 0]
        copies.start(("r_low", g), part.at[1, low], back.at[0, low], right)
        copies.arrived(("relay_l", g))
        part[3, high, :] = part[3, high, :] + relay[g, 1]
        copies.start(("l_high", g), part.at[3, high], back.at[1, high], left)

    tile = min(1024, width)

    def finish(g):
        for key in ("s1", "s2", "s3", "r_high", "l_low", "r_low", "l_high"):
            copies.arrived((key, g))
        span = rows_of(g)
        total_t = stat_t[g, 0] + stat_in[g, 0] + stat_in[g, 1] + stat_in[g, 2]
        stat[g, 0] = jnp.transpose(jnp.concatenate([total_t, jnp.zeros((HD - heads, rows), F32)], axis=0))[0:size, :]
        several = min(4, heads)

        @pl.loop(0, heads // several)
        def _(block):
            for k in range(several):
                h = block * several + k
                cols = columns(h)
                first = part[0, span, cols].astype(F32) + back[0, span, cols].astype(F32) + back[1, span, cols].astype(F32)
                lse_first = jnp.sum(jnp.where(lane_g == h, stat[g, 0, 0:size, :], 0.0), axis=1, keepdims=True)
                lse_own = jnp.sum(jnp.where(lane_g == h, own_stat[span, :], 0.0), axis=1, keepdims=True)
                top = jnp.maximum(lse_first, lse_own)
                a, b = jnp.exp(lse_first - top), jnp.exp(lse_own - top)
                attn[:, cols] = ((a * first + b * own[span, cols]) * (1.0 / (a + b))).astype(BF16)

        if g == 0:
            loads["weight"].wait()

        def project(j, squares):
            cols = pl.ds(pl.multiple_of(j * tile, tile), tile)
            weight = sums[:, :, cols].reshape(width, tile)
            res = hidden_ref[span, cols].astype(F32) + dot(attn[...], weight)
            own[span, cols] = res
            return squares + jnp.sum(res * res, axis=1, keepdims=True)

        squares = lax.fori_loop(0, width // tile, project, jnp.zeros((size, 1), F32))
        factor = lax.rsqrt(squares / width + 1e-05)

        @pl.loop(0, width // tile)
        def _(j):
            cols = pl.ds(pl.multiple_of(j * tile, tile), tile)
            tokens[0, span, cols] = (own[span, cols] * factor * gain_ref[:, cols]).astype(BF16)

    def view(dz, dy, start, count):
        return tokens.at[slot(dz, dy), pl.ds(start, count)]

    def start_of(kind):
        return kind[1] * size + (part_half if kind[0] == "b" else 0)

    def push(key, dz, dy, axis, step, start, count):
        device = {("z", 1): zp, ("z", -1): zm, ("y", 1): yp, ("y", -1): ym}[axis, step]
        tz, ty = ((dz - step) % SIDE, dy) if axis == "z" else (dz, (dy - step) % SIDE)
        copies.start((key, tz, ty), view(dz, dy, start, count), view(tz, ty, start, count), device)

    def both(kind, dz, dy, axis):
        push(kind, dz, dy, axis, 1, start_of(kind), part_half)
        push(kind, dz, dy, axis, -1, start_of(kind), part_half)

    def pass_on(kind, dz, dy, axis):
        behind = (dz if axis == "z" else dy) == 3
        start = start_of(kind) + (0 if behind else part_half // 2)
        push((kind, behind), dz, dy, axis, 1 if behind else -1, start, part_half // 2)

    waited = set()

    def have(kind, dz, dy):
        first, last = (dz, dy) if kind[0] == "a" else (dy, dz)
        if first == 0 and last == 0:
            return
        split = last == 2 or (last == 0 and first == 2)
        for key in ([(kind, True), (kind, False)] if split else [kind]):
            if (key, dz, dy) not in waited:
                waited.add((key, dz, dy))
                copies.arrived((key, dz, dy))

    def spread_0(g):
        both(("a", g), 0, 0, "z")
        both(("b", g), 0, 0, "y")
        both(("a", g), 0, 0, "y")
        both(("b", g), 0, 0, "z")

    def spread_1(g):
        for d in (3, 1):
            have(("a", g), d, 0)
            pass_on(("a", g), d, 0, "z")
            both(("a", g), d, 0, "y")
            have(("b", g), 0, d)
            pass_on(("b", g), 0, d, "y")
            both(("b", g), 0, d, "z")

    def spread_far(g):
        have(("a", g), 2, 0)
        both(("a", g), 2, 0, "y")
        have(("b", g), 0, 2)
        both(("b", g), 0, 2, "z")

    def pass_second(g, d):
        for near in (3, 1):
            have(("a", g), d, near)
            pass_on(("a", g), d, near, "y")
            have(("b", g), near, d)
            pass_on(("b", g), near, d, "z")

    ids = [e.astype(F32), (e + 1 - 2 * lax.rem(e, 2)).astype(F32)]
    span2 = 2 * CAP
    count = len(CHUNKS[0]) * CAP
    before = (
        lax.broadcasted_iota(jnp.int32, (rows, rows), 0) < lax.broadcasted_iota(jnp.int32, (rows, rows), 1)
    ).astype(BF16)
    slot_row = lax.broadcasted_iota(jnp.int32, (span2, rows), 0).astype(F32)

    pairs_of, total = {}, 0
    for chunk in CHUNKS:
        pairs_of[chunk] = [(total + i // 2, chunk[i:i + 2]) for i in range(0, len(chunk), 2)]
        total += len(chunk) // 2

    def place_tokens(chunk):
        for p, pair in pairs_of[chunk]:
            gates = [jnp.zeros((span2, 1), F32)] * 2
            for i, (dz, dy) in enumerate(pair):
                source = slot(dz, dy)
                both_chosen = []
                for k in range(2):
                    named = (meta[source, 0:8, :] == ids[k]).astype(F32)
                    mine = jnp.sum(named, axis=0, keepdims=True)
                    gate = jnp.sum(named * meta[source, 8:16, :], axis=0, keepdims=True)
                    rank = dot(jnp.broadcast_to(mine, (8, rows)).astype(BF16), before)[0:1, :]
                    place = jnp.where(mine > 0.0, rank + float(i * CAP), -1.0)
                    chosen = (slot_row == place).astype(F32)
                    gates[k] = gates[k] + jnp.sum(chosen * gate, axis=1, keepdims=True)
                    both_chosen.append(chosen)
                chosen = jnp.concatenate(both_chosen, axis=0)
                pmat[p, :, i * rows:(i + 1) * rows] = chosen.astype(BF16)
                pmat_t[p, i * rows:(i + 1) * rows, :] = jnp.transpose(chosen).astype(BF16)
            for k in range(2):
                gslot[:, 2 * p + k:2 * p + k + 1] = gates[k]

    def run_experts(chunk):
        pairs = pairs_of[chunk]
        held = len(chunk) * CAP
        tile = width
        for start in range(0, width, tile):
            cols = pl.ds(start, tile)
            for n, (p, pair) in enumerate(pairs):
                joint = jnp.concatenate([tokens[slot(dz, dy), :, cols] for dz, dy in pair], axis=0)
                rows_out = dot(pmat[p], joint).astype(BF16)
                for k in range(2):
                    qrows[k * count + n * span2:k * count + (n + 1) * span2, cols] = rows_out[k * span2:(k + 1) * span2, :]

        tile_f = min(256, inner)

        @pl.loop(0, inner // tile_f)
        def _(j):
            start = pl.multiple_of(j * tile_f, tile_f)
            for k in range(2):
                gate = dot(qrows[k * count:k * count + held, :], up[k, :, pl.ds(start, tile_f)])
                lift = dot(qrows[k * count:k * count + held, :], up[k, :, pl.ds(pl.multiple_of(inner + start, tile_f), tile_f)])
                hid[k, 0:held, pl.ds(start, tile_f)] = (gate / (1.0 + jnp.exp(-gate)) * lift).astype(BF16)

        tile_d = min(256, width)
        turns = min(2, width // tile_d)

        @pl.loop(0, width // (turns * tile_d))
        def _(block):
            joint = []
            for turn in range(turns):
                cols = pl.ds(pl.multiple_of((block * turns + turn) * tile_d, tile_d), tile_d)
                made = []
                for k in range(2):
                    gates = jnp.concatenate([gslot[:, 2 * p + k:2 * p + k + 1] for p, _ in pairs], axis=0)
                    made.append((dot(hid[k, 0:held, :], down[k, :, cols]) * gates).astype(BF16))
                joint.append([
                    jnp.concatenate([m[n * span2:(n + 1) * span2, :] for m in made], axis=0) for n in range(len(pairs))
                ])
            for turn in range(turns):
                cols = pl.ds(pl.multiple_of((block * turns + turn) * tile_d, tile_d), tile_d)
                for n, (p, pair) in enumerate(pairs):
                    placed = dot(pmat_t[p], joint[turn][n]).astype(BF16)
                    for i, (dz, dy) in enumerate(pair):
                        sums[slot(dz, dy), :, cols] = placed[i * rows:(i + 1) * rows, :]

    def sum_view(h, i, j, start, count):
        dz, dy = (i, j) if h == 0 else (j, i)
        return sums.at[slot(dz, dy), pl.ds(h * half + start, count)]

    first = ((yp, ym), (zp, zm))
    second = ((zp, zm), (yp, ym))

    def far_out(h, i):
        copies.start(("1+", h, i), sum_view(h, i, 2, 0, quarter), r1.at[h, i, pl.ds(0, quarter)], first[h][0])
        copies.start(("1-", h, i), sum_view(h, i, 2, quarter, quarter), r1.at[h, i, pl.ds(quarter, quarter)], first[h][1])

    def add_to(ref, more):
        ref[...] = (ref[...].astype(F32) + more[...].astype(F32)).astype(BF16)

    def near_out(h, i):
        copies.arrived(("1+", h, i))
        add_to(sum_view(h, i, 1, 0, quarter), r1.at[h, i, pl.ds(0, quarter)])
        copies.start(("2+", h, i), sum_view(h, i, 1, 0, half), r2.at[h, i, 0], first[h][0])
        copies.arrived(("1-", h, i))
        add_to(sum_view(h, i, 3, quarter, quarter), r1.at[h, i, pl.ds(quarter, quarter)])
        copies.start(("2-", h, i), sum_view(h, i, 3, 0, half), r2.at[h, i, 1], first[h][1])

    def gathered(h, i, start, count):
        span = pl.ds(start, count)
        return (
            sum_view(h, i, 0, start, count)[...].astype(F32)
            + r2[h, i, 0, span, :].astype(F32)
            + r2[h, i, 1, span, :].astype(F32)
        )

    def arrived_2(h, i):
        copies.arrived(("2+", h, i))
        copies.arrived(("2-", h, i))

    loads["cache"].wait()
    prefix(0, [0])
    q_on(0)
    own_part()
    copies.arrived("f1")
    copies.arrived("f3")
    q_near(0)
    prefix(0, [1, 3])
    direct_out(0)
    copies.arrived(("q2+", 0))
    copies.arrived(("q2-", 0))
    copies.arrived("f2")
    prefix(0, [2])
    relay_out(0)
    q_first(1)
    prefix(1, [0])
    relay_on(0)
    q_rest(1)
    for d in (3, 1):
        source = told(d, 0)
        tell(d, 3, source, yp)
        tell(d, 1, source, ym)
        if d == 3:
            tell(2, 0, source, zp)
    q_on(1)
    finish(0)
    spread_0(0)
    q_near(1)
    prefix(1, [1, 3])
    direct_out(1)
    spread_1(0)
    copies.arrived(("q2+", 1))
    copies.arrived(("q2-", 1))
    prefix(1, [2])
    relay_out(1)
    source = told(2, 0)
    tell(2, 3, source, yp)
    tell(2, 1, source, ym)
    pass_second(0, 0)
    relay_on(1)
    spread_far(0)
    for d in range(SIDE):
        tell(d, 2, told(d, 3), yp)
    finish(1)
    spread_0(1)
    pass_second(0, 1)
    pass_second(0, 3)
    for d in range(SIDE):
        told(d, 1)
        told(d, 2)
    place_tokens(CHUNKS[0])
    place_tokens(CHUNKS[1])
    place_tokens(CHUNKS[2])
    spread_1(1)
    pass_second(0, 2)
    place_tokens(CHUNKS[3])
    place_tokens(CHUNKS[4])
    pass_second(1, 0)
    for key in ("up", "down"):
        loads[key].wait()
        copies.arrived(key)
    for g in range(GROUPS):
        for key in ("q2+", "q2-", "r_high", "l_low", "relay_r", "relay_l", "r_low", "l_high"):
            copies.left((key, g))

    def run(chunk):
        for dz, dy in chunk:
            for g in range(GROUPS):
                have(("a", g), dz, dy)
                have(("b", g), dz, dy)
        run_experts(chunk)

    level = part
    lo, hi = pl.ds(0, quarter), pl.ds(quarter, quarter)

    def level_rows(h, start, count):
        return pl.ds(h * half + start, count)

    def level_far(h):
        arrived_2(h, 2)
        level[2, level_rows(h, 0, half), :] = gathered(h, 2, 0, half).astype(BF16)
        copies.start(("3+", h), level.at[2, level_rows(h, 0, quarter)], r3.at[h, lo], second[h][0])
        copies.start(("3-", h), level.at[2, level_rows(h, quarter, quarter)], r3.at[h, hi], second[h][1])

    run(CHUNKS[0])
    spread_far(1)
    pass_second(1, 1)
    pass_second(1, 3)
    run(CHUNKS[1])
    pass_second(1, 2)
    for h, i in ((0, 0), (1, 0)):
        far_out(h, i)
    run(CHUNKS[2])
    for h, i in ((0, 1), (1, 1)):
        far_out(h, i)
    for h, i in ((0, 0), (1, 0)):
        near_out(h, i)
    run(CHUNKS[3])
    for h, i in ((0, 2), (1, 2), (0, 3), (1, 3)):
        far_out(h, i)
    run(CHUNKS[4])
    for h, i in ((0, 2), (1, 2), (0, 1), (1, 1)):
        near_out(h, i)
    level_far(0)
    level_far(1)
    for h, i in ((0, 3), (1, 3)):
        near_out(h, i)
    for h in range(2):
        arrived_2(h, 1)
        copies.arrived(("3+", h))
        level[1, level_rows(h, 0, quarter), :] = (gathered(h, 1, 0, quarter) + r3[h, lo, :].astype(F32)).astype(BF16)
        level[1, level_rows(h, quarter, quarter), :] = gathered(h, 1, quarter, quarter).astype(BF16)
        copies.start(("4+", h), level.at[1, level_rows(h, 0, half)], r4.at[h, 0], second[h][0])
        arrived_2(h, 3)
        copies.arrived(("3-", h))
        level[3, level_rows(h, 0, quarter), :] = gathered(h, 3, 0, quarter).astype(BF16)
        level[3, level_rows(h, quarter, quarter), :] = (gathered(h, 3, quarter, quarter) + r3[h, hi, :].astype(F32)).astype(BF16)
        copies.start(("4-", h), level.at[3, level_rows(h, 0, half)], r4.at[h, 1], second[h][1])
    for h in range(2):
        arrived_2(h, 0)
        copies.arrived(("4+", h))
        copies.arrived(("4-", h))
        span = pl.ds(h * half, half)
        mixture = gathered(h, 0, 0, half) + r4[h, 0].astype(F32) + r4[h, 1].astype(F32)
        position = lax.broadcasted_iota(jnp.int32, (half, width), 0) + h * half
        out_ref[span, :] = jnp.where(position < length, own[span, :] + mixture, 0.0).astype(BF16)
    copies.drain()


def layer(length, group, owner, queries, pairs, cache, weight, hidden, gain, routes, gates, upward, downward):
    rows, width = queries.shape
    heads = width // HD
    inner = downward.shape[0]
    half = rows // 2
    slots = SIDE * SIDE
    count = len(CHUNKS[0]) * CAP
    dma = pltpu.SemaphoreType.DMA
    return pl.pallas_call(
        layer_kernel,
        out_shape=jax.ShapeDtypeStruct((rows, width), BF16),
        in_specs=[SMEM, SMEM, SMEM, VMEM, VMEM, ANY, ANY, VMEM, VMEM, VMEM, VMEM, ANY, ANY],
        out_specs=VMEM,
        scratch_shapes=[
            pltpu.VMEM((3 * rows, width), BF16),
            pltpu.VMEM((8, HD), F32),
            pltpu.VMEM((3, 8, HD), F32),
            pltpu.VMEM(cache.shape, BF16),
            pltpu.VMEM((4, rows, width), BF16),
            pltpu.VMEM((GROUPS, 4, rows // GROUPS, HD), F32),
            pltpu.VMEM((GROUPS, 4, heads, rows), F32),
            pltpu.VMEM((GROUPS, 3, heads, rows), F32),
            pltpu.VMEM((rows, width), F32),
            pltpu.VMEM((rows, HD), F32),
            pltpu.VMEM((GROUPS, 2, rows // GROUPS // 2, width), BF16),
            pltpu.VMEM((2, rows, width), BF16),
            pltpu.VMEM((rows // GROUPS, width), BF16),
            pltpu.VMEM((GROUPS, rows // GROUPS, cache.shape[1]), F32),
            pltpu.VMEM((slots, 16, rows), F32),
            pltpu.VMEM((slots, rows, width), BF16),
            pltpu.VMEM((2,) + upward.shape, BF16),
            pltpu.VMEM((2,) + downward.shape, BF16),
            pltpu.VMEM((slots // 2, 4 * CAP, 2 * rows), BF16),
            pltpu.VMEM((slots // 2, 2 * rows, 4 * CAP), BF16),
            pltpu.VMEM((2 * CAP, HD), F32),
            pltpu.VMEM((2, count, inner), BF16),
            pltpu.VMEM((slots, width // slots, width), BF16),
            pltpu.VMEM((2, SIDE, half, width), BF16),
            pltpu.VMEM((2, SIDE, 2, half, width), BF16),
            pltpu.VMEM((2, half, width), BF16),
            pltpu.VMEM((2, 2, half, width), BF16),
            dma((180,)),
            dma((180,)),
            dma((4,)),
        ],
        compiler_params=pltpu.CompilerParams(
            collective_id=0, has_side_effects=True, vmem_limit_bytes=VMEM_LIMIT
        ),
        name="layer",
    )(
        length, group, owner, queries, pairs, cache, weight.reshape(slots, width // slots, width), hidden, gain,
        routes, gates, upward, downward,
    )


def on_device(
    hidden_in, queries, suffix_pairs, prefix_cache, suffix_length, request_group, prefix_owner,
    out_weight, norm_gain, routes, gate_values, expert_upward, expert_downward,
):
    rows, width = hidden_in.shape[2:]
    out = layer(
        suffix_length, request_group, prefix_owner, queries[0, 0], suffix_pairs[0, 0], prefix_cache[0, 0], out_weight,
        hidden_in[0, 0], norm_gain.reshape(1, width), routes[0, 0], gate_values[0, 0], expert_upward[0], expert_downward[0],
    )
    return out.reshape(1, 1, rows, width)


def solution(mesh):
    in_specs = (
        P("req", "exp", None, None),
        P("req", "exp", None, None),
        P("req", "exp", None, None, None),
        P("exp", "req", None, None, None),
        P("req", "exp"),
        P("req", "exp"),
        P("exp", None),
        P(),
        P(),
        P("req", "exp", None, None),
        P("req", "exp", None, None),
        P("exp", None, None),
        P("exp", None, None),
    )
    out_specs = P("req", "exp", None, None)
    return jax.shard_map(
        on_device, mesh=mesh, in_specs=in_specs, out_specs=out_specs, check_vma=False
    )
```
